32 devices in a mesh: rep: 4 (over y, x), fsdp: 8 (over z, core).
Axes of the slice: x: 2, y: 2, z: 4, core: 2. Of those that a mesh axis runs over, the one named last changes fastest.
Arguments:
- tokens: bfloat16 [73728, 768], P(('rep', 'fsdp')), may hold values from -6 to 6
- cotangent: bfloat16 [73728, 768], P(('rep', 'fsdp')), may hold values from -6 to 6
- crop_heights: int32 [128], P(('rep', 'fsdp')), may hold values from 12 to 24, as said below
- rope_positions: int32 [128, 2, 576], P(('rep', 'fsdp')), may hold values from 0 to 31, as said below
- gain_attn: bfloat16 [768], P('fsdp'), may hold values from 0.5 to 1.5
- w_query: bfloat16 [768, 768], P('fsdp'), may hold values from -0.21875 to 0.21875
- w_key: bfloat16 [768, 768], P('fsdp'), may hold values from -0.21875 to 0.21875
- w_value: bfloat16 [768, 768], P('fsdp'), may hold values from -0.21875 to 0.21875
- w_out: bfloat16 [768, 768], P('fsdp'), may hold values from -0.875 to 0.875
- gain_mlp: bfloat16 [768], P('fsdp'), may hold values from 0.5 to 1.5
- w_gate: bfloat16 [768, 2048], P('fsdp'), may hold values from -0.21875 to 0.21875
- w_up: bfloat16 [768, 2048], P('fsdp'), may hold values from -0.21875 to 0.21875
- w_down: bfloat16 [2048, 768], P('fsdp'), may hold values from -0.125 to 0.125
Outputs:
- out_tokens: bfloat16 [73728, 768], P(('rep', 'fsdp'))
- grad_tokens: float32 [73728, 768], P(('rep', 'fsdp'))
- grad_gain_attn: float32 [768], P('fsdp')
- grad_query: float32 [768, 768], P('fsdp')
- grad_key: float32 [768, 768], P('fsdp')
- grad_value: float32 [768, 768], P('fsdp')
- grad_out: float32 [768, 768], P('fsdp')
- grad_gain_mlp: float32 [768], P('fsdp')
- grad_gate: float32 [768, 2048], P('fsdp')
- grad_up: float32 [768, 2048], P('fsdp')
- grad_down: float32 [2048, 768], P('fsdp')
The draws below stay inside these ranges and needn't reach their ends.
Inputs may be any that keep to these rules, and one draw needn't show every extreme that they name: Crop c holds 24 * crop_heights[c] valid tokens in the first slots of its 576; the rest are padding. `rope_positions`: the valid slots of a crop lie on consecutive grid rows starting at some row, 24 consecutive columns each, in row-major order; padding slots carry positions too.
All inputs are finite; a program needn't handle non-finite values.
Results may differ from the reference program's by a relative error of at most 0.015.
Values may be sent and summed in bfloat16 or wider, within the bound.
No kernel may reach another device: no remote copies, remote signals or barrier semaphores. Data moves between devices by JAX's collectives and lax.ppermute only.
A program may use at most 256 MiB of HBM per device.

```python
import jax
import jax.numpy as jnp
from jax import lax

D = 768
HEAD_DIM = 64
FF = 2048
COLS = 24
MAX_ROWS = 24
MIN_ROWS = 12
GRID = 32
SEQ_DEV = 4
SLOT = 576
CROPS = 128
TOKENS = 73728


def crop_plan(key):
    heights = jax.random.randint(jax.random.fold_in(key, 11), (CROPS,), MIN_ROWS, MAX_ROWS + 1, dtype=jnp.int32)
    heights = heights.at[0].set(MAX_ROWS).at[1].set(MIN_ROWS)
    top_rows = jax.random.randint(jax.random.fold_in(key, 12), (CROPS,), 0, GRID - heights + 1, dtype=jnp.int32)
    top_rows = top_rows.at[0].set(GRID - MAX_ROWS).at[1].set(0)
    left_cols = jax.random.randint(jax.random.fold_in(key, 13), (CROPS,), 0, GRID - COLS + 1, dtype=jnp.int32)
    left_cols = left_cols.at[0].set(GRID - COLS).at[1].set(0)
    return (heights, top_rows, left_cols)


def draw_crop_heights(key, part):
    return crop_plan(key)[0]


def draw_rope_positions(key, part):
    heights, top_rows, left_cols = crop_plan(key)
    cells = jnp.arange(SLOT, dtype=jnp.int32)
    row_pos = jnp.minimum(top_rows[:, None] + cells[None, :] // COLS, GRID - 1)
    col_pos = left_cols[:, None] + cells[None, :] % COLS
    return jnp.stack([row_pos, col_pos], axis=1).astype(jnp.int32)


def strengthened(drawn, stream_key, source, target, blocks, factor):
    def block_of(axis_at):
        return (jnp.arange(drawn.shape[axis_at]) // (drawn.shape[axis_at] // blocks)).reshape((-1,) + (1,) * (drawn.ndim - 1 - axis_at))

    near = jax.random.permutation(stream_key, blocks)[block_of(target)]
    far = (block_of(target) + blocks // 2) % blocks
    return jnp.where((block_of(source) == near) | (block_of(source) == far), factor * drawn, drawn)


def shard_levels(key, dims, cuts, low, largest):
    factor_of = 1.0
    for axis_at, parts in cuts:
        draws = jax.random.uniform(jax.random.fold_in(jax.random.fold_in(key, 6), axis_at), (parts,), jnp.float32, low / len(cuts), largest / len(cuts))
        factor_of = factor_of * jnp.repeat(jnp.exp(draws), dims[axis_at] // parts).reshape((-1,) + (1,) * (len(dims) - 1 - axis_at))
    return factor_of


def normal_values(stream_key, shape, spread, bound, cuts=(), kind=jnp.bfloat16):
    level = shard_levels(stream_key, shape, cuts, -0.22, 0.18) if cuts else 1.0
    array = jax.random.normal(stream_key, shape, jnp.float32) * spread * level
    return jnp.minimum(jnp.maximum(array, -bound), bound).astype(kind)


def bell_draw_with(own_key, shape, deviation, most, pieces, heavy, kind=jnp.bfloat16):
    result = deviation * jax.random.normal(own_key, shape, jnp.float32)
    if pieces:
        result = result * shard_levels(own_key, shape, pieces, -0.22, 0.18)
    return jnp.clip(strengthened(result, jax.random.fold_in(own_key, 3), *heavy), -most, most).astype(kind)


def setup_inputs(seed: int = 0) -> dict:
    keys = jax.random.split(jax.random.key(seed), 14)
    return {
        "tokens": bell_draw_with(keys[0], (TOKENS, D), 1.0, 6.0, ((0, 32),), (0, 1, 32, 2.75)),
        "cotangent": bell_draw_with(keys[1], (TOKENS, D), 1.0, 6.0, ((0, 32),), (0, 1, 32, 2.75)),
        "crop_heights": draw_crop_heights(jax.random.fold_in(keys[13], 71), 0),
        "rope_positions": draw_rope_positions(jax.random.fold_in(keys[13], 71), 0),
        "gain_attn": jnp.clip(1.0 + 0.1 * jax.random.normal(keys[4], (D,), jnp.float32), 0.5, 1.5).astype(jnp.bfloat16),
        "w_query": normal_values(keys[5], (D, D), D ** -0.5, 0.21875, ((0, 8),)),
        "w_key": normal_values(keys[6], (D, D), D ** -0.5, 0.21875, ((0, 8),)),
        "w_value": normal_values(keys[7], (D, D), D ** -0.5, 0.21875, ((0, 8),)),
        "w_out": normal_values(keys[8], (D, D), (D // 16) ** -0.5, 0.875, ((0, 8),)),
        "gain_mlp": jnp.clip(1.0 + 0.1 * jax.random.normal(keys[9], (D,), jnp.float32), 0.5, 1.5).astype(jnp.bfloat16),
        "w_gate": normal_values(keys[10], (D, FF), D ** -0.5, 0.21875, ((0, 8),)),
        "w_up": normal_values(keys[11], (D, FF), D ** -0.5, 0.21875, ((0, 8),)),
        "w_down": normal_values(keys[12], (FF, D), FF ** -0.5, 0.125, ((0, 8),)),
    }


EPSILON = 1e-05
HIGHEST = lax.Precision.HIGHEST
NEGATIVE = -1e+30

@jax.custom_vjp
def low(v):
    return lax.optimization_barrier(v.astype(jnp.bfloat16)).astype(jnp.float32)

@jax.custom_vjp
def low_back(v):
    return v

def low_keep(v):
    return (low(v), None)

def low_pass(kept, grad):
    return (grad,)

def back_keep(v):
    return (v, None)

def back_low(kept, grad):
    return (low(grad),)
low.defvjp(low_keep, low_pass)
low_back.defvjp(back_keep, back_low)

def product(left, right):
    return jnp.matmul(left, right, precision=HIGHEST)

def angle_tables(positions):
    frequency = 1.0 / 10000.0 ** (jnp.arange(HEAD_DIM // 4, dtype=jnp.float32) * 4.0 / HEAD_DIM)
    row_angle = positions[:, 0, :, None].astype(jnp.float32) * frequency
    col_angle = positions[:, 1, :, None].astype(jnp.float32) * frequency
    angles = jnp.concatenate([row_angle, col_angle], axis=-1)
    return (jnp.cos(angles)[:, :, None, :], jnp.sin(angles)[:, :, None, :])

def rotate(field, cosine, sine_table):
    half_dim = field.shape[-1] // 2
    first_half = field[..., :half_dim]
    second_half = field[..., half_dim:]
    return jnp.concatenate([first_half * cosine - second_half * sine_table, first_half * sine_table + second_half * cosine], axis=-1)

def inverse_rms(field):
    return lax.rsqrt(lax.optimization_barrier(jnp.mean(field * field, axis=-1, keepdims=True)) + EPSILON)

def layer_group(inputs, cosine, sine_table, valid_rows, params):
    gain_attn, w_query, w_key, w_value, w_out, gain_mlp, w_gate, w_up, w_down = params
    crop_count, slot_len, model_width = inputs.shape
    head_count = model_width // HEAD_DIM
    normed = low(inputs * inverse_rms(inputs) * gain_attn)

    def per_head(weight):
        return product(normed, weight).reshape(crop_count, slot_len, head_count, HEAD_DIM)
    queries = low(rotate(low_back(per_head(w_query)), cosine, sine_table))
    keys_rot = low(rotate(low_back(per_head(w_key)), cosine, sine_table))
    values_in = low_back(low(per_head(w_value)))
    scores = low_back(jnp.einsum('cqhd,ckhd->chqk', queries, keys_rot, precision=HIGHEST) * HEAD_DIM ** (-0.5))
    causal = jnp.arange(slot_len)[:, None] >= jnp.arange(slot_len)[None, :]
    scores = jnp.where(causal, scores, NEGATIVE)
    maximum = lax.optimization_barrier(jnp.max(scores, axis=-1, keepdims=True))
    exponent = jnp.exp(scores - maximum)
    attn_probs = low(exponent / lax.optimization_barrier(jnp.sum(exponent, axis=-1, keepdims=True)))
    mixed = jnp.einsum('chqk,ckhd->cqhd', attn_probs, values_in, precision=HIGHEST)
    attended = low_back(low(mixed.reshape(crop_count, slot_len, model_width)))
    middle = inputs + valid_rows * low_back(product(attended, w_out))
    normed_mlp = low(middle * inverse_rms(middle) * gain_mlp)
    gate_val = low_back(product(normed_mlp, w_gate))
    up_val = low_back(product(normed_mlp, w_up))
    hidden = low(gate_val * jax.nn.sigmoid(gate_val) * up_val)
    return middle + valid_rows * low_back(product(hidden, w_down))

def reference(tokens, cotangent, crop_heights, rope_positions, gain_attn, w_query, w_key, w_value, w_out, gain_mlp, w_gate, w_up, w_down):
    crop_count = crop_heights.shape[0]
    group_count = crop_count // SEQ_DEV
    cosine, sine_table = angle_tables(rope_positions)
    valid_rows = (jnp.arange(SLOT)[None, :] < (crop_heights * COLS)[:, None]).astype(jnp.float32)[:, :, None]

    def grouped(field):
        return field.reshape((group_count, SEQ_DEV) + field.shape[1:])
    inputs = grouped(tokens.astype(jnp.float32).reshape(crop_count, SLOT, D))
    params = (gain_attn.astype(jnp.float32), w_query.astype(jnp.float32), w_key.astype(jnp.float32), w_value.astype(jnp.float32), w_out.astype(jnp.float32), gain_mlp.astype(jnp.float32), w_gate.astype(jnp.float32), w_up.astype(jnp.float32), w_down.astype(jnp.float32))
    tables = (grouped(cosine), grouped(sine_table), grouped(valid_rows))

    def forward(group_inputs, group_params):

        def one_group(member):
            return layer_group(member[0], member[1], member[2], member[3], group_params)
        return lax.map(jax.checkpoint(one_group), (group_inputs,) + tables)
    outputs, pullback = jax.vjp(forward, inputs, params)
    grad_inputs, grads = pullback(grouped(cotangent.astype(jnp.float32).reshape(crop_count, SLOT, D)))
    return (outputs.reshape(crop_count * SLOT, D).astype(jnp.bfloat16), grad_inputs.reshape(crop_count * SLOT, D), grads[0], grads[1], grads[2], grads[3], grads[4], grads[5], grads[6], grads[7], grads[8])
```

```python
import functools
import jax
import jax.numpy as jnp
import numpy as np
from jax import lax
from jax.experimental import pallas as pl
from jax.experimental.pallas import tpu as pltpu
from jax.sharding import PartitionSpec as P

HEAD_DIM = 64
COLS = 24
EPSILON = 1e-05
GROUP = 4
GW = GROUP * HEAD_DIM
HALF = GW // 2
BF = jnp.bfloat16
F32 = jnp.float32


def nn(a, b):
    return lax.dot_general(a, b, (((1,), (0,)), ((), ())), preferred_element_type=F32)


def nt(a, b):
    return lax.dot_general(a, b, (((1,), (1,)), ((), ())), preferred_element_type=F32)


def tn(a, b):
    return lax.dot_general(a, b, (((0,), (0,)), ((), ())), preferred_element_type=F32)


def params(limit=60):
    return pltpu.CompilerParams(vmem_limit_bytes=limit * 1024 * 1024)


def norm_kernel(x_ref, gain_ref, out_ref):
    x = x_ref[...].astype(F32)
    inv = lax.rsqrt(jnp.mean(x * x, axis=-1, keepdims=True) + EPSILON)
    out_ref[...] = (x * inv * gain_ref[...]).astype(BF)


def norm_call(x, gain, rows):
    n, d = x.shape
    return pl.pallas_call(
        norm_kernel,
        grid=(n // rows,),
        in_specs=[pl.BlockSpec((rows, d), lambda i: (i, 0)), pl.BlockSpec((1, d), lambda i: (0, 0))],
        out_specs=pl.BlockSpec((rows, d), lambda i: (i, 0)),
        out_shape=jax.ShapeDtypeStruct((n, d), BF),
        compiler_params=params(),
        name="norm_in",
    )(x, gain)


def head_masks():
    lane = lax.broadcasted_iota(jnp.int32, (1, GW), 1)
    rot = [((lane % HALF) // (HEAD_DIM // 2) == h) for h in range(GROUP)]
    nat = [(lane // HEAD_DIM == h) for h in range(GROUP)]
    return rot, nat


def mask_to(x, m):
    return x * jnp.where(m, 1.0, 0.0).astype(x.dtype)


def blocks_of(total, size):
    return [(s, min(s + size, total)) for s in range(0, total, size)]


def attn_fwd_kernel(slot, size, nm_ref, w_ref, cos_ref, sin_ref, qkv_ref, att_ref, lse_ref):
    nm = nm_ref[...]
    cos = cos_ref[...]
    sin = sin_ref[...]
    rot_m, nat_m = head_masks()

    def rotated(lo, scale):
        u = nn(nm, w_ref[:, lo : lo + GW])
        a, b = u[:, :HALF], u[:, HALF:]
        r = jnp.concatenate([a * cos - b * sin, a * sin + b * cos], axis=1)
        return r.astype(BF) * jnp.asarray(scale, BF)

    q = rotated(0, HEAD_DIM ** (-0.5))
    k = rotated(GW, 1.0)
    v = nn(nm, w_ref[:, 2 * GW :]).astype(BF)
    qkv_ref[:, :GW] = q
    qkv_ref[:, GW : 2 * GW] = k
    qkv_ref[:, 2 * GW :] = v
    qs = [mask_to(q, m) for m in rot_m]
    vs = [mask_to(v, m) for m in nat_m]
    lane = lax.broadcasted_iota(jnp.int32, (1, 128), 1)
    for s, e in blocks_of(slot, size):
        row = lax.broadcasted_iota(jnp.int32, (e - s, e - s), 0)
        col = lax.broadcasted_iota(jnp.int32, (e - s, e - s), 1)
        causal = row >= col
        out = None
        logs = jnp.zeros((e - s, 128), F32)
        for h in range(GROUP):
            qh = qs[h][s:e]
            diag = jnp.where(causal, nt(qh, k[s:e]), -1e30)
            top = jnp.max(diag, axis=-1, keepdims=True)
            if s:
                left = nt(qh, k[:s])
                top = jnp.maximum(top, jnp.max(left, axis=-1, keepdims=True))
            pd = jnp.exp(diag - top)
            total = jnp.sum(pd, axis=-1, keepdims=True)
            o = nn(pd.astype(BF), vs[h][s:e])
            if s:
                pleft = jnp.exp(left - top)
                total = total + jnp.sum(pleft, axis=-1, keepdims=True)
                o = o + nn(pleft.astype(BF), vs[h][:s])
            o = o * (1.0 / total)
            out = o if out is None else out + o
            logs = jnp.where(lane == h, top + jnp.log(total), logs)
        att_ref[s:e, :] = out.astype(BF)
        lse_ref[0, 0, :, s:e] = logs.T[:8]


def attn_fwd(nm, w, cos, sin, slot, size=256):
    n, d = nm.shape
    crops = n // slot
    groups = w.shape[1] // (3 * GW)
    return pl.pallas_call(
        functools.partial(attn_fwd_kernel, slot, size),
        grid=(groups, crops),
        in_specs=[
            pl.BlockSpec((slot, d), lambda g, c: (c, 0)),
            pl.BlockSpec((d, 3 * GW), lambda g, c: (0, g)),
            pl.BlockSpec((slot, HALF), lambda g, c: (c, 0)),
            pl.BlockSpec((slot, HALF), lambda g, c: (c, 0)),
        ],
        out_specs=[
            pl.BlockSpec((slot, 3 * GW), lambda g, c: (c, g)),
            pl.BlockSpec((slot, GW), lambda g, c: (c, g)),
            pl.BlockSpec((1, 1, 8, slot), lambda g, c: (g, c, 0, 0)),
        ],
        out_shape=[
            jax.ShapeDtypeStruct((n, groups * 3 * GW), BF),
            jax.ShapeDtypeStruct((n, groups * GW), BF),
            jax.ShapeDtypeStruct((groups, crops, 8, slot), F32),
        ],
        compiler_params=params(),
        name="attn_fwd",
    )(nm, w, cos, sin)


def attn_bwd_kernel(slot, size, qkv_ref, go_ref, att_ref, lse_ref, nm_ref, cos_ref, sin_ref,
                    gqkv_ref, dw_ref, dst_ref, dq_ref, acc_ref):
    crop = pl.program_id(1)
    q = qkv_ref[:, :GW]
    k = qkv_ref[:, GW : 2 * GW]
    v = qkv_ref[:, 2 * GW :]
    go = go_ref[...]
    rot_m, nat_m = head_masks()
    prod = go.astype(F32) * att_ref[...].astype(F32)
    hi = prod.astype(BF)
    lo = (prod - hi.astype(F32)).astype(BF)
    pick = (
        lax.broadcasted_iota(jnp.int32, (8, GW), 1) // HEAD_DIM
        == lax.broadcasted_iota(jnp.int32, (8, GW), 0)
    )
    pick = jnp.where(pick, 1.0, 0.0).astype(BF)
    delta = nt(pick, hi) + nt(pick, lo)
    blocks = blocks_of(slot, size)
    dk = [None] * len(blocks)
    dv = [None] * len(blocks)
    for h in range(GROUP):
        qm = mask_to(q, rot_m[h])
        km = mask_to(k, rot_m[h])
        gm = mask_to(go, nat_m[h])
        for j, (s, e) in enumerate(blocks):
            w = e - s
            row = lax.broadcasted_iota(jnp.int32, (w, w), 0)
            col = lax.broadcasted_iota(jnp.int32, (w, w), 1)
            parts = [(s, e, True)] + ([(e, slot, False)] if e < slot else [])
            for ps, pe, diag in parts:
                sc = nt(k[s:e], qm[ps:pe])
                p = jnp.exp(sc - lse_ref[0, 0, h : h + 1, ps:pe])
                if diag:
                    p = jnp.where(col >= row, p, 0.0)
                dp = nt(v[s:e], gm[ps:pe])
                ds = (p * (dp - delta[h : h + 1, ps:pe])).astype(BF)
                dst_ref[s:e, ps:pe] = ds
                dvp = nn(p.astype(BF), gm[ps:pe])
                dkp = nn(ds, qm[ps:pe])
                dv[j] = dvp if dv[j] is None else dv[j] + dvp
                dk[j] = dkp if dk[j] is None else dk[j] + dkp
        for s, e in blocks:
            part = tn(dst_ref[:e, s:e], km[:e])
            if h:
                dq_ref[s:e] += part
            else:
                dq_ref[s:e] = part
    cos = cos_ref[...]
    sin = sin_ref[...]

    def back(u, c, t):
        a, b = u[:, :HALF], u[:, HALF:]
        return jnp.concatenate([a * c + b * t, b * c - a * t], axis=1).astype(BF)

    for j, (s, e) in enumerate(blocks):
        c, t = cos[s:e], sin[s:e]
        gqkv_ref[s:e, :GW] = back(dq_ref[s:e] * (HEAD_DIM ** (-0.5)), c, t)
        gqkv_ref[s:e, GW : 2 * GW] = back(dk[j], c, t)
        gqkv_ref[s:e, 2 * GW :] = dv[j].astype(BF)
    part = tn(nm_ref[...], gqkv_ref[...])

    @pl.when(crop == 0)
    def _():
        acc_ref[...] = part

    @pl.when(crop != 0)
    def _():
        acc_ref[...] += part

    @pl.when(crop == pl.num_programs(1) - 1)
    def _():
        dw_ref[...] = acc_ref[...].astype(BF)


def attn_bwd(qkv, go, att, lse, nm, cos, sin, slot, size=256):
    n, d = nm.shape
    crops = n // slot
    groups = lse.shape[0]
    row_spec = lambda w: pl.BlockSpec((slot, w), lambda g, c: (c, g))
    crop_spec = lambda w: pl.BlockSpec((slot, w), lambda g, c: (c, 0))
    return pl.pallas_call(
        functools.partial(attn_bwd_kernel, slot, size),
        grid=(groups, crops),
        in_specs=[
            row_spec(3 * GW),
            row_spec(GW),
            row_spec(GW),
            pl.BlockSpec((1, 1, 8, slot), lambda g, c: (g, c, 0, 0)),
            crop_spec(d),
            crop_spec(HALF),
            crop_spec(HALF),
        ],
        out_specs=[row_spec(3 * GW), pl.BlockSpec((d, 3 * GW), lambda g, c: (0, g))],
        out_shape=[
            jax.ShapeDtypeStruct((n, groups * 3 * GW), BF),
            jax.ShapeDtypeStruct((d, groups * 3 * GW), BF),
        ],
        scratch_shapes=[
            pltpu.VMEM((slot, slot), BF),
            pltpu.VMEM((slot, GW), F32),
            pltpu.VMEM((d, 3 * GW), F32),
        ],
        compiler_params=params(),
        name="attn_bwd",
    )(qkv, go, att, lse, nm, cos, sin)


def valid_rows(heights_ref, c, slot):
    return lax.broadcasted_iota(jnp.int32, (slot, 1), 0) < heights_ref[c] * COLS


def out_proj_kernel(slot, heights_ref, x_ref, att_ref, wo_ref, gain_ref, mid_ref, nm_ref):
    valid = valid_rows(heights_ref, pl.program_id(0), slot)
    proj = nn(att_ref[...], wo_ref[...])
    mid = x_ref[...].astype(F32) + jnp.where(valid, proj, 0.0)
    mid_ref[...] = mid
    inv = lax.rsqrt(jnp.mean(mid * mid, axis=-1, keepdims=True) + EPSILON)
    nm_ref[...] = (mid * inv * gain_ref[...]).astype(BF)


def out_proj(heights, x, att, wo, gain, slot):
    n, d = x.shape
    rows = pl.BlockSpec((slot, d), lambda c, *_: (c, 0))
    return pl.pallas_call(
        functools.partial(out_proj_kernel, slot),
        grid_spec=pltpu.PrefetchScalarGridSpec(
            num_scalar_prefetch=1,
            grid=(n // slot,),
            in_specs=[
                rows,
                rows,
                pl.BlockSpec((d, d), lambda c, *_: (0, 0)),
                pl.BlockSpec((1, d), lambda c, *_: (0, 0)),
            ],
            out_specs=[rows, rows],
        ),
        out_shape=[jax.ShapeDtypeStruct((n, d), F32), jax.ShapeDtypeStruct((n, d), BF)],
        compiler_params=params(),
        name="out_proj",
    )(heights, x, att, wo, gain)


def mlp_kernel(slot, heights_ref, nm_ref, cot_ref, mid_ref, wg_ref, wu_ref, wd_ref,
               out_ref, dn_ref, dwg_ref, dwu_ref, dwd_ref,
               nmt_ref, gbt_ref, oacc_ref, dacc_ref, ag_ref, au_ref, ad_ref):
    f = pl.program_id(0)
    c = pl.program_id(1)
    last_f = pl.num_programs(0) - 1
    last_c = pl.num_programs(1) - 1
    valid = valid_rows(heights_ref, c, slot)
    nm = nm_ref[...]
    gb = jnp.where(valid, cot_ref[...], jnp.zeros((), BF))

    @pl.when(f == 0)
    def _():
        nmt_ref[c] = nm.T
        gbt_ref[c] = gb.T

    g = nn(nm, wg_ref[...])
    u = nn(nm, wu_ref[...])
    gh = nt(gb, wd_ref[...])
    sg = 1.0 / (1.0 + jnp.exp(-g))
    act = g * sg
    hid = (act * u).astype(BF)
    gu = (gh * act).astype(BF)
    gg = (gh * u * (sg * (1.0 + g * (1.0 - sg)))).astype(BF)
    o = nn(hid, wd_ref[...])
    dn = nt(gg, wg_ref[...]) + nt(gu, wu_ref[...])
    nmt = nmt_ref[c]
    dg = nn(nmt, gg)
    du = nn(nmt, gu)
    dd = nn(gbt_ref[c], hid)

    @pl.when(f == 0)
    def _():
        oacc_ref[c] = o
        dacc_ref[c] = dn

    @pl.when(f != 0)
    def _():
        oacc_ref[c] += o
        dacc_ref[c] += dn

    @pl.when(c == 0)
    def _():
        ag_ref[...] = dg
        au_ref[...] = du
        ad_ref[...] = dd

    @pl.when(c != 0)
    def _():
        ag_ref[...] += dg
        au_ref[...] += du
        ad_ref[...] += dd

    @pl.when(c == last_c)
    def _():
        dwg_ref[...] = ag_ref[...].astype(BF)
        dwu_ref[...] = au_ref[...].astype(BF)
        dwd_ref[...] = ad_ref[...].astype(BF).T

    @pl.when(f == last_f)
    def _():
        out_ref[...] = (mid_ref[...] + jnp.where(valid, oacc_ref[c], 0.0)).astype(BF)
        dn_ref[...] = dacc_ref[c]


def mlp(heights, nm, cot, mid, wg, wu, wd, slot, chunk=512):
    n, d = nm.shape
    crops = n // slot
    ff = wg.shape[1]
    nf = ff // chunk

    def last(f, c, *_):
        return (jnp.where(f == nf - 1, c, 0), 0)

    every = pl.BlockSpec((slot, d), lambda f, c, *_: (c, 0))
    wide = pl.BlockSpec((d, chunk), lambda f, c, *_: (0, f))
    tall = pl.BlockSpec((chunk, d), lambda f, c, *_: (f, 0))
    return pl.pallas_call(
        functools.partial(mlp_kernel, slot),
        grid_spec=pltpu.PrefetchScalarGridSpec(
            num_scalar_prefetch=1,
            grid=(nf, crops),
            in_specs=[every, every, pl.BlockSpec((slot, d), last), wide, wide, tall],
            out_specs=[pl.BlockSpec((slot, d), last), pl.BlockSpec((slot, d), last), wide, wide, tall],
            scratch_shapes=[
                pltpu.VMEM((crops, d, slot), BF),
                pltpu.VMEM((crops, d, slot), BF),
                pltpu.VMEM((crops, slot, d), F32),
                pltpu.VMEM((crops, slot, d), F32),
                pltpu.VMEM((d, chunk), F32),
                pltpu.VMEM((d, chunk), F32),
                pltpu.VMEM((d, chunk), F32),
            ],
        ),
        out_shape=[
            jax.ShapeDtypeStruct((n, d), BF),
            jax.ShapeDtypeStruct((n, d), F32),
            jax.ShapeDtypeStruct((d, ff), BF),
            jax.ShapeDtypeStruct((d, ff), BF),
            jax.ShapeDtypeStruct((ff, d), BF),
        ],
        compiler_params=params(),
        name="mlp",
    )(heights, nm, cot, mid, wg, wu, wd)


def mid_grad_kernel(slot, heights_ref, cot_ref, mid_ref, dn_ref, gain_ref, wo_ref, att_ref,
                    gmid_ref, gatt_ref, dwo_ref, acc_ref):
    c = pl.program_id(0)
    valid = valid_rows(heights_ref, c, slot)
    mid = mid_ref[...]
    inv = lax.rsqrt(jnp.mean(mid * mid, axis=-1, keepdims=True) + EPSILON)
    e = dn_ref[...] * gain_ref[...]
    gm = (
        cot_ref[...].astype(F32)
        + inv * e
        - mid * (inv * inv * inv * jnp.mean(e * mid, axis=-1, keepdims=True))
    )
    gmid_ref[...] = gm
    ga = jnp.where(valid, gm, 0.0).astype(BF)
    gatt_ref[...] = nt(ga, wo_ref[...]).astype(BF)
    part = tn(att_ref[...], ga)

    @pl.when(c == 0)
    def _():
        acc_ref[...] = part

    @pl.when(c != 0)
    def _():
        acc_ref[...] += part

    @pl.when(c == pl.num_programs(0) - 1)
    def _():
        dwo_ref[...] = acc_ref[...].astype(BF)


def mid_grad(heights, cot, mid, dn, gain, wo, att, slot):
    n, d = cot.shape
    rows = pl.BlockSpec((slot, d), lambda c, *_: (c, 0))
    whole = pl.BlockSpec((d, d), lambda c, *_: (0, 0))
    return pl.pallas_call(
        functools.partial(mid_grad_kernel, slot),
        grid_spec=pltpu.PrefetchScalarGridSpec(
            num_scalar_prefetch=1,
            grid=(n // slot,),
            in_specs=[rows, rows, rows, pl.BlockSpec((1, d), lambda c, *_: (0, 0)), whole, rows],
            out_specs=[rows, rows, whole],
            scratch_shapes=[pltpu.VMEM((d, d), F32)],
        ),
        out_shape=[
            jax.ShapeDtypeStruct((n, d), F32),
            jax.ShapeDtypeStruct((n, d), BF),
            jax.ShapeDtypeStruct((d, d), BF),
        ],
        compiler_params=params(),
        name="mid_grad",
    )(heights, cot, mid, dn, gain, wo, att)


def input_grad_kernel(gqkv_ref, w_ref, x_ref, gain_ref, gmid_ref, out_ref):
    gn = nt(gqkv_ref[...], w_ref[...])
    x = x_ref[...].astype(F32)
    inv = lax.rsqrt(jnp.mean(x * x, axis=-1, keepdims=True) + EPSILON)
    e = gn * gain_ref[...]
    out_ref[...] = (
        gmid_ref[...]
        + inv * e
        - x * (inv * inv * inv * jnp.mean(e * x, axis=-1, keepdims=True))
    )


def input_grad(gqkv, w, x, gain, gmid, rows):
    n, d = x.shape
    cols = w.shape[1]
    return pl.pallas_call(
        input_grad_kernel,
        grid=(n // rows,),
        in_specs=[
            pl.BlockSpec((rows, cols), lambda i: (i, 0)),
            pl.BlockSpec((d, cols), lambda i: (0, 0)),
            pl.BlockSpec((rows, d), lambda i: (i, 0)),
            pl.BlockSpec((1, d), lambda i: (0, 0)),
            pl.BlockSpec((rows, d), lambda i: (i, 0)),
        ],
        out_specs=pl.BlockSpec((rows, d), lambda i: (i, 0)),
        out_shape=jax.ShapeDtypeStruct((n, d), F32),
        compiler_params=params(),
        name="input_grad",
    )(gqkv, w, x, gain, gmid)


def angle_tables(positions):
    frequency = 1.0 / 10000.0 ** (jnp.arange(HEAD_DIM // 4, dtype=F32) * 4.0 / HEAD_DIM)
    frequency = jnp.tile(frequency, 8)
    first = (jnp.arange(HALF) // (HEAD_DIM // 4)) % 2 == 0
    crops, _, slot = positions.shape
    place = jnp.where(first, positions[:, 0, :, None], positions[:, 1, :, None])
    angles = (place.astype(F32) * frequency).reshape(crops * slot, HALF)
    return jnp.cos(angles), jnp.sin(angles)


def rot_order(w):
    rows, cols = w.shape
    w = w.reshape(rows, cols // GW, GROUP, 2, HEAD_DIM // 2)
    return w.transpose(0, 1, 3, 2, 4).reshape(rows, cols)


def natural_order(w):
    rows, cols = w.shape
    w = w.reshape(rows, cols // GW, 2, GROUP, HEAD_DIM // 2)
    return w.transpose(0, 1, 3, 2, 4).reshape(rows, cols)


def join_qkv(wq, wk, wv):
    rows, cols = wq.shape
    parts = [w.reshape(rows, cols // GW, GW) for w in (rot_order(wq), rot_order(wk), wv)]
    return jnp.concatenate(parts, axis=2).reshape(rows, 3 * cols)


def split_qkv(w):
    rows, cols = w.shape
    w = w.reshape(rows, cols // (3 * GW), 3, GW)
    q, k, v = (w[:, :, i].reshape(rows, cols // 3) for i in range(3))
    return natural_order(q), natural_order(k), v


def body(tokens, cotangent, crop_heights, rope_positions, gain_attn, w_query, w_key, w_value, w_out,
         gain_mlp, w_gate, w_up, w_down):
    crops = crop_heights.shape[0]
    rows, d = tokens.shape
    slot = rows // crops

    def gather(w):
        return lax.all_gather(w, "fsdp", axis=0, tiled=True)

    def reduce(g):
        local = lax.psum_scatter(g, "fsdp", scatter_dimension=0, tiled=True)
        return lax.psum(local, "rep").astype(F32)

    gains = lax.all_gather(jnp.stack([gain_attn, gain_mlp]), "fsdp", axis=1, tiled=True).astype(F32)
    gain1, gain2 = gains[:1], gains[1:]
    qkv_shard = join_qkv(w_query, w_key, w_value)
    wqkv = gather(qkv_shard)
    wo = gather(w_out)
    wg = gather(w_gate)
    wu = gather(w_up)
    wd = gather(w_down)
    cos, sin = angle_tables(rope_positions)
    nm1 = norm_call(tokens, gain1, slot)
    qkv, att, lse = attn_fwd(nm1, wqkv, cos, sin, slot)
    mid, nm2 = out_proj(crop_heights, tokens, att, wo, gain2, slot)
    out, dn, dwg, dwu, dwd = mlp(crop_heights, nm2, cotangent, mid, wg, wu, wd, slot)
    dwg, dwu, dwd = reduce(dwg), reduce(dwu), reduce(dwd)
    gmid, gatt, dwo = mid_grad(crop_heights, cotangent, mid, dn, gain2, wo, att, slot)
    dwo = reduce(dwo)
    gqkv, dwqkv = attn_bwd(qkv, gatt, att, lse, nm1, cos, sin, slot)
    dwqkv = reduce(dwqkv)
    grad_tokens = input_grad(gqkv, wqkv, tokens, gain1, gmid, slot)
    g1 = jnp.sum(dwqkv * qkv_shard.astype(F32), axis=1) / gain_attn.astype(F32)
    g2 = (
        jnp.sum(dwg * w_gate.astype(F32), axis=1) + jnp.sum(dwu * w_up.astype(F32), axis=1)
    ) / gain_mlp.astype(F32)
    dwq, dwk, dwv = split_qkv(dwqkv)
    return out, grad_tokens, g1, dwq, dwk, dwv, dwo, g2, dwg, dwu, dwd


def solution(mesh):
    in_specs = (
        P(("rep", "fsdp"), None),
        P(("rep", "fsdp"), None),
        P(("rep", "fsdp")),
        P(("rep", "fsdp"), None, None),
        P("fsdp"),
        P("fsdp", None),
        P("fsdp", None),
        P("fsdp", None),
        P("fsdp", None),
        P("fsdp"),
        P("fsdp", None),
        P("fsdp", None),
        P("fsdp", None),
    )
    out_specs = (
        P(("rep", "fsdp"), None),
        P(("rep", "fsdp"), None),
        P("fsdp"),
        P("fsdp", None),
        P("fsdp", None),
        P("fsdp", None),
        P("fsdp", None),
        P("fsdp"),
        P("fsdp", None),
        P("fsdp", None),
        P("fsdp", None),
    )
    return jax.shard_map(body, mesh=mesh, in_specs=in_specs, out_specs=out_specs, check_vma=False)
```

```python
import functools
import jax
import jax.numpy as jnp
import numpy as np
from jax import lax
from jax.experimental import pallas as pl
from jax.experimental.pallas import tpu as pltpu
from jax.sharding import PartitionSpec as P

HEAD_DIM = 64
COLS = 24
EPSILON = 1e-05
GROUP = 4
GW = GROUP * HEAD_DIM
HALF = GW // 2
BF = jnp.bfloat16
F32 = jnp.float32


def nn(a, b):
    return lax.dot_general(a, b, (((1,), (0,)), ((), ())), preferred_element_type=F32)


def nt(a, b):
    return lax.dot_general(a, b, (((1,), (1,)), ((), ())), preferred_element_type=F32)


def tn(a, b):
    return lax.dot_general(a, b, (((0,), (0,)), ((), ())), preferred_element_type=F32)


def params(limit=60):
    return pltpu.CompilerParams(vmem_limit_bytes=limit * 1024 * 1024)


def cost(flops, moved):
    return pl.CostEstimate(flops=int(flops), transcendentals=0, bytes_accessed=int(moved))


def inverse_rms(x):
    return lax.rsqrt(jnp.mean(x * x, axis=-1, keepdims=True) + EPSILON)


def norm_kernel(x_ref, out_ref):
    x = x_ref[...].astype(F32)
    out_ref[...] = (x * inverse_rms(x)).astype(BF)


def norm_call(x, rows):
    n, d = x.shape
    spec = pl.BlockSpec((rows, d), lambda i: (i, 0))
    return pl.pallas_call(
        norm_kernel,
        grid=(n // rows,),
        in_specs=[spec],
        out_specs=spec,
        out_shape=jax.ShapeDtypeStruct((n, d), BF),
        compiler_params=params(),
        cost_estimate=cost(0, 4 * n * d),
        name="norm_in",
    )(x)


def head_masks():
    lane = lax.broadcasted_iota(jnp.int32, (1, GW), 1)
    rot = [((lane % HALF) // (HEAD_DIM // 2) == h) for h in range(GROUP)]
    nat = [(lane // HEAD_DIM == h) for h in range(GROUP)]
    return rot, nat


def mask_to(x, m):
    return x * jnp.where(m, 1.0, 0.0).astype(x.dtype)


def blocks_of(total, size):
    return [(s, min(s + size, total)) for s in range(0, total, size)]


def attn_fwd_kernel(slot, size, ids_ref, nm_ref, cos_ref, sin_ref, own_hbm, oth_hbm,
                    qkv_ref, att_ref, lse_ref, w_out_ref, sem):
    group = pl.program_id(0)
    crop = pl.program_id(1)
    crops = pl.num_programs(1)
    zs = own_hbm.shape[1]
    rep, z, core = ids_ref[crops], ids_ref[crops + 1], ids_ref[crops + 2]

    @pl.when(crop == 0)
    def _():
        made = []
        for hbm, place in ((own_hbm, core), (oth_hbm, 1 - core)):
            for kind in range(4):
                for j in range(zs):
                    src = hbm.at[kind ^ rep, j, :, pl.ds(pl.multiple_of(group * GW, GW), GW)]
                    dst = w_out_ref.at[(z + j) & (zs - 1), place, :, pl.ds(kind * GW, GW)]
                    made.append(pltpu.make_async_copy(src, dst, sem.at[len(made)]))
        for copy in made:
            copy.start()
        for copy in made:
            copy.wait()

    nm = nm_ref[...]
    cos = cos_ref[...]
    sin = sin_ref[...]
    rot_m, nat_m = head_masks()
    d = nm.shape[1]

    def rotated(lo, scale):
        u = nn(nm, w_out_ref[:, :, :, lo : lo + GW].reshape(d, GW))
        a, b = u[:, :HALF], u[:, HALF:]
        r = jnp.concatenate([a * cos - b * sin, a * sin + b * cos], axis=1)
        return r.astype(BF) * jnp.asarray(scale, BF)

    q = rotated(0, HEAD_DIM ** (-0.5))
    k = rotated(GW, 1.0)
    v = nn(nm, w_out_ref[:, :, :, 2 * GW : 3 * GW].reshape(d, GW)).astype(BF)
    qkv_ref[:, :GW] = q
    qkv_ref[:, GW : 2 * GW] = k
    qkv_ref[:, 2 * GW :] = v
    qs = [mask_to(q, m) for m in rot_m]
    vs = [mask_to(v, m) for m in nat_m]
    lane = lax.broadcasted_iota(jnp.int32, (1, 128), 1)
    units = [(s, e, h) for s, e in blocks_of(slot, size) for h in range(GROUP)]

    def scores(s, e, h):
        qh = qs[h][s:e]
        return nt(qh, k[s:e]), nt(qh, k[:s]) if s else None

    out = logs = None
    ready = scores(*units[0])
    for i, (s, e, h) in enumerate(units):
        later = scores(*units[i + 1]) if i + 1 < len(units) else None
        diag, left = ready
        row = lax.broadcasted_iota(jnp.int32, (e - s, e - s), 0)
        col = lax.broadcasted_iota(jnp.int32, (e - s, e - s), 1)
        diag = jnp.where(row >= col, diag, -1e30)
        top = jnp.max(diag, axis=-1, keepdims=True)
        if s:
            top = jnp.maximum(top, jnp.max(left, axis=-1, keepdims=True))
        pd = jnp.exp(diag - top)
        total = jnp.sum(pd, axis=-1, keepdims=True)
        o = nn(pd.astype(BF), vs[h][s:e])
        if s:
            pleft = jnp.exp(left - top)
            total = total + jnp.sum(pleft, axis=-1, keepdims=True)
            o = o + nn(pleft.astype(BF), vs[h][:s])
        o = o * (1.0 / total)
        out = out + o if h else o
        logs = jnp.where(lane == h, top + jnp.log(total), logs if h else 0.0)
        if h == GROUP - 1:
            att_ref[s:e, :] = out.astype(BF)
            lse_ref[0, 0, :, s:e] = logs.T[:8]
        ready = later


def attn_fwd(ids, nm, cos, sin, own, oth, slot, size=256):
    n, d = nm.shape
    crops = n // slot
    kinds, zs, rows, width = own.shape
    groups = width // GW
    hbm = pl.BlockSpec(memory_space=pl.ANY)
    crop_spec = lambda w: pl.BlockSpec((slot, w), lambda g, c, *_: (c, 0))
    qkv, att, lse, w = pl.pallas_call(
        functools.partial(attn_fwd_kernel, slot, size),
        grid_spec=pltpu.PrefetchScalarGridSpec(
            num_scalar_prefetch=1,
            grid=(groups, crops),
            in_specs=[crop_spec(d), crop_spec(HALF), crop_spec(HALF), hbm, hbm],
            out_specs=[
                pl.BlockSpec((slot, 3 * GW), lambda g, c, *_: (c, g)),
                pl.BlockSpec((slot, GW), lambda g, c, *_: (c, g)),
                pl.BlockSpec((1, 1, 8, slot), lambda g, c, *_: (g, c, 0, 0)),
                pl.BlockSpec((zs, 2, rows, 4 * GW), lambda g, c, *_: (0, 0, 0, g)),
            ],
            scratch_shapes=[pltpu.SemaphoreType.DMA((8 * zs,))],
        ),
        out_shape=[
            jax.ShapeDtypeStruct((n, groups * 3 * GW), BF),
            jax.ShapeDtypeStruct((n, groups * GW), BF),
            jax.ShapeDtypeStruct((groups, crops, 8, slot), F32),
            jax.ShapeDtypeStruct((zs, 2, rows, groups * 4 * GW), BF),
        ],
        compiler_params=params(),
        cost_estimate=cost(8e6 * groups * n, 2 * n * d),
        name="attn_fwd",
    )(ids, nm, cos, sin, own, oth)
    return qkv, att, lse, w.reshape(d, groups * 4 * GW)


def attn_bwd_kernel(slot, size, qkv_ref, go_ref, att_ref, lse_ref, nm_ref, cos_ref, sin_ref, *refs):
    gqkv_ref, dw_ref, dst_ref, dq_ref, acc_ref = refs[-5:]
    crop = pl.program_id(1)
    q = qkv_ref[:, :GW]
    k = qkv_ref[:, GW : 2 * GW]
    v = qkv_ref[:, 2 * GW :]
    go = go_ref[...]
    rot_m, nat_m = head_masks()
    prod = go.astype(F32) * att_ref[...].astype(F32)
    hi = prod.astype(BF)
    lo = (prod - hi.astype(F32)).astype(BF)
    pick = (
        lax.broadcasted_iota(jnp.int32, (8, GW), 1) // HEAD_DIM
        == lax.broadcasted_iota(jnp.int32, (8, GW), 0)
    )
    pick = jnp.where(pick, 1.0, 0.0).astype(BF)
    delta = nt(pick, hi) + nt(pick, lo)
    blocks = blocks_of(slot, size)
    dk = [None] * len(blocks)
    dv = [None] * len(blocks)
    qms = [mask_to(q, m) for m in rot_m]
    kms = [mask_to(k, m) for m in rot_m]
    gms = [mask_to(go, m) for m in nat_m]
    units = []
    for h in range(GROUP):
        for j, (s, e) in enumerate(blocks):
            units.append((h, j, s, e, s, e))
            if e < slot:
                units.append((h, j, s, e, e, slot))

    def scores(h, j, s, e, ps, pe):
        return nt(k[s:e], qms[h][ps:pe]), nt(v[s:e], gms[h][ps:pe])

    ready = scores(*units[0])
    for i, (h, j, s, e, ps, pe) in enumerate(units):
        later = scores(*units[i + 1]) if i + 1 < len(units) else None
        sc, dp = ready
        p = jnp.exp(sc - lse_ref[0, 0, h : h + 1, ps:pe])
        if ps == s:
            row = lax.broadcasted_iota(jnp.int32, (e - s, e - s), 0)
            col = lax.broadcasted_iota(jnp.int32, (e - s, e - s), 1)
            p = jnp.where(col >= row, p, 0.0)
        ds = (p * (dp - delta[h : h + 1, ps:pe])).astype(BF)
        dst_ref[h, s:e, ps:pe] = ds
        dvp = nn(p.astype(BF), gms[h][ps:pe])
        dkp = nn(ds, qms[h][ps:pe])
        dv[j] = dvp if dv[j] is None else dv[j] + dvp
        dk[j] = dkp if dk[j] is None else dk[j] + dkp
        if i + 1 == len(units) or units[i + 1][0] != h:
            for bs, be in blocks:
                part = tn(dst_ref[h, :be, bs:be], kms[h][:be])
                if h:
                    dq_ref[bs:be] += part
                else:
                    dq_ref[bs:be] = part
        ready = later
    cos = cos_ref[...]
    sin = sin_ref[...]

    def back(u, c, t):
        a, b = u[:, :HALF], u[:, HALF:]
        return jnp.concatenate([a * c + b * t, b * c - a * t], axis=1).astype(BF)

    for j, (s, e) in enumerate(blocks):
        c, t = cos[s:e], sin[s:e]
        gqkv_ref[s:e, :GW] = back(dq_ref[s:e] * (HEAD_DIM ** (-0.5)), c, t)
        gqkv_ref[s:e, GW : 2 * GW] = back(dk[j], c, t)
        gqkv_ref[s:e, 2 * GW :] = dv[j].astype(BF)
    part = tn(nm_ref[...], gqkv_ref[...])

    @pl.when(crop == 0)
    def _():
        acc_ref[...] = part

    @pl.when(crop != 0)
    def _():
        acc_ref[...] += part

    @pl.when(crop == pl.num_programs(1) - 1)
    def _():
        dw_ref[...] = acc_ref[...].astype(BF)


def attn_bwd(qkv, go, att, lse, nm, cos, sin, slot, place, first, joint=None, size=256):
    n, d = nm.shape
    crops = n // slot
    more = [] if joint is None else [joint]
    column = 0 if joint is None else first + place + 1
    row_spec = lambda w, at: pl.BlockSpec((slot, w), lambda g, c: (c, at))
    crop_spec = lambda w: pl.BlockSpec((slot, w), lambda g, c: (c, 0))
    return pl.pallas_call(
        functools.partial(attn_bwd_kernel, slot, size),
        grid=(1, crops),
        in_specs=[
            row_spec(3 * GW, place),
            row_spec(GW, first + place),
            row_spec(GW, place),
            pl.BlockSpec((1, 1, 8, slot), lambda g, c: (place, c, 0, 0)),
            crop_spec(d),
            crop_spec(HALF),
            crop_spec(HALF),
        ]
        + [pl.BlockSpec(memory_space=pl.ANY)] * len(more),
        out_specs=[crop_spec(3 * GW), pl.BlockSpec((d, 3 * GW), lambda g, c: (0, column))],
        out_shape=[
            jax.ShapeDtypeStruct((n, 3 * GW), BF),
            jax.ShapeDtypeStruct((d, 3 * GW) if joint is None else joint.shape, BF),
        ],
        input_output_aliases={7: 1} if more else {},
        scratch_shapes=[
            pltpu.VMEM((GROUP, slot, slot), BF),
            pltpu.VMEM((slot, GW), F32),
            pltpu.VMEM((d, 3 * GW), F32),
        ],
        compiler_params=params(),
        cost_estimate=cost(12e6 * n, 2 * n * d),
        name="attn_bwd",
    )(qkv, go, att, lse, nm, cos, sin, *more)


def valid_rows(ids_ref, tile, rows, slot):
    row = tile * rows + lax.broadcasted_iota(jnp.int32, (rows, 1), 0)
    crop = row // slot
    first = tile * rows // slot
    limit = jnp.zeros((rows, 1), jnp.int32)
    for i in range(-(-rows // slot) + 1):
        index = first + i
        limit = jnp.where(crop == index, ids_ref[index] * COLS, limit)
    return row - crop * slot < limit


def out_weights(weights, d):
    arrays, specs = [], []
    for w in weights:
        for g in range(w.shape[1] // (4 * GW)):
            arrays.append(w)
            specs.append(pl.BlockSpec((d, GW), lambda c, *_, g=g: (0, 4 * g + 3)))
    return arrays, specs


def out_proj_kernel(slot, n_att, ids_ref, x_ref, *refs):
    att_refs, refs = refs[:n_att], refs[n_att:]
    *wo_refs, mid_ref, nm_ref = refs
    valid = valid_rows(ids_ref, pl.program_id(0), x_ref.shape[0], slot)
    att = jnp.concatenate([a[...] for a in att_refs], axis=1)
    proj = jnp.concatenate([nn(att, w[...]) for w in wo_refs], axis=1)
    mid = x_ref[...].astype(F32) + jnp.where(valid, proj, 0.0)
    mid_ref[...] = mid
    nm_ref[...] = (mid * inverse_rms(mid)).astype(BF)


def out_proj(ids, x, atts, weights, slot, tile):
    n, d = x.shape
    rows = lambda w: pl.BlockSpec((tile, w), lambda c, *_: (c, 0))
    wos, wo_specs = out_weights(weights, d)
    return pl.pallas_call(
        functools.partial(out_proj_kernel, slot, len(atts)),
        grid_spec=pltpu.PrefetchScalarGridSpec(
            num_scalar_prefetch=1,
            grid=(n // tile,),
            in_specs=[rows(d)] + [rows(a.shape[1]) for a in atts] + wo_specs,
            out_specs=[rows(d), rows(d)],
        ),
        out_shape=[jax.ShapeDtypeStruct((n, d), F32), jax.ShapeDtypeStruct((n, d), BF)],
        compiler_params=params(),
        cost_estimate=cost(2 * n * d * d, 10 * n * d),
        name="out_proj",
    )(ids, x, *atts, *wos)


PACK = 512
TILE = 768
SHARDS = 8


def halves(w, axis):
    shape = w.shape[:axis] + (-1, 2, w.shape[axis] // (2 * SHARDS) if axis else w.shape[0] // 2) + w.shape[axis + 1 :]
    w = w.reshape(shape)
    return [
        lax.index_in_dim(w, i, axis + 1, keepdims=False).reshape(w.shape[:axis] + (-1,) + w.shape[axis + 3 :])
        for i in range(2)
    ]


def pack_mlp(gate, up, down):
    wide = [w[:, i : i + PACK] for w in (gate, up) for i in range(0, w.shape[1], PACK)]
    half = down.shape[0] // 2
    tail = down[:, PACK:]
    fold = jnp.concatenate([tail[:half], tail[half:]], axis=1)
    return jnp.concatenate(wide + [down[:, :PACK], fold], axis=0)


def unpack_mlp(pack, rows, d):
    chunks = 2
    gate, up = (
        jnp.concatenate([pack[i * rows : (i + 1) * rows] for i in range(s, s + chunks)], axis=1)
        for s in (0, chunks)
    )
    base = 2 * chunks * rows
    deep = (pack.shape[0] - base) * PACK // d
    fold = pack[base + deep :]
    tail = jnp.concatenate([fold[:, : d - PACK], fold[:, d - PACK :]], axis=0)
    return gate, up, jnp.concatenate([pack[base : base + deep], tail], axis=1)


def mlp_kernel(slot, final, step, ids_ref, nm_ref, cot_ref, part_ref, *refs):
    if final:
        before_ref, *refs = refs
    (pack_hbm, out_ref, dn_ref, grad_hbm, wg_buf, wu_buf, wd_buf, hid_ref, gg_ref, gu_ref,
     ag_ref, au_ref, ad_ref, sg_ref, su_ref, sd_ref, in_sem, out_sem) = refs
    tile = pl.program_id(0)
    d = nm_ref.shape[1]
    chunks, shards, rows, _ = sg_ref.shape
    units = chunks * PACK
    some = shards // chunks
    deep = sd_ref.shape[1]
    base = 2 * chunks * rows
    side = d - PACK

    def pieces(hbm, wg, wu, wd):
        for i in range(chunks):
            yield hbm.at[:, pl.ds(i * rows, rows), :], wg.at[i]
            yield hbm.at[:, pl.ds((chunks + i) * rows, rows), :], wu.at[i]
        yield hbm.at[:, pl.ds(base, deep), :], wd.at[:, :, pl.ds(0, PACK)]
        for i in range(2):
            yield (
                hbm.at[:, pl.ds(base + deep, deep // 2), pl.ds(i * side, side)],
                wd.at[:, pl.ds(i * (deep // 2), deep // 2), pl.ds(PACK, side)],
            )

    @pl.when(tile == 0)
    def _():
        made = pieces(pack_hbm, wg_buf, wu_buf, wd_buf)
        made = [pltpu.make_async_copy(a, b, in_sem.at[i]) for i, (a, b) in enumerate(made)]
        for copy in made:
            copy.start()
        ag_ref[...] = jnp.zeros_like(ag_ref)
        au_ref[...] = jnp.zeros_like(au_ref)
        ad_ref[...] = jnp.zeros_like(ad_ref)
        for copy in made:
            copy.wait()

    valid = valid_rows(ids_ref, tile, nm_ref.shape[0], slot)
    nm = nm_ref[...]
    gb = jnp.where(valid, cot_ref[...], jnp.zeros((), BF))
    wd = wd_buf[...].reshape(units, d)

    def wide(buf, i):
        at = i * step
        return buf[at // PACK, :, :, at % PACK : at % PACK + step].reshape(d, step)

    def first(i):
        return (
            nn(nm, wide(wg_buf, i)),
            nn(nm, wide(wu_buf, i)),
            nt(gb, wd[i * step : (i + 1) * step]),
        )

    def second(i, g, u, gh):
        cols = slice(i * step, (i + 1) * step)
        sg = 0.5 * jnp.tanh(0.5 * g) + 0.5
        act = g * sg
        hid_ref[:, cols] = (act * u).astype(BF)
        gu_ref[:, cols] = (gh * act).astype(BF)
        gg_ref[:, cols] = (gh * u * (sg + act * (1.0 - sg))).astype(BF)

    ready = first(0)
    for i in range(1, units // step):
        later = first(i)
        second(i - 1, *ready)
        ready = later
    second(units // step - 1, *ready)
    nmt = nm.T
    gbt = gb.T
    o = part_ref[...] + jnp.where(valid, nn(hid_ref[...], wd), 0.0)
    out_ref[...] = o.astype(out_ref.dtype)
    dn = before_ref[...] if final else 0.0
    for i in range(chunks):
        cols = slice(i * PACK, (i + 1) * PACK)
        dn = dn + nt(gg_ref[:, cols], wg_buf[i].reshape(d, PACK)) + nt(gu_ref[:, cols], wu_buf[i].reshape(d, PACK))
    dn_ref[...] = dn
    for i in range(chunks):
        cols = slice(i * PACK, (i + 1) * PACK)
        ag_ref[i] += nn(nmt, gg_ref[:, cols])
        au_ref[i] += nn(nmt, gu_ref[:, cols])
        ad_ref[i] += nn(gbt, hid_ref[:, cols])

    @pl.when(tile == pl.num_programs(0) - 1)
    def _():
        sg_ref[...] = ag_ref[...].astype(BF).reshape(sg_ref.shape)
        su_ref[...] = au_ref[...].astype(BF).reshape(su_ref.shape)
        for i in range(chunks):
            sd_ref[i * some : (i + 1) * some] = ad_ref[i].astype(BF).T.reshape(some, deep, d)
        made = pieces(grad_hbm, sg_ref, su_ref, sd_ref)
        made = [pltpu.make_async_copy(b, a, out_sem.at[i]) for i, (a, b) in enumerate(made)]
        for copy in made:
            copy.start()
        for copy in made:
            copy.wait()


def mlp(ids, nm, cot, part, before, pack, slot, tile, step=256):
    n, d = nm.shape
    rows = d // SHARDS
    chunks = 2
    deep = chunks * PACK // SHARDS
    final = before is not None
    spec = pl.BlockSpec((tile, d), lambda i, *_: (i, 0))
    hbm = pl.BlockSpec(memory_space=pl.ANY)
    packed = pltpu.VMEM((chunks, SHARDS, rows, PACK), BF)
    units = pltpu.VMEM((tile, chunks * PACK), BF)
    sums = pltpu.VMEM((chunks, d, PACK), F32)
    return pl.pallas_call(
        functools.partial(mlp_kernel, slot, final, step),
        grid_spec=pltpu.PrefetchScalarGridSpec(
            num_scalar_prefetch=1,
            grid=(n // tile,),
            in_specs=[spec] * (3 + final) + [hbm],
            out_specs=[spec, spec, hbm],
            scratch_shapes=[packed, packed, pltpu.VMEM((SHARDS, deep, d), BF)]
            + [units] * 3
            + [sums] * 3
            + [packed, packed, pltpu.VMEM((SHARDS, deep, d), BF)]
            + [pltpu.SemaphoreType.DMA((2 * chunks + 3,))] * 2,
        ),
        out_shape=[
            jax.ShapeDtypeStruct((n, d), BF if final else F32),
            jax.ShapeDtypeStruct((n, d), F32),
            jax.ShapeDtypeStruct(pack.shape, BF),
        ],
        compiler_params=params(),
        cost_estimate=cost(24e6 * n, 20 * n * d),
        name="mlp",
    )(ids, nm, cot, part, *([before] if final else []), pack)


def norm_back(scaled, field):
    inv = inverse_rms(field)
    return inv * scaled - field * (inv * inv * inv * jnp.mean(scaled * field, axis=-1, keepdims=True))


def mid_grad_kernel(slot, n_att, ids_ref, cot_ref, mid_ref, dn_ref, *refs):
    att_refs, refs = refs[:n_att], refs[n_att:]
    *wo_refs, gmid_ref, gatt_ref, dwo_ref, acc_ref = refs
    c = pl.program_id(0)
    valid = valid_rows(ids_ref, c, cot_ref.shape[0], slot)
    gm = cot_ref[...].astype(F32) + norm_back(dn_ref[...], mid_ref[...])
    gmid_ref[...] = gm
    ga = jnp.where(valid, gm, 0.0).astype(BF)
    gatt = sum(nt(ga[:, i * GW : (i + 1) * GW], w[...]) for i, w in enumerate(wo_refs))
    gatt_ref[...] = gatt.astype(BF)
    part = tn(jnp.concatenate([a[...] for a in att_refs], axis=1), ga)

    @pl.when(c == 0)
    def _():
        acc_ref[...] = part

    @pl.when(c != 0)
    def _():
        acc_ref[...] += part

    @pl.when(c == pl.num_programs(0) - 1)
    def _():
        dwo_ref[...] = acc_ref[...].astype(BF)


def mid_grad(ids, cot, mid, dn, atts, weights, slot, tile):
    n, d = cot.shape
    rows = lambda w: pl.BlockSpec((tile, w), lambda c, *_: (c, 0))
    wos, wo_specs = out_weights(weights, d)
    return pl.pallas_call(
        functools.partial(mid_grad_kernel, slot, len(atts)),
        grid_spec=pltpu.PrefetchScalarGridSpec(
            num_scalar_prefetch=1,
            grid=(n // tile,),
            in_specs=[rows(d)] * 3 + [rows(a.shape[1]) for a in atts] + wo_specs,
            out_specs=[rows(d), rows(d), pl.BlockSpec((d, d), lambda c, *_: (0, 0))],
            scratch_shapes=[pltpu.VMEM((d, d), F32)],
        ),
        out_shape=[
            jax.ShapeDtypeStruct((n, d), F32),
            jax.ShapeDtypeStruct((n, d), BF),
            jax.ShapeDtypeStruct((d, 3 * d), BF),
        ],
        compiler_params=params(),
        cost_estimate=cost(4 * n * d * d, 18 * n * d),
        name="mid_grad",
    )(ids, cot, mid, dn, *atts, *wos)


def input_grad_kernel(n_group, *refs):
    g_refs, w_refs = refs[:n_group], refs[n_group : 4 * n_group]
    x_ref, gmid_ref = refs[4 * n_group : 4 * n_group + 2]
    out_ref = refs[-1]
    e = 0.0
    for i, g in enumerate(g_refs):
        w = jnp.concatenate([w[...] for w in w_refs[3 * i : 3 * i + 3]], axis=1)
        e = e + nt(g[...], w)
    out_ref[...] = gmid_ref[...] + norm_back(e, x_ref[...].astype(F32))


def input_grad(gqkvs, weights, x, gmid, rows, start, stop, filled=None):
    n, d = x.shape
    arrays = [(w, 4 * g + i) for w in weights for g in range(w.shape[1] // (4 * GW)) for i in range(3)]
    spec = lambda w: pl.BlockSpec((rows, w), lambda i: (start + i, 0))
    more = [] if filled is None else [filled]
    n_in = 4 * len(gqkvs) + 2
    count = (stop - start) * rows
    return pl.pallas_call(
        functools.partial(input_grad_kernel, len(gqkvs)),
        grid=(stop - start,),
        in_specs=[spec(3 * GW)] * len(gqkvs)
        + [pl.BlockSpec((d, GW), lambda i, g=g: (0, g)) for _, g in arrays]
        + [spec(d), spec(d)]
        + [pl.BlockSpec(memory_space=pl.ANY)] * len(more),
        out_specs=spec(d),
        out_shape=jax.ShapeDtypeStruct((n, d), F32),
        input_output_aliases={n_in: 0} if more else {},
        compiler_params=params(),
        cost_estimate=cost(6 * count * d * d, 16 * count * d),
        name="input_grad",
    )(*gqkvs, *[w for w, _ in arrays], x, gmid, *more)


def angle_tables(positions):
    frequency = 1.0 / 10000.0 ** (jnp.arange(HEAD_DIM // 4, dtype=F32) * 4.0 / HEAD_DIM)
    frequency = jnp.tile(frequency, 8)
    first = (jnp.arange(HALF) // (HEAD_DIM // 4)) % 2 == 0
    crops, _, slot = positions.shape
    place = jnp.where(first, positions[:, 0, :, None], positions[:, 1, :, None])
    angles = (place.astype(F32) * frequency).reshape(crops * slot, HALF)
    return jnp.cos(angles), jnp.sin(angles)


def rot_order(w):
    rows, cols = w.shape
    w = w.reshape(rows, cols // GW, GROUP, 2, HEAD_DIM // 2)
    return w.transpose(0, 1, 3, 2, 4).reshape(rows, cols)


def natural_order(w):
    rows, cols = w.shape
    w = w.reshape(rows, cols // GW, 2, GROUP, HEAD_DIM // 2)
    return w.transpose(0, 1, 3, 2, 4).reshape(rows, cols)


def join_attn(wq, wk, wv, wo, gain):
    scaled = [(w.astype(F32) * gain).astype(BF) for w in (rot_order(wq), rot_order(wk), wv)]
    return jnp.stack(scaled + [wo])


def swap(x, axis, bit, size):
    return lax.ppermute(x, axis, [(i, i ^ bit) for i in range(size)])


def shift(x, step, size):
    half = size // 2
    return lax.ppermute(x, "fsdp", [(((i // 2 + step) % half) * 2 + i % 2, i) for i in range(size)])


def pick(x, index, axis=0):
    return lax.dynamic_index_in_dim(x, index, axis, keepdims=False)


def total(*parts):
    return sum(p.astype(F32) for p in parts).astype(BF)


def along_z(mine, size):
    return jnp.stack([mine] + [shift(mine, k, size) for k in range(1, size // 2)])


def over_reps(x, reps):
    return jnp.stack([x] + [swap(x, "rep", bit, reps) for bit in range(1, reps)])


def sum_reps(x, reps):
    if reps != 4:
        return lax.psum(x, "rep").astype(F32)
    x = (x.astype(F32) + swap(x, "rep", 1, reps).astype(F32)).astype(BF)
    return x.astype(F32) + swap(x, "rep", 2, reps).astype(F32)


def body(tokens, cotangent, crop_heights, rope_positions, gain_attn, w_query, w_key, w_value, w_out,
         gain_mlp, w_gate, w_up, w_down, *, reps, size):
    crops = crop_heights.shape[0]
    n, d = tokens.shape
    slot = n // crops
    tile = TILE if n % TILE == 0 else slot
    gain1 = gain_attn.astype(F32)[:, None]
    gain2 = gain_mlp.astype(F32)[:, None]

    def gather(w):
        return lax.all_gather(w, "fsdp", axis=0, tiled=True)

    def scatter(g):
        return lax.psum_scatter(g, "fsdp", scatter_dimension=0, tiled=True)

    def reduce(g):
        return sum_reps(scatter(g), reps)

    pin = lax.optimization_barrier
    links = reps == 4 and size == SHARDS
    rep, f = lax.axis_index("rep"), lax.axis_index("fsdp")
    joined = join_attn(w_query, w_key, w_value, w_out, gain1)
    if links:
        place = jnp.stack([rep, f // 2, f % 2]).astype(jnp.int32)
        mine = pick(joined, rep)
        mine, w_gate, w_up, w_down, rope_positions = pin((mine, w_gate, w_up, w_down, rope_positions))
        lines = [along_z(m, size) for m in (mine[:, :GW], mine[:, GW:])]
        lines[0], tokens_1 = pin((lines[0], tokens))
        sides = [swap(lines[0], "rep", bit, reps) for bit in range(1, reps)]
    else:
        place = jnp.zeros((3,), jnp.int32)
        every = lax.all_gather(joined, "fsdp", axis=1, tiled=True)
        every = every.reshape(4, SHARDS // 2, 2, d // SHARDS, d)
    ids = jnp.concatenate([crop_heights, place])
    cos, sin = angle_tables(rope_positions)
    if not links:
        tokens_1 = tokens
    nm1 = norm_call(tokens_1, tile)
    if links:
        *sides, lines[1], nm1, cos, sin = pin((*sides, lines[1], nm1, cos, sin))
        own = jnp.stack([lines[0]] + sides)
        own, w_gate, w_up, w_down = pin((own, w_gate, w_up, w_down))
        oth = swap(own, "fsdp", 1, size)
    scaled = [(w.astype(F32) * gain2).astype(BF) for w in (w_gate, w_up)]
    split = list(zip(halves(scaled[0], 1), halves(scaled[1], 1), halves(w_down, 0)))
    if size == SHARDS:
        packs = [lax.all_gather(pack_mlp(*part), "fsdp", axis=0, tiled=False) for part in split]
    else:
        wide = [gather(w).reshape(SHARDS, -1, w.shape[1]) for w in scaled]
        down = gather(w_down).reshape(SHARDS, -1, d)
        split = zip(*[[jnp.stack(h) for h in zip(*[halves(w, a) for w in ws])] for ws, a in
                      ((wide[0], 1), (wide[1], 1), (down, 0))])
        packs = [jax.vmap(pack_mlp)(*part) for part in split]

    attended, weights = [], []
    for i, cols in enumerate((slice(0, GW), slice(GW, d))):
        if not links:
            own, oth = every[:, :, 0, :, cols], every[:, :, 1, :, cols]
        elif i:
            *parts, _ = pin((lines[1], *sides, atts))
            own = jnp.stack(parts)
            oth = swap(own, "fsdp", 1, size)
        else:
            sides = [swap(lines[1], "rep", bit, reps) for bit in range(1, reps)]
        *some, w = attn_fwd(ids, nm1, cos, sin, own, oth, slot)
        attended.append(some)
        weights.append(w)
        atts = [a for _, a, _ in attended]
    mid, nm2 = out_proj(ids, tokens, atts, weights, slot, tile)
    part, dn, grad_a = mlp(ids, nm2, cotangent, mid, None, packs[0], slot, tile)
    out, dn, grad_b = mlp(ids, nm2, cotangent, part, dn, packs[1], slot, tile)
    local_a = scatter(grad_a.reshape(-1, PACK)) if size == SHARDS else grad_a
    local_b = scatter(grad_b.reshape(-1, PACK)) if size == SHARDS else grad_b
    gmid, gatt, joint = mid_grad(ids, cotangent, mid, dn, atts, weights, slot, tile)

    def backward(index, gatt, joint=None):
        w = 0 if index == 0 else 1
        qkv, att, lse = attended[w]
        return attn_bwd(qkv, gatt, att, lse, nm1, cos, sin, slot, index - w, w, joint)

    fast = size == SHARDS
    if links:
        local_a, gatt = pin((local_a, gatt))
        local_a = total(local_a, swap(local_a, "rep", 1, reps))
    gqkv0, joint = backward(0, gatt, joint)
    if links:
        local_a, gatt, gqkv0 = pin((local_a, gatt, gqkv0))
        other_a = swap(local_a, "rep", 2, reps)
    gqkv1, joint = backward(1, gatt, joint)
    if links:
        other_a, local_b, joint, gatt, gqkv1 = pin((other_a, local_b, joint, gatt, gqkv1))
        local_b = total(local_b, swap(local_b, "rep", 1, reps))
    joint = scatter(joint)
    gqkv2, dw2 = backward(2, gatt)
    gqkvs = [gqkv0, gqkv1, gqkv2]
    part = tile // 3 if tile % 48 == 0 else tile
    count = n // part
    cuts = [0, count // 3, 2 * count // 3, count]
    grad = lambda i, gmid, filled: input_grad(
        gqkvs, weights, tokens, gmid, part, cuts[i], cuts[i + 1], filled
    )
    if links:
        y, x, z, core = rep // 2, rep % 2, f // 2, f % 2
        zs, rows = size // 2, d // size
        cut = dw2.reshape(zs, 2, 2, 2, rows // reps, 3 * GW)
        keep, send = pick(cut, core, 1), pick(cut, 1 - core, 1)
        got = swap(send, "fsdp", 1, size)
        keep, local_b, gqkvs[2] = pin((keep, local_b, gqkvs[2]))
        other_b = swap(local_b, "rep", 2, reps)
        grad_tokens = grad(0, gmid, None)
        grad_tokens, keep, got, joint, other_b = pin((grad_tokens, keep, got, joint, other_b))
        side = swap(total(pick(keep, 1 - x, 2), pick(got, 1 - x, 2)), "rep", 1, reps)
        joint_x = swap(joint, "rep", 1, reps)
        keep = total(pick(keep, x, 2), pick(got, x, 2))
        keep, gmid = pin((keep, gmid))
        grad_tokens = grad(1, gmid, grad_tokens)
        grad_tokens, keep, side, joint_x = pin((grad_tokens, keep, side, joint_x))
        got = swap(total(pick(keep, 1 - y, 1), pick(side, 1 - y, 1)), "rep", 2, reps)
        joint = total(joint, joint_x)
        joint_y = swap(joint, "rep", 2, reps)
        keep, side = pick(keep, y, 1), pick(side, y, 1)
        keep, side, gmid = pin((keep, side, gmid))
        grad_tokens = grad(2, gmid, grad_tokens)
        grad_tokens, keep, side, got, joint_y = pin((grad_tokens, keep, side, got, joint_y))

        def at(k):
            i = (z + k) % zs
            return total(pick(keep, i), pick(side, i), pick(got, i))

        part = total(at(0), *[shift(at(zs - k), k, size) for k in range(1, zs)])
        every = over_reps(part, reps)
        dw2 = jnp.concatenate([pick(every, r ^ rep) for r in range(reps)], axis=0).astype(F32)
        joint = joint.astype(F32) + joint_y.astype(F32)
        sum_a = local_a.astype(F32) + other_a.astype(F32)
        sum_b = local_b.astype(F32) + other_b.astype(F32)
    else:
        grad_tokens = None
        for i in range(3):
            grad_tokens = grad(i, gmid, grad_tokens)
        dw2 = reduce(dw2)
        joint = sum_reps(joint, reps)
        if fast:
            sum_a, sum_b = sum_reps(local_a, reps), sum_reps(local_b, reps)
    dwo, dws = joint[:, :d], [joint[:, d : d + 3 * GW], joint[:, d + 3 * GW :], dw2]

    both = []
    if fast:
        both = [unpack_mlp(x, d // SHARDS, d) for x in (sum_a, sum_b)]
    else:
        both = [jax.vmap(lambda p: unpack_mlp(p, d // SHARDS, d))(grad) for grad in (grad_a, grad_b)]

    def rejoin(pair, axis):
        lead = pair[0].shape[:axis]
        rest = pair[0].shape[axis + 1 :]
        parts = [p.reshape(lead + (SHARDS if axis else 1, -1) + rest) for p in pair]
        return jnp.stack(parts, axis=axis + 1).reshape(lead + (-1,) + rest)

    if size == SHARDS:
        raw = [rejoin([b[i] for b in both], axis) for i, axis in ((0, 1), (1, 1), (2, 0))]
    else:
        raw = []
        for i, axis in ((0, 1), (1, 1), (2, 0)):
            whole = jax.vmap(lambda a, b: rejoin([a, b], axis))(both[0][i], both[1][i])
            raw.append(reduce(whole.reshape(-1, whole.shape[-1])))
    g2 = jnp.sum(raw[0] * w_gate.astype(F32), axis=1) + jnp.sum(raw[1] * w_up.astype(F32), axis=1)
    dwg, dwu, dwd = raw[0] * gain2, raw[1] * gain2, raw[2]

    raw = [jnp.concatenate([w[:, i * GW : (i + 1) * GW] for w in dws], axis=1) for i in range(3)]
    raw = [natural_order(raw[0]), natural_order(raw[1]), raw[2]]
    g1 = sum(jnp.sum(r * w.astype(F32), axis=1) for r, w in zip(raw, (w_query, w_key, w_value)))
    dwq, dwk, dwv = (r * gain1 for r in raw)
    return out, grad_tokens, g1, dwq, dwk, dwv, dwo, g2, dwg, dwu, dwd


def solution(mesh):
    in_specs = (
        P(("rep", "fsdp"), None),
        P(("rep", "fsdp"), None),
        P(("rep", "fsdp")),
        P(("rep", "fsdp"), None, None),
        P("fsdp"),
        P("fsdp", None),
        P("fsdp", None),
        P("fsdp", None),
        P("fsdp", None),
        P("fsdp"),
        P("fsdp", None),
        P("fsdp", None),
        P("fsdp", None),
    )
    out_specs = (
        P(("rep", "fsdp"), None),
        P(("rep", "fsdp"), None),
        P("fsdp"),
        P("fsdp", None),
        P("fsdp", None),
        P("fsdp", None),
        P("fsdp", None),
        P("fsdp"),
        P("fsdp", None),
        P("fsdp", None),
        P("fsdp", None),
    )
    sizes = dict(reps=mesh.shape["rep"], size=mesh.shape["fsdp"])
    return jax.shard_map(functools.partial(body, **sizes), mesh=mesh, in_specs=in_specs, out_specs=out_specs, check_vma=False)
```

```python
import functools
import jax
import jax.numpy as jnp
import numpy as np
from jax import lax
from jax.experimental import pallas as pl
from jax.experimental.pallas import tpu as pltpu
from jax.sharding import PartitionSpec as P

HEAD_DIM = 64
COLS = 24
GRID = 32
EPSILON = 1e-05
GROUP = 4
GW = GROUP * HEAD_DIM
HALF = GW // 2
BF = jnp.bfloat16
F32 = jnp.float32


def nn(a, b):
    return lax.dot_general(a, b, (((1,), (0,)), ((), ())), preferred_element_type=F32)


def nt(a, b):
    return lax.dot_general(a, b, (((1,), (1,)), ((), ())), preferred_element_type=F32)


def tn(a, b):
    return lax.dot_general(a, b, (((0,), (0,)), ((), ())), preferred_element_type=F32)


def params(limit=60):
    return pltpu.CompilerParams(vmem_limit_bytes=limit * 1024 * 1024)


def cost(flops, moved):
    return pl.CostEstimate(flops=int(flops), transcendentals=0, bytes_accessed=int(moved))


def inverse_rms(x):
    return lax.rsqrt(jnp.mean(x * x, axis=-1, keepdims=True) + EPSILON)


def angle_table():
    lane = np.arange(HALF)
    theta = (1.0 / 10000.0 ** (np.arange(HEAD_DIM // 4) * 4.0 / HEAD_DIM)).astype(np.float32)
    angle = np.arange(GRID, dtype=np.float32)[:, None] * theta[lane % (HEAD_DIM // 4)]
    by_row = (lane // (HEAD_DIM // 4)) % 2 == 0
    both = np.concatenate([np.cos(angle.astype(np.float64)), np.sin(angle.astype(np.float64))], axis=1)
    use = np.concatenate([by_row, by_row])
    left = np.concatenate([np.where(use, both, 0.0), np.where(use, 0.0, both)], axis=0).astype(np.float32)
    parts = []
    for _ in range(3):
        part = left.astype(jnp.bfloat16)
        parts.append(part)
        left = left - part.astype(np.float32)
    return np.concatenate(parts, axis=1)


def norm_kernel(x_ref, rope_ref, table_ref, out_ref, cos_ref, sin_ref):
    x = x_ref[...].astype(F32)
    out_ref[...] = (x * inverse_rms(x)).astype(BF)
    slot = x.shape[0]
    place = lax.broadcasted_iota(jnp.int32, (GRID, slot), 0)
    hot = jnp.concatenate([place == rope_ref[0, i : i + 1, :] for i in range(2)], axis=0)
    found = tn(jnp.where(hot, 1.0, 0.0).astype(BF), table_ref[...])
    found = found[:, :GW] + found[:, GW : 2 * GW] + found[:, 2 * GW :]
    cos_ref[...] = found[:, :HALF]
    sin_ref[...] = found[:, HALF:]


def norm_call(x, positions):
    n, d = x.shape
    crops, two, slot = positions.shape
    spec = lambda w: pl.BlockSpec((slot, w), lambda i: (i, 0))
    table = jnp.asarray(angle_table())
    return pl.pallas_call(
        norm_kernel,
        grid=(crops,),
        in_specs=[
            spec(d),
            pl.BlockSpec((1, two, slot), lambda i: (i, 0, 0)),
            pl.BlockSpec(table.shape, lambda i: (0, 0)),
        ],
        out_specs=[spec(d), spec(HALF), spec(HALF)],
        out_shape=[
            jax.ShapeDtypeStruct((n, d), BF),
            jax.ShapeDtypeStruct((n, HALF), F32),
            jax.ShapeDtypeStruct((n, HALF), F32),
        ],
        compiler_params=params(),
        cost_estimate=cost(0, 12 * n * d),
        name="norm_in",
    )(x, positions, table)


def head_masks():
    lane = lax.broadcasted_iota(jnp.int32, (1, GW), 1)
    rot = [((lane % HALF) // (HEAD_DIM // 2) == h) for h in range(GROUP)]
    nat = [(lane // HEAD_DIM == h) for h in range(GROUP)]
    return rot, nat


def mask_to(x, m):
    return x * jnp.where(m, 1.0, 0.0).astype(x.dtype)


def blocks_of(total, size):
    return [(s, min(s + size, total)) for s in range(0, total, size)]


def attn_fwd_kernel(slot, size, pair, ids_ref, nm_ref, cos_ref, sin_ref, own_hbm, oth_hbm,
                    qkv_ref, att_ref, lse_ref, w_out_ref, sem):
    group = pl.program_id(0)
    crop = pl.program_id(1)
    crops = pl.num_programs(1)
    zs = own_hbm.shape[1]
    rep, z, core = ids_ref[crops], ids_ref[crops + 1], ids_ref[crops + 2]

    @pl.when(crop == 0)
    def _():
        made = []
        for hbm, place in ((own_hbm, core), (oth_hbm, 1 - core)):
            for kind in range(4):
                for j in range(zs):
                    src = hbm.at[kind ^ rep, j, :, pl.ds(pl.multiple_of(group * GW, GW), GW)]
                    dst = w_out_ref.at[(z + j) & (zs - 1), place, :, pl.ds(kind * GW, GW)]
                    made.append(pltpu.make_async_copy(src, dst, sem.at[len(made)]))
        for copy in made:
            copy.start()
        for copy in made:
            copy.wait()

    nm = nm_ref[...]
    cos = cos_ref[...]
    sin = sin_ref[...]
    rot_m, nat_m = head_masks()
    d = nm.shape[1]

    def rotated(lo, scale):
        u = nn(nm, w_out_ref[:, :, :, lo : lo + GW].reshape(d, GW))
        a, b = u[:, :HALF], u[:, HALF:]
        r = jnp.concatenate([a * cos - b * sin, a * sin + b * cos], axis=1)
        return r.astype(BF) * jnp.asarray(scale, BF)

    q = rotated(0, HEAD_DIM ** (-0.5))
    k = rotated(GW, 1.0)
    v = nn(nm, w_out_ref[:, :, :, 2 * GW : 3 * GW].reshape(d, GW)).astype(BF)
    qkv_ref[:, :GW] = q
    qkv_ref[:, GW : 2 * GW] = k
    qkv_ref[:, 2 * GW :] = v
    qs = [mask_to(q, m) for m in rot_m]
    lane = lax.broadcasted_iota(jnp.int32, (1, 128), 1)
    units = [(s, e, h) for s, e in blocks_of(slot, size) for h in range(0, GROUP, pair)]

    def scores(s, e, h):
        stack = jnp.concatenate([qs[i][s:e] for i in range(h, h + pair)], axis=0)
        return nt(stack, k[s:e]), nt(stack, k[:s]) if s else None

    out = logs = None
    ready = scores(*units[0])
    for i, (s, e, h) in enumerate(units):
        later = scores(*units[i + 1]) if i + 1 < len(units) else None
        diag, left = ready
        w = e - s
        row = lax.broadcasted_iota(jnp.int32, (pair, w, w), 1).reshape(pair * w, w)
        col = lax.broadcasted_iota(jnp.int32, (pair, w, w), 2).reshape(pair * w, w)
        diag = jnp.where(row >= col, diag, -1e30)
        top = jnp.max(diag, axis=-1, keepdims=True)
        if s:
            top = jnp.maximum(top, jnp.max(left, axis=-1, keepdims=True))
        pd = jnp.exp(diag - top)
        total = jnp.sum(pd, axis=-1, keepdims=True)
        o = nn(pd.astype(BF), v[s:e])
        if s:
            pleft = jnp.exp(left - top)
            total = total + jnp.sum(pleft, axis=-1, keepdims=True)
            o = o + nn(pleft.astype(BF), v[:s])
        o = o * (1.0 / total)
        log = top + jnp.log(total)
        for g in range(pair):
            part = slice(g * w, (g + 1) * w)
            out = jnp.where(nat_m[h + g], o[part], out if h + g else 0.0)
            logs = jnp.where(lane == h + g, log[part], logs if h + g else 0.0)
        if h + pair == GROUP:
            att_ref[s:e, :] = out.astype(BF)
            lse_ref[0, 0, :, s:e] = logs.T[:8]
        ready = later


def attn_fwd(ids, nm, cos, sin, own, oth, slot, size=256, pair=4):
    n, d = nm.shape
    crops = n // slot
    kinds, zs, rows, width = own.shape
    groups = width // GW
    hbm = pl.BlockSpec(memory_space=pl.ANY)
    crop_spec = lambda w: pl.BlockSpec((slot, w), lambda g, c, *_: (c, 0))
    qkv, att, lse, w = pl.pallas_call(
        functools.partial(attn_fwd_kernel, slot, size, pair),
        grid_spec=pltpu.PrefetchScalarGridSpec(
            num_scalar_prefetch=1,
            grid=(groups, crops),
            in_specs=[crop_spec(d), crop_spec(HALF), crop_spec(HALF), hbm, hbm],
            out_specs=[
                pl.BlockSpec((slot, 3 * GW), lambda g, c, *_: (c, g)),
                pl.BlockSpec((slot, GW), lambda g, c, *_: (c, g)),
                pl.BlockSpec((1, 1, 8, slot), lambda g, c, *_: (g, c, 0, 0)),
                pl.BlockSpec((zs, 2, rows, 4 * GW), lambda g, c, *_: (0, 0, 0, g)),
            ],
            scratch_shapes=[pltpu.SemaphoreType.DMA((8 * zs,))],
        ),
        out_shape=[
            jax.ShapeDtypeStruct((n, groups * 3 * GW), BF),
            jax.ShapeDtypeStruct((n, groups * GW), BF),
            jax.ShapeDtypeStruct((groups, crops, 8, slot), F32),
            jax.ShapeDtypeStruct((zs, 2, rows, groups * 4 * GW), BF),
        ],
        compiler_params=params(),
        cost_estimate=cost(8e6 * groups * n, 2 * n * d),
        name="attn_fwd",
    )(ids, nm, cos, sin, own, oth)
    return qkv, att, lse, w.reshape(d, groups * 4 * GW)


def attn_bwd_kernel(slot, size, pair, qkv_ref, go_ref, att_ref, lse_ref, nm_ref, cos_ref, sin_ref, *refs):
    gqkv_ref, dw_ref, ds_ref, dq_ref, acc_ref = refs[-5:]
    crop = pl.program_id(1)
    q = qkv_ref[:, :GW]
    k = qkv_ref[:, GW : 2 * GW]
    v = qkv_ref[:, 2 * GW :]
    go = go_ref[...]
    rot_m, nat_m = head_masks()
    prod = go.astype(F32) * att_ref[...].astype(F32)
    hi = prod.astype(BF)
    lo = (prod - hi.astype(F32)).astype(BF)
    pick = (
        lax.broadcasted_iota(jnp.int32, (8, GW), 1) // HEAD_DIM
        == lax.broadcasted_iota(jnp.int32, (8, GW), 0)
    )
    pick = jnp.where(pick, 1.0, 0.0).astype(BF)
    delta = nt(pick, hi) + nt(pick, lo)
    blocks = blocks_of(slot, size)
    dk = [None] * len(blocks)
    dv = [None] * len(blocks)
    kms = [mask_to(k, m) for m in rot_m]
    vms = [mask_to(v, m) for m in nat_m]
    units = [(j, s, e, h) for j, (s, e) in enumerate(blocks) for h in range(0, GROUP, pair)]

    def stacked(parts, s, e, h):
        return jnp.concatenate([parts[i][s:e] for i in range(h, h + pair)], axis=0)

    def scores(j, s, e, h):
        return nt(stacked(kms, s, e, h), q[s:]), nt(stacked(vms, s, e, h), go[s:])

    ready = scores(*units[0])
    for i, (j, s, e, h) in enumerate(units):
        later = scores(*units[i + 1]) if i + 1 < len(units) else None
        w = e - s
        row = lax.broadcasted_iota(jnp.int32, (w, w), 0)
        col = lax.broadcasted_iota(jnp.int32, (w, w), 1)
        ps, dss = [], []
        for g in range(pair):
            sc, dp = (x[g * w : (g + 1) * w] for x in ready)
            p = jnp.exp(sc - lse_ref[0, 0, h + g : h + g + 1, s:])
            first = jnp.where(col >= row, p[:, :w], 0.0)
            p = jnp.concatenate([first, p[:, w:]], axis=1) if e < slot else first
            ds = (p * (dp - delta[h + g : h + g + 1, s:])).astype(BF)
            ds_ref[h + g, s:, s:e] = ds.T
            ps.append(p.astype(BF))
            dss.append(ds)
        dvp = nn(jnp.concatenate(ps, axis=0), go[s:])
        dkp = nn(jnp.concatenate(dss, axis=0), q[s:])
        for g in range(pair):
            part = slice(g * w, (g + 1) * w)
            dv[j] = jnp.where(nat_m[h + g], dvp[part], dv[j] if h + g else 0.0)
            dk[j] = jnp.where(rot_m[h + g], dkp[part], dk[j] if h + g else 0.0)
        ready = later
    for s, e in blocks:
        w = e - s
        parts = nn(ds_ref[:, s:e, :e].reshape(GROUP * w, e), k[:e])
        dq = 0.0
        for h in range(GROUP):
            dq = jnp.where(rot_m[h], parts[h * w : (h + 1) * w], dq)
        dq_ref[s:e] = dq
    cos = cos_ref[...]
    sin = sin_ref[...]

    def back(u, c, t):
        a, b = u[:, :HALF], u[:, HALF:]
        return jnp.concatenate([a * c + b * t, b * c - a * t], axis=1).astype(BF)

    for j, (s, e) in enumerate(blocks):
        c, t = cos[s:e], sin[s:e]
        gqkv_ref[s:e, :GW] = back(dq_ref[s:e] * (HEAD_DIM ** (-0.5)), c, t)
        gqkv_ref[s:e, GW : 2 * GW] = back(dk[j], c, t)
        gqkv_ref[s:e, 2 * GW :] = dv[j].astype(BF)
    part = tn(nm_ref[...], gqkv_ref[...])

    @pl.when(crop == 0)
    def _():
        acc_ref[...] = part

    @pl.when(crop != 0)
    def _():
        acc_ref[...] += part

    @pl.when(crop == pl.num_programs(1) - 1)
    def _():
        dw_ref[...] = acc_ref[...].astype(BF)


def attn_bwd(qkv, go, att, lse, nm, cos, sin, slot, place, first, joint=None, size=128, pair=4):
    n, d = nm.shape
    crops = n // slot
    more = [] if joint is None else [joint]
    column = 0 if joint is None else first + place + 1
    row_spec = lambda w, at: pl.BlockSpec((slot, w), lambda g, c: (c, at))
    crop_spec = lambda w: pl.BlockSpec((slot, w), lambda g, c: (c, 0))
    return pl.pallas_call(
        functools.partial(attn_bwd_kernel, slot, size, pair),
        grid=(1, crops),
        in_specs=[
            row_spec(3 * GW, place),
            row_spec(GW, first + place),
            row_spec(GW, place),
            pl.BlockSpec((1, 1, 8, slot), lambda g, c: (place, c, 0, 0)),
            crop_spec(d),
            crop_spec(HALF),
            crop_spec(HALF),
        ]
        + [pl.BlockSpec(memory_space=pl.ANY)] * len(more),
        out_specs=[crop_spec(3 * GW), pl.BlockSpec((d, 3 * GW), lambda g, c: (0, column))],
        out_shape=[
            jax.ShapeDtypeStruct((n, 3 * GW), BF),
            jax.ShapeDtypeStruct((d, 3 * GW) if joint is None else joint.shape, BF),
        ],
        input_output_aliases={7: 1} if more else {},
        scratch_shapes=[
            pltpu.VMEM((GROUP, slot, slot), BF),
            pltpu.VMEM((slot, GW), F32),
            pltpu.VMEM((d, 3 * GW), F32),
        ],
        compiler_params=params(),
        cost_estimate=cost(12e6 * n, 2 * n * d),
        name="attn_bwd",
    )(qkv, go, att, lse, nm, cos, sin, *more)


def valid_rows(ids_ref, tile, rows, slot):
    row = tile * rows + lax.broadcasted_iota(jnp.int32, (rows, 1), 0)
    crop = row // slot
    first = tile * rows // slot
    limit = jnp.zeros((rows, 1), jnp.int32)
    for i in range(-(-rows // slot) + 1):
        index = first + i
        limit = jnp.where(crop == index, ids_ref[index] * COLS, limit)
    return row - crop * slot < limit


def out_weights(weights, d):
    arrays, specs = [], []
    for w in weights:
        for g in range(w.shape[1] // (4 * GW)):
            arrays.append(w)
            specs.append(pl.BlockSpec((d, GW), lambda c, *_, g=g: (0, 4 * g + 3)))
    return arrays, specs


def out_proj_kernel(slot, n_att, ids_ref, x_ref, *refs):
    att_refs, refs = refs[:n_att], refs[n_att:]
    *wo_refs, mid_ref, nm_ref = refs
    valid = valid_rows(ids_ref, pl.program_id(0), x_ref.shape[0], slot)
    att = jnp.concatenate([a[...] for a in att_refs], axis=1)
    proj = jnp.concatenate([nn(att, w[...]) for w in wo_refs], axis=1)
    mid = x_ref[...].astype(F32) + jnp.where(valid, proj, 0.0)
    mid_ref[...] = mid
    nm_ref[...] = (mid * inverse_rms(mid)).astype(BF)


def out_proj(ids, x, atts, weights, slot, tile):
    n, d = x.shape
    rows = lambda w: pl.BlockSpec((tile, w), lambda c, *_: (c, 0))
    wos, wo_specs = out_weights(weights, d)
    return pl.pallas_call(
        functools.partial(out_proj_kernel, slot, len(atts)),
        grid_spec=pltpu.PrefetchScalarGridSpec(
            num_scalar_prefetch=1,
            grid=(n // tile,),
            in_specs=[rows(d)] + [rows(a.shape[1]) for a in atts] + wo_specs,
            out_specs=[rows(d), rows(d)],
        ),
        out_shape=[jax.ShapeDtypeStruct((n, d), F32), jax.ShapeDtypeStruct((n, d), BF)],
        compiler_params=params(),
        cost_estimate=cost(2 * n * d * d, 10 * n * d),
        name="out_proj",
    )(ids, x, *atts, *wos)


PACK = 512
TILE = 768
SHARDS = 8


def halves(w, axis):
    shape = w.shape[:axis] + (-1, 2, w.shape[axis] // (2 * SHARDS) if axis else w.shape[0] // 2) + w.shape[axis + 1 :]
    w = w.reshape(shape)
    return [
        lax.index_in_dim(w, i, axis + 1, keepdims=False).reshape(w.shape[:axis] + (-1,) + w.shape[axis + 3 :])
        for i in range(2)
    ]


def pack_mlp(gate, up, down):
    wide = [w[:, i : i + PACK] for w in (gate, up) for i in range(0, w.shape[1], PACK)]
    half = down.shape[0] // 2
    tail = down[:, PACK:]
    fold = jnp.concatenate([tail[:half], tail[half:]], axis=1)
    return jnp.concatenate(wide + [down[:, :PACK], fold], axis=0)


def unpack_mlp(pack, rows, d):
    chunks = 2
    gate, up = (
        jnp.concatenate([pack[i * rows : (i + 1) * rows] for i in range(s, s + chunks)], axis=1)
        for s in (0, chunks)
    )
    base = 2 * chunks * rows
    deep = (pack.shape[0] - base) * PACK // d
    fold = pack[base + deep :]
    tail = jnp.concatenate([fold[:, : d - PACK], fold[:, d - PACK :]], axis=0)
    return gate, up, jnp.concatenate([pack[base : base + deep], tail], axis=1)


def mlp_kernel(slot, final, step, ids_ref, nm_ref, cot_ref, part_ref, *refs):
    if final:
        before_ref, *refs = refs
    (pack_hbm, out_ref, dn_ref, grad_hbm, wg_buf, wu_buf, wd_buf, hid_ref, gg_ref, gu_ref,
     ag_ref, au_ref, ad_ref, sg_ref, su_ref, sd_ref, in_sem, out_sem) = refs
    tile = pl.program_id(0)
    d = nm_ref.shape[1]
    chunks, shards, rows, _ = sg_ref.shape
    units = chunks * PACK
    some = shards // chunks
    deep = sd_ref.shape[1]
    base = 2 * chunks * rows
    side = d - PACK

    def pieces(hbm, wg, wu, wd):
        for i in range(chunks):
            yield hbm.at[:, pl.ds(i * rows, rows), :], wg.at[i]
            yield hbm.at[:, pl.ds((chunks + i) * rows, rows), :], wu.at[i]
        yield hbm.at[:, pl.ds(base, deep), :], wd.at[:, :, pl.ds(0, PACK)]
        for i in range(2):
            yield (
                hbm.at[:, pl.ds(base + deep, deep // 2), pl.ds(i * side, side)],
                wd.at[:, pl.ds(i * (deep // 2), deep // 2), pl.ds(PACK, side)],
            )

    @pl.when(tile == 0)
    def _():
        made = pieces(pack_hbm, wg_buf, wu_buf, wd_buf)
        made = [pltpu.make_async_copy(a, b, in_sem.at[i]) for i, (a, b) in enumerate(made)]
        for copy in made:
            copy.start()
        ag_ref[...] = jnp.zeros_like(ag_ref)
        au_ref[...] = jnp.zeros_like(au_ref)
        ad_ref[...] = jnp.zeros_like(ad_ref)
        for copy in made:
            copy.wait()

    valid = valid_rows(ids_ref, tile, nm_ref.shape[0], slot)
    nm = nm_ref[...]
    gb = jnp.where(valid, cot_ref[...], jnp.zeros((), BF))
    wd = wd_buf[...].reshape(units, d)

    def wide(buf, i):
        at = i * step
        return buf[at // PACK, :, :, at % PACK : at % PACK + step].reshape(d, step)

    def first(i):
        return (
            nn(nm, wide(wg_buf, i)),
            nn(nm, wide(wu_buf, i)),
            nt(gb, wd[i * step : (i + 1) * step]),
        )

    def second(i, g, u, gh):
        cols = slice(i * step, (i + 1) * step)
        sg = 0.5 * jnp.tanh(0.5 * g) + 0.5
        act = g * sg
        hid_ref[:, cols] = (act * u).astype(BF)
        gu_ref[:, cols] = (gh * act).astype(BF)
        gg_ref[:, cols] = (gh * u * (sg + act * (1.0 - sg))).astype(BF)

    ready = first(0)
    for i in range(1, units // step):
        later = first(i)
        second(i - 1, *ready)
        ready = later
    second(units // step - 1, *ready)
    nmt = nm.T
    gbt = gb.T
    o = part_ref[...] + jnp.where(valid, nn(hid_ref[...], wd), 0.0)
    out_ref[...] = o.astype(out_ref.dtype)
    dn = before_ref[...] if final else 0.0
    for i in range(chunks):
        cols = slice(i * PACK, (i + 1) * PACK)
        dn = dn + nt(gg_ref[:, cols], wg_buf[i].reshape(d, PACK)) + nt(gu_ref[:, cols], wu_buf[i].reshape(d, PACK))
    dn_ref[...] = dn
    for i in range(chunks):
        cols = slice(i * PACK, (i + 1) * PACK)
        ag_ref[i] += nn(nmt, gg_ref[:, cols])
        au_ref[i] += nn(nmt, gu_ref[:, cols])
        ad_ref[i] += nn(gbt, hid_ref[:, cols])

    @pl.when(tile == pl.num_programs(0) - 1)
    def _():
        sg_ref[...] = ag_ref[...].astype(BF).reshape(sg_ref.shape)
        su_ref[...] = au_ref[...].astype(BF).reshape(su_ref.shape)
        for i in range(chunks):
            sd_ref[i * some : (i + 1) * some] = ad_ref[i].astype(BF).T.reshape(some, deep, d)
        made = pieces(grad_hbm, sg_ref, su_ref, sd_ref)
        made = [pltpu.make_async_copy(b, a, out_sem.at[i]) for i, (a, b) in enumerate(made)]
        for copy in made:
            copy.start()
        for copy in made:
            copy.wait()


def mlp(ids, nm, cot, part, before, pack, slot, tile, step=256):
    n, d = nm.shape
    rows = d // SHARDS
    chunks = 2
    deep = chunks * PACK // SHARDS
    final = before is not None
    spec = pl.BlockSpec((tile, d), lambda i, *_: (i, 0))
    hbm = pl.BlockSpec(memory_space=pl.ANY)
    packed = pltpu.VMEM((chunks, SHARDS, rows, PACK), BF)
    units = pltpu.VMEM((tile, chunks * PACK), BF)
    sums = pltpu.VMEM((chunks, d, PACK), F32)
    return pl.pallas_call(
        functools.partial(mlp_kernel, slot, final, step),
        grid_spec=pltpu.PrefetchScalarGridSpec(
            num_scalar_prefetch=1,
            grid=(n // tile,),
            in_specs=[spec] * (3 + final) + [hbm],
            out_specs=[spec, spec, hbm],
            scratch_shapes=[packed, packed, pltpu.VMEM((SHARDS, deep, d), BF)]
            + [units] * 3
            + [sums] * 3
            + [packed, packed, pltpu.VMEM((SHARDS, deep, d), BF)]
            + [pltpu.SemaphoreType.DMA((2 * chunks + 3,))] * 2,
        ),
        out_shape=[
            jax.ShapeDtypeStruct((n, d), BF if final else F32),
            jax.ShapeDtypeStruct((n, d), F32),
            jax.ShapeDtypeStruct(pack.shape, BF),
        ],
        compiler_params=params(),
        cost_estimate=cost(24e6 * n, 20 * n * d),
        name="mlp",
    )(ids, nm, cot, part, *([before] if final else []), pack)


def norm_back(scaled, field):
    inv = inverse_rms(field)
    return inv * scaled - field * (inv * inv * inv * jnp.mean(scaled * field, axis=-1, keepdims=True))


def mid_grad_kernel(slot, n_att, ids_ref, cot_ref, mid_ref, dn_ref, *refs):
    att_refs, refs = refs[:n_att], refs[n_att:]
    *wo_refs, gmid_ref, gatt_ref, dwo_ref, acc_ref = refs
    c = pl.program_id(0)
    valid = valid_rows(ids_ref, c, cot_ref.shape[0], slot)
    gm = cot_ref[...].astype(F32) + norm_back(dn_ref[...], mid_ref[...])
    gmid_ref[...] = gm
    ga = jnp.where(valid, gm, 0.0).astype(BF)
    gatt = sum(nt(ga[:, i * GW : (i + 1) * GW], w[...]) for i, w in enumerate(wo_refs))
    gatt_ref[...] = gatt.astype(BF)
    part = tn(jnp.concatenate([a[...] for a in att_refs], axis=1), ga)

    @pl.when(c == 0)
    def _():
        acc_ref[...] = part

    @pl.when(c != 0)
    def _():
        acc_ref[...] += part

    @pl.when(c == pl.num_programs(0) - 1)
    def _():
        dwo_ref[...] = acc_ref[...].astype(BF)


def mid_grad(ids, cot, mid, dn, atts, weights, slot, tile):
    n, d = cot.shape
    rows = lambda w: pl.BlockSpec((tile, w), lambda c, *_: (c, 0))
    wos, wo_specs = out_weights(weights, d)
    return pl.pallas_call(
        functools.partial(mid_grad_kernel, slot, len(atts)),
        grid_spec=pltpu.PrefetchScalarGridSpec(
            num_scalar_prefetch=1,
            grid=(n // tile,),
            in_specs=[rows(d)] * 3 + [rows(a.shape[1]) for a in atts] + wo_specs,
            out_specs=[rows(d), rows(d), pl.BlockSpec((d, d), lambda c, *_: (0, 0))],
            scratch_shapes=[pltpu.VMEM((d, d), F32)],
        ),
        out_shape=[
            jax.ShapeDtypeStruct((n, d), F32),
            jax.ShapeDtypeStruct((n, d), BF),
            jax.ShapeDtypeStruct((d, 3 * d), BF),
        ],
        compiler_params=params(),
        cost_estimate=cost(4 * n * d * d, 18 * n * d),
        name="mid_grad",
    )(ids, cot, mid, dn, *atts, *wos)


def input_grad_kernel(n_group, *refs):
    g_refs, w_refs = refs[:n_group], refs[n_group : 4 * n_group]
    x_ref, gmid_ref = refs[4 * n_group : 4 * n_group + 2]
    out_ref = refs[-1]
    e = 0.0
    for i, g in enumerate(g_refs):
        w = jnp.concatenate([w[...] for w in w_refs[3 * i : 3 * i + 3]], axis=1)
        e = e + nt(g[...], w)
    out_ref[...] = gmid_ref[...] + norm_back(e, x_ref[...].astype(F32))


def input_grad(gqkvs, weights, x, gmid, rows, start, stop, filled=None):
    n, d = x.shape
    arrays = [(w, 4 * g + i) for w in weights for g in range(w.shape[1] // (4 * GW)) for i in range(3)]
    spec = lambda w: pl.BlockSpec((rows, w), lambda i: (start + i, 0))
    more = [] if filled is None else [filled]
    n_in = 4 * len(gqkvs) + 2
    count = (stop - start) * rows
    return pl.pallas_call(
        functools.partial(input_grad_kernel, len(gqkvs)),
        grid=(stop - start,),
        in_specs=[spec(3 * GW)] * len(gqkvs)
        + [pl.BlockSpec((d, GW), lambda i, g=g: (0, g)) for _, g in arrays]
        + [spec(d), spec(d)]
        + [pl.BlockSpec(memory_space=pl.ANY)] * len(more),
        out_specs=spec(d),
        out_shape=jax.ShapeDtypeStruct((n, d), F32),
        input_output_aliases={n_in: 0} if more else {},
        compiler_params=params(),
        cost_estimate=cost(6 * count * d * d, 16 * count * d),
        name="input_grad",
    )(*gqkvs, *[w for w, _ in arrays], x, gmid, *more)


def row_of(column):
    return jnp.broadcast_to(column, (column.shape[0], 128)).T[:1]


def mlp_end_kernel(a0_ref, a1_ref, b0_ref, b1_ref, wg_ref, wu_ref, gain_ref, dwg_ref, dwu_ref, dwd_ref, g_ref):
    rows = wg_ref.shape[0]
    units = wg_ref.shape[1] // (2 * SHARDS)
    deep = dwd_ref.shape[0] // 2
    side = dwd_ref.shape[1] - PACK
    chunks = wg_ref.shape[1] // (2 * PACK)
    base = 2 * chunks * rows
    gain = gain_ref[...]
    dot = jnp.zeros((rows, units), F32)
    for half, (left, right) in enumerate(((a0_ref, a1_ref), (b0_ref, b1_ref))):
        for w_ref, out_ref, first in ((wg_ref, dwg_ref, 0), (wu_ref, dwu_ref, chunks)):
            for i in range(chunks):
                at = (first + i) * rows
                block = left[at : at + rows].astype(F32) + right[at : at + rows].astype(F32)
                for j in range(PACK // units):
                    to = (i * (PACK // units) + j) * 2 * units + half * units
                    part = block[:, j * units : (j + 1) * units]
                    dot = dot + part * w_ref[:, to : to + units].astype(F32)
                    out_ref[:, to : to + units] = part * gain
        down = left[base:].astype(F32) + right[base:].astype(F32)
        at = half * deep
        dwd_ref[at : at + deep, :PACK] = down[:deep]
        for i in range(2):
            to = at + i * (deep // 2)
            dwd_ref[to : to + deep // 2, PACK:] = down[deep:, i * side : (i + 1) * side]
    g_ref[...] = row_of(jnp.sum(dot, axis=1, keepdims=True))


def mlp_end(a0, a1, b0, b1, wg, wu, gain, down_shape):
    rows = wg.shape[0]
    return pl.pallas_call(
        mlp_end_kernel,
        out_shape=[
            jax.ShapeDtypeStruct(wg.shape, F32),
            jax.ShapeDtypeStruct(wu.shape, F32),
            jax.ShapeDtypeStruct(down_shape, F32),
            jax.ShapeDtypeStruct((1, rows), F32),
        ],
        compiler_params=params(),
        cost_estimate=cost(0, 6e6),
        name="mlp_end",
    )(a0, a1, b0, b1, wg, wu, gain)


def attn_end_kernel(place_ref, left_ref, right_ref, last_ref, wq_ref, wk_ref, wv_ref, gain_ref,
                    dwq_ref, dwk_ref, dwv_ref, dwo_ref, g_ref, last_buf):
    rows, d = wq_ref.shape
    reps, few, _ = last_ref.shape
    gain = gain_ref[...]
    for r in range(reps):
        last_buf[r * few : (r + 1) * few] = last_ref[r ^ place_ref[0]].astype(F32)
    dwo_ref[...] = left_ref[:, :d].astype(F32) + right_ref[:, :d].astype(F32)
    lane = lax.broadcasted_iota(jnp.int32, (GW, GW), 1)
    half = HEAD_DIM // 2
    source = lane // HEAD_DIM * half + lane % half + jnp.where(lane % HEAD_DIM < half, 0, HALF)
    order = jnp.where(lax.broadcasted_iota(jnp.int32, (GW, GW), 0) == source, 1.0, 0.0).astype(BF)
    groups = d // GW
    dot = jnp.zeros((rows, GW), F32)
    for g in range(groups):
        for kind, (w_ref, out_ref) in enumerate(((wq_ref, dwq_ref), (wk_ref, dwk_ref), (wv_ref, dwv_ref))):
            at = d + (3 * g + kind) * GW
            if g == groups - 1:
                block = last_buf[:, kind * GW : (kind + 1) * GW]
            else:
                block = left_ref[:, at : at + GW].astype(F32) + right_ref[:, at : at + GW].astype(F32)
            if kind < 2:
                moved = 0.0
                for _ in range(3):
                    part = block.astype(BF)
                    moved = moved + nn(part, order)
                    block = block - part.astype(F32)
                block = moved
            cols = slice(g * GW, (g + 1) * GW)
            dot = dot + block * w_ref[:, cols].astype(F32)
            out_ref[:, cols] = block * gain
    g_ref[...] = row_of(jnp.sum(dot, axis=1, keepdims=True))


def attn_end(place, left, right, last, wq, wk, wv, gain):
    rows, d = wq.shape
    vmem = pl.BlockSpec(memory_space=pltpu.VMEM)
    return pl.pallas_call(
        attn_end_kernel,
        grid_spec=pltpu.PrefetchScalarGridSpec(
            num_scalar_prefetch=1,
            grid=(1,),
            in_specs=[vmem] * 7,
            out_specs=[vmem] * 5,
            scratch_shapes=[pltpu.VMEM((rows, 3 * GW), F32)],
        ),
        out_shape=[jax.ShapeDtypeStruct((rows, d), F32)] * 4 + [jax.ShapeDtypeStruct((1, rows), F32)],
        compiler_params=params(),
        cost_estimate=cost(0, 6e6),
        name="attn_end",
    )(place, left, right, last, wq, wk, wv, gain)


def rot_order(w):
    rows, cols = w.shape
    w = w.reshape(rows, cols // GW, GROUP, 2, HEAD_DIM // 2)
    return w.transpose(0, 1, 3, 2, 4).reshape(rows, cols)


def natural_order(w):
    rows, cols = w.shape
    w = w.reshape(rows, cols // GW, 2, GROUP, HEAD_DIM // 2)
    return w.transpose(0, 1, 3, 2, 4).reshape(rows, cols)


def join_attn(wq, wk, wv, wo, gain):
    scaled = [(w.astype(F32) * gain).astype(BF) for w in (rot_order(wq), rot_order(wk), wv)]
    return jnp.stack(scaled + [wo])


def swap(x, axis, bit, size):
    return lax.ppermute(x, axis, [(i, i ^ bit) for i in range(size)])


def shift(x, step, size):
    half = size // 2
    return lax.ppermute(x, "fsdp", [(((i // 2 + step) % half) * 2 + i % 2, i) for i in range(size)])


def pick(x, index, axis=0):
    return lax.dynamic_index_in_dim(x, index, axis, keepdims=False)


def total(*parts):
    return sum(p.astype(F32) for p in parts).astype(BF)


def along_z(mine, size):
    return jnp.stack([mine] + [shift(mine, k, size) for k in range(1, size // 2)])


def over_reps(x, reps):
    return jnp.stack([x] + [swap(x, "rep", bit, reps) for bit in range(1, reps)])


def sum_reps(x, reps):
    if reps != 4:
        return lax.psum(x, "rep").astype(F32)
    x = (x.astype(F32) + swap(x, "rep", 1, reps).astype(F32)).astype(BF)
    return x.astype(F32) + swap(x, "rep", 2, reps).astype(F32)


def body(tokens, cotangent, crop_heights, rope_positions, gain_attn, w_query, w_key, w_value, w_out,
         gain_mlp, w_gate, w_up, w_down, *, reps, size):
    crops = crop_heights.shape[0]
    n, d = tokens.shape
    slot = n // crops
    tile = TILE if n % TILE == 0 else slot
    gain1 = gain_attn.astype(F32)[:, None]
    gain2 = gain_mlp.astype(F32)[:, None]

    def gather(w):
        return lax.all_gather(w, "fsdp", axis=0, tiled=True)

    def scatter(g):
        return lax.psum_scatter(g, "fsdp", scatter_dimension=0, tiled=True)

    def reduce(g):
        return sum_reps(scatter(g), reps)

    pin = lax.optimization_barrier
    links = reps == 4 and size == SHARDS
    rep, f = lax.axis_index("rep"), lax.axis_index("fsdp")
    joined = join_attn(w_query, w_key, w_value, w_out, gain1)
    if links:
        place = jnp.stack([rep, f // 2, f % 2]).astype(jnp.int32)
        mine = pick(joined, rep)
        mine, w_gate, w_up, w_down = pin((mine, w_gate, w_up, w_down))
        lines = [along_z(m, size) for m in (mine[:, :GW], mine[:, GW:])]
        tokens_1 = tokens
        sides = [swap(lines[0], "rep", bit, reps) for bit in range(1, reps)]
    else:
        place = jnp.zeros((3,), jnp.int32)
        every = lax.all_gather(joined, "fsdp", axis=1, tiled=True)
        every = every.reshape(4, SHARDS // 2, 2, d // SHARDS, d)
    ids = jnp.concatenate([crop_heights, place])
    if not links:
        tokens_1 = tokens
    nm1, cos, sin = norm_call(tokens_1, rope_positions)
    if links:
        *sides, lines[1], nm1, cos, sin = pin((*sides, lines[1], nm1, cos, sin))
        own = jnp.stack([lines[0]] + sides)
        own, w_gate, w_up, w_down = pin((own, w_gate, w_up, w_down))
        oth = swap(own, "fsdp", 1, size)
    scaled = [(w.astype(F32) * gain2).astype(BF) for w in (w_gate, w_up)]
    split = list(zip(halves(scaled[0], 1), halves(scaled[1], 1), halves(w_down, 0)))
    if size == SHARDS:
        packs = [lax.all_gather(pack_mlp(*part), "fsdp", axis=0, tiled=False) for part in split]
    else:
        wide = [gather(w).reshape(SHARDS, -1, w.shape[1]) for w in scaled]
        down = gather(w_down).reshape(SHARDS, -1, d)
        split = zip(*[[jnp.stack(h) for h in zip(*[halves(w, a) for w in ws])] for ws, a in
                      ((wide[0], 1), (wide[1], 1), (down, 0))])
        packs = [jax.vmap(pack_mlp)(*part) for part in split]

    attended, weights = [], []
    for i, cols in enumerate((slice(0, GW), slice(GW, d))):
        if not links:
            own, oth = every[:, :, 0, :, cols], every[:, :, 1, :, cols]
        elif i:
            *parts, _ = pin((lines[1], *sides, atts))
            own = jnp.stack(parts)
            oth = swap(own, "fsdp", 1, size)
        else:
            sides = [swap(lines[1], "rep", bit, reps) for bit in range(1, reps)]
        *some, w = attn_fwd(ids, nm1, cos, sin, own, oth, slot)
        attended.append(some)
        weights.append(w)
        atts = [a for _, a, _ in attended]
    mid, nm2 = out_proj(ids, tokens, atts, weights, slot, tile)
    part, dn, grad_a = mlp(ids, nm2, cotangent, mid, None, packs[0], slot, tile)
    out, dn, grad_b = mlp(ids, nm2, cotangent, part, dn, packs[1], slot, tile)
    local_a = scatter(grad_a.reshape(-1, PACK)) if size == SHARDS else grad_a
    local_b = scatter(grad_b.reshape(-1, PACK)) if size == SHARDS else grad_b
    gmid, gatt, joint = mid_grad(ids, cotangent, mid, dn, atts, weights, slot, tile)

    def backward(index, gatt, joint=None):
        w = 0 if index == 0 else 1
        qkv, att, lse = attended[w]
        return attn_bwd(qkv, gatt, att, lse, nm1, cos, sin, slot, index - w, w, joint)

    fast = size == SHARDS
    if links:
        local_a, gatt = pin((local_a, gatt))
        local_a = total(local_a, swap(local_a, "rep", 1, reps))
    gqkv0, joint = backward(0, gatt, joint)
    if links:
        local_a, gatt, gqkv0 = pin((local_a, gatt, gqkv0))
        other_a = swap(local_a, "rep", 2, reps)
    gqkv1, joint = backward(1, gatt, joint)
    if links:
        other_a, local_b, joint, gatt, gqkv1 = pin((other_a, local_b, joint, gatt, gqkv1))
        local_b = total(local_b, swap(local_b, "rep", 1, reps))
    joint = scatter(joint)
    gqkv2, dw2 = backward(2, gatt)
    gqkvs = [gqkv0, gqkv1, gqkv2]
    grad = lambda gmid: input_grad(gqkvs, weights, tokens, gmid, tile // 2, 0, 2 * n // tile)
    if links:
        y, x, z, core = rep // 2, rep % 2, f // 2, f % 2
        zs, rows = size // 2, d // size
        cut = dw2.reshape(zs, 2, 2, 2, rows // reps, 3 * GW)
        keep, send = pick(cut, core, 1), pick(cut, 1 - core, 1)
        got = swap(send, "fsdp", 1, size)
        keep, local_b, gqkvs[2] = pin((keep, local_b, gqkvs[2]))
        other_b = swap(local_b, "rep", 2, reps)
        side = swap(total(pick(keep, 1 - x, 2), pick(got, 1 - x, 2)), "rep", 1, reps)
        keep = total(pick(keep, x, 2), pick(got, x, 2))
        keep, gmid = pin((keep, gmid))
        grad_tokens = grad(gmid)
        grad_tokens, keep, side, joint, local_a, other_a = pin((grad_tokens, keep, side, joint, local_a, other_a))
        got = swap(total(pick(keep, 1 - y, 1), pick(side, 1 - y, 1)), "rep", 2, reps)
        joint_x = swap(joint, "rep", 1, reps)
        keep, side = pick(keep, y, 1), pick(side, y, 1)
        *dmlp, g2 = mlp_end(local_a, other_a, local_b, other_b, w_gate, w_up, gain2, w_down.shape)
        dmlp[0], keep, side, got, joint, joint_x = pin((dmlp[0], keep, side, got, joint, joint_x))

        def at(k):
            i = (z + k) % zs
            return total(pick(keep, i), pick(side, i), pick(got, i))

        joint = total(joint, joint_x)
        joint_y = swap(joint, "rep", 2, reps)
        part = total(at(0), *[shift(at(zs - k), k, size) for k in range(1, zs)])
        every = over_reps(part, reps)
        *dattn, g1 = attn_end(place, joint, joint_y, every, w_query, w_key, w_value, gain1)
        return (out, grad_tokens, g1.reshape(-1), *dattn, g2.reshape(-1), *dmlp)

    grad_tokens = grad(gmid)
    dw2 = reduce(dw2)
    joint = sum_reps(joint, reps)
    if fast:
        sum_a, sum_b = sum_reps(local_a, reps), sum_reps(local_b, reps)
    both = []
    if fast:
        both = [unpack_mlp(x, d // SHARDS, d) for x in (sum_a, sum_b)]
    else:
        both = [jax.vmap(lambda p: unpack_mlp(p, d // SHARDS, d))(grad) for grad in (grad_a, grad_b)]

    def rejoin(pair, axis):
        lead = pair[0].shape[:axis]
        rest = pair[0].shape[axis + 1 :]
        parts = [p.reshape(lead + (SHARDS if axis else 1, -1) + rest) for p in pair]
        return jnp.stack(parts, axis=axis + 1).reshape(lead + (-1,) + rest)

    if size == SHARDS:
        raw = [rejoin([b[i] for b in both], axis) for i, axis in ((0, 1), (1, 1), (2, 0))]
    else:
        raw = []
        for i, axis in ((0, 1), (1, 1), (2, 0)):
            whole = jax.vmap(lambda a, b: rejoin([a, b], axis))(both[0][i], both[1][i])
            raw.append(reduce(whole.reshape(-1, whole.shape[-1])))
    g2 = jnp.sum(raw[0] * w_gate.astype(F32), axis=1) + jnp.sum(raw[1] * w_up.astype(F32), axis=1)
    dwg, dwu, dwd = raw[0] * gain2, raw[1] * gain2, raw[2]

    dwo, dws = joint[:, :d], [joint[:, d : d + 3 * GW], joint[:, d + 3 * GW :], dw2]
    raw = [jnp.concatenate([w[:, i * GW : (i + 1) * GW] for w in dws], axis=1) for i in range(3)]
    raw = [natural_order(raw[0]), natural_order(raw[1]), raw[2]]
    g1 = sum(jnp.sum(r * w.astype(F32), axis=1) for r, w in zip(raw, (w_query, w_key, w_value)))
    dwq, dwk, dwv = (r * gain1 for r in raw)
    return out, grad_tokens, g1, dwq, dwk, dwv, dwo, g2, dwg, dwu, dwd


def solution(mesh):
    in_specs = (
        P(("rep", "fsdp"), None),
        P(("rep", "fsdp"), None),
        P(("rep", "fsdp")),
        P(("rep", "fsdp"), None, None),
        P("fsdp"),
        P("fsdp", None),
        P("fsdp", None),
        P("fsdp", None),
        P("fsdp", None),
        P("fsdp"),
        P("fsdp", None),
        P("fsdp", None),
        P("fsdp", None),
    )
    out_specs = (
        P(("rep", "fsdp"), None),
        P(("rep", "fsdp"), None),
        P("fsdp"),
        P("fsdp", None),
        P("fsdp", None),
        P("fsdp", None),
        P("fsdp", None),
        P("fsdp"),
        P("fsdp", None),
        P("fsdp", None),
        P("fsdp", None),
    )
    sizes = dict(reps=mesh.shape["rep"], size=mesh.shape["fsdp"])
    return jax.shard_map(functools.partial(body, **sizes), mesh=mesh, in_specs=in_specs, out_specs=out_specs, check_vma=False)
```

```python
import functools
import jax
import jax.numpy as jnp
import numpy as np
from jax import lax
from jax.experimental import pallas as pl
from jax.experimental.pallas import tpu as pltpu
from jax.sharding import PartitionSpec as P

HEAD_DIM = 64
COLS = 24
GRID = 32
EPSILON = 1e-05
GROUP = 4
GW = GROUP * HEAD_DIM
HALF = GW // 2
BF = jnp.bfloat16
F32 = jnp.float32


def nn(a, b):
    return lax.dot_general(a, b, (((1,), (0,)), ((), ())), preferred_element_type=F32)


def nt(a, b):
    return lax.dot_general(a, b, (((1,), (1,)), ((), ())), preferred_element_type=F32)


def tn(a, b):
    return lax.dot_general(a, b, (((0,), (0,)), ((), ())), preferred_element_type=F32)


def params(limit=60):
    return pltpu.CompilerParams(vmem_limit_bytes=limit * 1024 * 1024)


def cost(flops, moved):
    return pl.CostEstimate(flops=int(flops), transcendentals=0, bytes_accessed=int(moved))


def inverse_rms(x):
    return lax.rsqrt(jnp.mean(x * x, axis=-1, keepdims=True) + EPSILON)


def angle_table():
    lane = np.arange(HALF)
    theta = (1.0 / 10000.0 ** (np.arange(HEAD_DIM // 4) * 4.0 / HEAD_DIM)).astype(np.float32)
    angle = np.arange(GRID, dtype=np.float32)[:, None] * theta[lane % (HEAD_DIM // 4)]
    by_row = (lane // (HEAD_DIM // 4)) % 2 == 0
    both = np.concatenate([np.cos(angle.astype(np.float64)), np.sin(angle.astype(np.float64))], axis=1)
    use = np.concatenate([by_row, by_row])
    left = np.concatenate([np.where(use, both, 0.0), np.where(use, 0.0, both)], axis=0).astype(np.float32)
    parts = []
    for _ in range(3):
        part = left.astype(jnp.bfloat16)
        parts.append(part)
        left = left - part.astype(np.float32)
    return np.concatenate(parts, axis=1)


def norm_kernel(x_ref, rope_ref, table_ref, out_ref, cos_ref, sin_ref):
    x = x_ref[...].astype(F32)
    out_ref[...] = (x * inverse_rms(x)).astype(BF)
    slot = x.shape[0]
    place = lax.broadcasted_iota(jnp.int32, (GRID, slot), 0)
    hot = jnp.concatenate([place == rope_ref[0, i : i + 1, :] for i in range(2)], axis=0)
    found = tn(jnp.where(hot, 1.0, 0.0).astype(BF), table_ref[...])
    found = found[:, :GW] + found[:, GW : 2 * GW] + found[:, 2 * GW :]
    cos_ref[...] = found[:, :HALF]
    sin_ref[...] = found[:, HALF:]


def norm_call(x, positions):
    n, d = x.shape
    crops, two, slot = positions.shape
    spec = lambda w: pl.BlockSpec((slot, w), lambda i: (i, 0))
    table = jnp.asarray(angle_table())
    return pl.pallas_call(
        norm_kernel,
        grid=(crops,),
        in_specs=[
            spec(d),
            pl.BlockSpec((1, two, slot), lambda i: (i, 0, 0)),
            pl.BlockSpec(table.shape, lambda i: (0, 0)),
        ],
        out_specs=[spec(d), spec(HALF), spec(HALF)],
        out_shape=[
            jax.ShapeDtypeStruct((n, d), BF),
            jax.ShapeDtypeStruct((n, HALF), F32),
            jax.ShapeDtypeStruct((n, HALF), F32),
        ],
        compiler_params=params(),
        cost_estimate=cost(0, 12 * n * d),
        name="norm_in",
    )(x, positions, table)


def head_masks():
    lane = lax.broadcasted_iota(jnp.int32, (1, GW), 1)
    rot = [((lane % HALF) // (HEAD_DIM // 2) == h) for h in range(GROUP)]
    nat = [(lane // HEAD_DIM == h) for h in range(GROUP)]
    return rot, nat


def mask_to(x, m):
    return x * jnp.where(m, 1.0, 0.0).astype(x.dtype)


def blocks_of(total, size):
    return [(s, min(s + size, total)) for s in range(0, total, size)]


def attn_fwd_kernel(slot, size, pair, ids_ref, nm_ref, cos_ref, sin_ref, own_hbm, oth_hbm,
                    qkv_ref, att_ref, lse_ref, w_out_ref, sem):
    group = pl.program_id(0)
    crop = pl.program_id(1)
    crops = pl.num_programs(1)
    zs = own_hbm.shape[1]
    rep, z, core = ids_ref[crops], ids_ref[crops + 1], ids_ref[crops + 2]

    @pl.when(crop == 0)
    def _():
        made = []
        for hbm, place in ((own_hbm, core), (oth_hbm, 1 - core)):
            for kind in range(4):
                for j in range(zs):
                    src = hbm.at[kind ^ rep, j, :, pl.ds(pl.multiple_of(group * GW, GW), GW)]
                    dst = w_out_ref.at[(z + j) & (zs - 1), place, :, pl.ds(kind * GW, GW)]
                    made.append(pltpu.make_async_copy(src, dst, sem.at[len(made)]))
        for copy in made:
            copy.start()
        for copy in made:
            copy.wait()

    nm = nm_ref[...]
    cos = cos_ref[...]
    sin = sin_ref[...]
    rot_m, nat_m = head_masks()
    d = nm.shape[1]

    def rotated(lo, scale):
        u = nn(nm, w_out_ref[:, :, :, lo : lo + GW].reshape(d, GW))
        a, b = u[:, :HALF], u[:, HALF:]
        r = jnp.concatenate([a * cos - b * sin, a * sin + b * cos], axis=1)
        return r.astype(BF) * jnp.asarray(scale, BF)

    q = rotated(0, HEAD_DIM ** (-0.5))
    k = rotated(GW, 1.0)
    v = nn(nm, w_out_ref[:, :, :, 2 * GW : 3 * GW].reshape(d, GW)).astype(BF)
    qkv_ref[:, :GW] = q
    qkv_ref[:, GW : 2 * GW] = k
    qkv_ref[:, 2 * GW :] = v
    qs = [mask_to(q, m) for m in rot_m]
    lane = lax.broadcasted_iota(jnp.int32, (1, 128), 1)
    units = [(s, e, h) for s, e in blocks_of(slot, size) for h in range(0, GROUP, pair)]

    def scores(s, e, h):
        stack = jnp.concatenate([qs[i][s:e] for i in range(h, h + pair)], axis=0)
        return nt(stack, k[s:e]), nt(stack, k[:s]) if s else None

    out = logs = None
    ready = scores(*units[0])
    for i, (s, e, h) in enumerate(units):
        later = scores(*units[i + 1]) if i + 1 < len(units) else None
        diag, left = ready
        w = e - s
        row = lax.broadcasted_iota(jnp.int32, (pair, w, w), 1).reshape(pair * w, w)
        col = lax.broadcasted_iota(jnp.int32, (pair, w, w), 2).reshape(pair * w, w)
        diag = jnp.where(row >= col, diag, -1e30)
        top = jnp.max(diag, axis=-1, keepdims=True)
        if s:
            top = jnp.maximum(top, jnp.max(left, axis=-1, keepdims=True))
        pd = jnp.exp(diag - top)
        total = jnp.sum(pd, axis=-1, keepdims=True)
        o = nn(pd.astype(BF), v[s:e])
        if s:
            pleft = jnp.exp(left - top)
            total = total + jnp.sum(pleft, axis=-1, keepdims=True)
            o = o + nn(pleft.astype(BF), v[:s])
        o = o * (1.0 / total)
        log = top + jnp.log(total)
        for g in range(pair):
            part = slice(g * w, (g + 1) * w)
            out = jnp.where(nat_m[h + g], o[part], out if h + g else 0.0)
            logs = jnp.where(lane == h + g, log[part], logs if h + g else 0.0)
        if h + pair == GROUP:
            att_ref[s:e, :] = out.astype(BF)
            lse_ref[0, 0, :, s:e] = logs.T[:8]
        ready = later


def attn_fwd(ids, nm, cos, sin, own, oth, slot, size=256, pair=4):
    n, d = nm.shape
    crops = n // slot
    kinds, zs, rows, width = own.shape
    groups = width // GW
    hbm = pl.BlockSpec(memory_space=pl.ANY)
    crop_spec = lambda w: pl.BlockSpec((slot, w), lambda g, c, *_: (c, 0))
    qkv, att, lse, w = pl.pallas_call(
        functools.partial(attn_fwd_kernel, slot, size, pair),
        grid_spec=pltpu.PrefetchScalarGridSpec(
            num_scalar_prefetch=1,
            grid=(groups, crops),
            in_specs=[crop_spec(d), crop_spec(HALF), crop_spec(HALF), hbm, hbm],
            out_specs=[
                pl.BlockSpec((slot, 3 * GW), lambda g, c, *_: (c, g)),
                pl.BlockSpec((slot, GW), lambda g, c, *_: (c, g)),
                pl.BlockSpec((1, 1, 8, slot), lambda g, c, *_: (g, c, 0, 0)),
                pl.BlockSpec((zs, 2, rows, 4 * GW), lambda g, c, *_: (0, 0, 0, g)),
            ],
            scratch_shapes=[pltpu.SemaphoreType.DMA((8 * zs,))],
        ),
        out_shape=[
            jax.ShapeDtypeStruct((n, groups * 3 * GW), BF),
            jax.ShapeDtypeStruct((n, groups * GW), BF),
            jax.ShapeDtypeStruct((groups, crops, 8, slot), F32),
            jax.ShapeDtypeStruct((zs, 2, rows, groups * 4 * GW), BF),
        ],
        compiler_params=params(),
        cost_estimate=cost(8e6 * groups * n, 2 * n * d),
        name="attn_fwd",
    )(ids, nm, cos, sin, own, oth)
    return qkv, att, lse, w.reshape(d, groups * 4 * GW)


def attn_bwd_kernel(slot, size, pair, qkv_ref, go_ref, att_ref, lse_ref, nm_ref, cos_ref, sin_ref, *refs):
    gqkv_ref, dw_ref, ds_ref, dq_ref, acc_ref = refs[-5:]
    crop = pl.program_id(1)
    q = qkv_ref[:, :GW]
    k = qkv_ref[:, GW : 2 * GW]
    v = qkv_ref[:, 2 * GW :]
    go = go_ref[...]
    rot_m, nat_m = head_masks()
    prod = go.astype(F32) * att_ref[...].astype(F32)
    hi = prod.astype(BF)
    lo = (prod - hi.astype(F32)).astype(BF)
    pick = (
        lax.broadcasted_iota(jnp.int32, (8, GW), 1) // HEAD_DIM
        == lax.broadcasted_iota(jnp.int32, (8, GW), 0)
    )
    pick = jnp.where(pick, 1.0, 0.0).astype(BF)
    delta = nt(pick, hi) + nt(pick, lo)
    blocks = blocks_of(slot, size)
    dk = [None] * len(blocks)
    dv = [None] * len(blocks)
    kms = [mask_to(k, m) for m in rot_m]
    vms = [mask_to(v, m) for m in nat_m]
    units = [(j, s, e, h) for j, (s, e) in enumerate(blocks) for h in range(0, GROUP, pair)]

    def stacked(parts, s, e, h):
        return jnp.concatenate([parts[i][s:e] for i in range(h, h + pair)], axis=0)

    def scores(j, s, e, h):
        return nt(stacked(kms, s, e, h), q[s:]), nt(stacked(vms, s, e, h), go[s:])

    ready = scores(*units[0])
    for i, (j, s, e, h) in enumerate(units):
        later = scores(*units[i + 1]) if i + 1 < len(units) else None
        w = e - s
        row = lax.broadcasted_iota(jnp.int32, (w, w), 0)
        col = lax.broadcasted_iota(jnp.int32, (w, w), 1)
        ps, dss = [], []
        for g in range(pair):
            sc, dp = (x[g * w : (g + 1) * w] for x in ready)
            p = jnp.exp(sc - lse_ref[0, 0, h + g : h + g + 1, s:])
            first = jnp.where(col >= row, p[:, :w], 0.0)
            p = jnp.concatenate([first, p[:, w:]], axis=1) if e < slot else first
            ds = (p * (dp - delta[h + g : h + g + 1, s:])).astype(BF)
            ds_ref[h + g, s:, s:e] = ds.T
            ps.append(p.astype(BF))
            dss.append(ds)
        dvp = nn(jnp.concatenate(ps, axis=0), go[s:])
        dkp = nn(jnp.concatenate(dss, axis=0), q[s:])
        for g in range(pair):
            part = slice(g * w, (g + 1) * w)
            dv[j] = jnp.where(nat_m[h + g], dvp[part], dv[j] if h + g else 0.0)
            dk[j] = jnp.where(rot_m[h + g], dkp[part], dk[j] if h + g else 0.0)
        ready = later
    for s, e in blocks:
        w = e - s
        parts = nn(ds_ref[:, s:e, :e].reshape(GROUP * w, e), k[:e])
        dq = 0.0
        for h in range(GROUP):
            dq = jnp.where(rot_m[h], parts[h * w : (h + 1) * w], dq)
        dq_ref[s:e] = dq
    cos = cos_ref[...]
    sin = sin_ref[...]

    def back(u, c, t):
        a, b = u[:, :HALF], u[:, HALF:]
        return jnp.concatenate([a * c + b * t, b * c - a * t], axis=1).astype(BF)

    for j, (s, e) in enumerate(blocks):
        c, t = cos[s:e], sin[s:e]
        gqkv_ref[s:e, :GW] = back(dq_ref[s:e] * (HEAD_DIM ** (-0.5)), c, t)
        gqkv_ref[s:e, GW : 2 * GW] = back(dk[j], c, t)
        gqkv_ref[s:e, 2 * GW :] = dv[j].astype(BF)
    part = tn(nm_ref[...], gqkv_ref[...])

    @pl.when(crop == 0)
    def _():
        acc_ref[...] = part

    @pl.when(crop != 0)
    def _():
        acc_ref[...] += part

    @pl.when(crop == pl.num_programs(1) - 1)
    def _():
        dw_ref[...] = acc_ref[...].astype(BF)


def attn_bwd(qkv, go, att, lse, nm, cos, sin, slot, place, first, joint=None, size=128, pair=4):
    n, d = nm.shape
    crops = n // slot
    more = [] if joint is None else [joint]
    column = 0 if joint is None else first + place + 1
    row_spec = lambda w, at: pl.BlockSpec((slot, w), lambda g, c: (c, at))
    crop_spec = lambda w: pl.BlockSpec((slot, w), lambda g, c: (c, 0))
    return pl.pallas_call(
        functools.partial(attn_bwd_kernel, slot, size, pair),
        grid=(1, crops),
        in_specs=[
            row_spec(3 * GW, place),
            row_spec(GW, first + place),
            row_spec(GW, place),
            pl.BlockSpec((1, 1, 8, slot), lambda g, c: (place, c, 0, 0)),
            crop_spec(d),
            crop_spec(HALF),
            crop_spec(HALF),
        ]
        + [pl.BlockSpec(memory_space=pl.ANY)] * len(more),
        out_specs=[crop_spec(3 * GW), pl.BlockSpec((d, 3 * GW), lambda g, c: (0, column))],
        out_shape=[
            jax.ShapeDtypeStruct((n, 3 * GW), BF),
            jax.ShapeDtypeStruct((d, 3 * GW) if joint is None else joint.shape, BF),
        ],
        input_output_aliases={7: 1} if more else {},
        scratch_shapes=[
            pltpu.VMEM((GROUP, slot, slot), BF),
            pltpu.VMEM((slot, GW), F32),
            pltpu.VMEM((d, 3 * GW), F32),
        ],
        compiler_params=params(),
        cost_estimate=cost(12e6 * n, 2 * n * d),
        name="attn_bwd",
    )(qkv, go, att, lse, nm, cos, sin, *more)


def valid_rows(ids_ref, tile, rows, slot):
    row = tile * rows + lax.broadcasted_iota(jnp.int32, (rows, 1), 0)
    crop = row // slot
    first = tile * rows // slot
    limit = jnp.zeros((rows, 1), jnp.int32)
    for i in range(-(-rows // slot) + 1):
        index = first + i
        limit = jnp.where(crop == index, ids_ref[index] * COLS, limit)
    return row - crop * slot < limit


def out_weights(weights, d):
    arrays, specs = [], []
    for w in weights:
        for g in range(w.shape[1] // (4 * GW)):
            arrays.append(w)
            specs.append(pl.BlockSpec((d, GW), lambda c, *_, g=g: (0, 4 * g + 3)))
    return arrays, specs


def out_proj_kernel(slot, n_att, ids_ref, x_ref, *refs):
    att_refs, refs = refs[:n_att], refs[n_att:]
    *wo_refs, mid_ref, nm_ref = refs
    valid = valid_rows(ids_ref, pl.program_id(0), x_ref.shape[0], slot)
    att = jnp.concatenate([a[...] for a in att_refs], axis=1)
    proj = jnp.concatenate([nn(att, w[...]) for w in wo_refs], axis=1)
    mid = x_ref[...].astype(F32) + jnp.where(valid, proj, 0.0)
    mid_ref[...] = mid.astype(BF)
    nm_ref[...] = (mid * inverse_rms(mid)).astype(BF)


def out_proj(ids, x, atts, weights, slot, tile):
    n, d = x.shape
    rows = lambda w: pl.BlockSpec((tile, w), lambda c, *_: (c, 0))
    wos, wo_specs = out_weights(weights, d)
    return pl.pallas_call(
        functools.partial(out_proj_kernel, slot, len(atts)),
        grid_spec=pltpu.PrefetchScalarGridSpec(
            num_scalar_prefetch=1,
            grid=(n // tile,),
            in_specs=[rows(d)] + [rows(a.shape[1]) for a in atts] + wo_specs,
            out_specs=[rows(d), rows(d)],
        ),
        out_shape=[jax.ShapeDtypeStruct((n, d), BF), jax.ShapeDtypeStruct((n, d), BF)],
        compiler_params=params(),
        cost_estimate=cost(2 * n * d * d, 10 * n * d),
        name="out_proj",
    )(ids, x, *atts, *wos)


PACK = 512
TILE = 768
SHARDS = 8


def halves(w, axis):
    shape = w.shape[:axis] + (-1, 2, w.shape[axis] // (2 * SHARDS) if axis else w.shape[0] // 2) + w.shape[axis + 1 :]
    w = w.reshape(shape)
    return [
        lax.index_in_dim(w, i, axis + 1, keepdims=False).reshape(w.shape[:axis] + (-1,) + w.shape[axis + 3 :])
        for i in range(2)
    ]


def pack_mlp(gate, up, down):
    wide = [w[:, i : i + PACK] for w in (gate, up) for i in range(0, w.shape[1], PACK)]
    half = down.shape[0] // 2
    tail = down[:, PACK:]
    fold = jnp.concatenate([tail[:half], tail[half:]], axis=1)
    return jnp.concatenate(wide + [down[:, :PACK], fold], axis=0)


def unpack_mlp(pack, rows, d):
    chunks = 2
    gate, up = (
        jnp.concatenate([pack[i * rows : (i + 1) * rows] for i in range(s, s + chunks)], axis=1)
        for s in (0, chunks)
    )
    base = 2 * chunks * rows
    deep = (pack.shape[0] - base) * PACK // d
    fold = pack[base + deep :]
    tail = jnp.concatenate([fold[:, : d - PACK], fold[:, d - PACK :]], axis=0)
    return gate, up, jnp.concatenate([pack[base : base + deep], tail], axis=1)


def mlp_kernel(slot, final, step, ids_ref, nm_ref, cot_ref, part_ref, *refs):
    if final:
        before_ref, *refs = refs
    (pack_hbm, out_ref, dn_ref, grad_hbm, wg_buf, wu_buf, wd_buf, hid_ref, gg_ref, gu_ref,
     ag_ref, au_ref, ad_ref, sg_ref, su_ref, sd_ref, in_sem, out_sem) = refs
    tile = pl.program_id(0)
    d = nm_ref.shape[1]
    chunks, shards, rows, _ = sg_ref.shape
    units = chunks * PACK
    some = shards // chunks
    deep = sd_ref.shape[1]
    base = 2 * chunks * rows
    side = d - PACK

    def pieces(hbm, wg, wu, wd):
        for i in range(chunks):
            yield hbm.at[:, pl.ds(i * rows, rows), :], wg.at[i]
            yield hbm.at[:, pl.ds((chunks + i) * rows, rows), :], wu.at[i]
        yield hbm.at[:, pl.ds(base, deep), :], wd.at[:, :, pl.ds(0, PACK)]
        for i in range(2):
            yield (
                hbm.at[:, pl.ds(base + deep, deep // 2), pl.ds(i * side, side)],
                wd.at[:, pl.ds(i * (deep // 2), deep // 2), pl.ds(PACK, side)],
            )

    @pl.when(tile == 0)
    def _():
        made = pieces(pack_hbm, wg_buf, wu_buf, wd_buf)
        made = [pltpu.make_async_copy(a, b, in_sem.at[i]) for i, (a, b) in enumerate(made)]
        for copy in made:
            copy.start()
        ag_ref[...] = jnp.zeros_like(ag_ref)
        au_ref[...] = jnp.zeros_like(au_ref)
        ad_ref[...] = jnp.zeros_like(ad_ref)
        for copy in made:
            copy.wait()

    valid = valid_rows(ids_ref, tile, nm_ref.shape[0], slot)
    nm = nm_ref[...]
    gb = jnp.where(valid, cot_ref[...], jnp.zeros((), BF))
    wd = wd_buf[...].reshape(units, d)

    def wide(buf, i):
        at = i * step
        return buf[at // PACK, :, :, at % PACK : at % PACK + step].reshape(d, step)

    def first(i):
        return (
            nn(nm, wide(wg_buf, i)),
            nn(nm, wide(wu_buf, i)),
            nt(gb, wd[i * step : (i + 1) * step]),
        )

    def second(i, g, u, gh):
        cols = slice(i * step, (i + 1) * step)
        sg = 0.5 * jnp.tanh(0.5 * g) + 0.5
        act = g * sg
        hid_ref[:, cols] = (act * u).astype(BF)
        gu_ref[:, cols] = (gh * act).astype(BF)
        gg_ref[:, cols] = (gh * u * (sg + act * (1.0 - sg))).astype(BF)

    ready = first(0)
    for i in range(1, units // step):
        later = first(i)
        second(i - 1, *ready)
        ready = later
    second(units // step - 1, *ready)
    nmt = nm.T
    gbt = gb.T
    o = part_ref[...] + jnp.where(valid, nn(hid_ref[...], wd), 0.0)
    out_ref[...] = o.astype(out_ref.dtype)
    dn = before_ref[...] if final else 0.0
    for i in range(chunks):
        cols = slice(i * PACK, (i + 1) * PACK)
        dn = dn + nt(gg_ref[:, cols], wg_buf[i].reshape(d, PACK)) + nt(gu_ref[:, cols], wu_buf[i].reshape(d, PACK))
    dn_ref[...] = dn.astype(dn_ref.dtype)
    for i in range(chunks):
        cols = slice(i * PACK, (i + 1) * PACK)
        ag_ref[i] += nn(nmt, gg_ref[:, cols])
        au_ref[i] += nn(nmt, gu_ref[:, cols])
        ad_ref[i] += nn(gbt, hid_ref[:, cols])

    @pl.when(tile == pl.num_programs(0) - 1)
    def _():
        sg_ref[...] = ag_ref[...].astype(BF).reshape(sg_ref.shape)
        su_ref[...] = au_ref[...].astype(BF).reshape(su_ref.shape)
        for i in range(chunks):
            sd_ref[i * some : (i + 1) * some] = ad_ref[i].astype(BF).T.reshape(some, deep, d)
        made = pieces(grad_hbm, sg_ref, su_ref, sd_ref)
        made = [pltpu.make_async_copy(b, a, out_sem.at[i]) for i, (a, b) in enumerate(made)]
        for copy in made:
            copy.start()
        for copy in made:
            copy.wait()


def mlp(ids, nm, cot, part, before, pack, slot, tile, step=256):
    n, d = nm.shape
    rows = d // SHARDS
    chunks = 2
    deep = chunks * PACK // SHARDS
    final = before is not None
    spec = pl.BlockSpec((tile, d), lambda i, *_: (i, 0))
    hbm = pl.BlockSpec(memory_space=pl.ANY)
    packed = pltpu.VMEM((chunks, SHARDS, rows, PACK), BF)
    units = pltpu.VMEM((tile, chunks * PACK), BF)
    sums = pltpu.VMEM((chunks, d, PACK), F32)
    return pl.pallas_call(
        functools.partial(mlp_kernel, slot, final, step),
        grid_spec=pltpu.PrefetchScalarGridSpec(
            num_scalar_prefetch=1,
            grid=(n // tile,),
            in_specs=[spec] * (3 + final) + [hbm],
            out_specs=[spec, spec, hbm],
            scratch_shapes=[packed, packed, pltpu.VMEM((SHARDS, deep, d), BF)]
            + [units] * 3
            + [sums] * 3
            + [packed, packed, pltpu.VMEM((SHARDS, deep, d), BF)]
            + [pltpu.SemaphoreType.DMA((2 * chunks + 3,))] * 2,
        ),
        out_shape=[
            jax.ShapeDtypeStruct((n, d), BF if final else F32),
            jax.ShapeDtypeStruct((n, d), BF if final else F32),
            jax.ShapeDtypeStruct(pack.shape, BF),
        ],
        compiler_params=params(),
        cost_estimate=cost(24e6 * n, 20 * n * d),
        name="mlp",
    )(ids, nm, cot, part, *([before] if final else []), pack)


def norm_back(scaled, field):
    inv = inverse_rms(field)
    return inv * scaled - field * (inv * inv * inv * jnp.mean(scaled * field, axis=-1, keepdims=True))


def mid_grad_kernel(slot, n_att, ids_ref, cot_ref, mid_ref, dn_ref, *refs):
    att_refs, refs = refs[:n_att], refs[n_att:]
    *wo_refs, gmid_ref, gatt_ref, dwo_ref, acc_ref = refs
    c = pl.program_id(0)
    valid = valid_rows(ids_ref, c, cot_ref.shape[0], slot)
    gm = cot_ref[...].astype(F32) + norm_back(dn_ref[...].astype(F32), mid_ref[...].astype(F32))
    gmid_ref[...] = gm.astype(BF)
    ga = jnp.where(valid, gm, 0.0).astype(BF)
    gatt = sum(nt(ga[:, i * GW : (i + 1) * GW], w[...]) for i, w in enumerate(wo_refs))
    gatt_ref[...] = gatt.astype(BF)
    part = tn(jnp.concatenate([a[...] for a in att_refs], axis=1), ga)

    @pl.when(c == 0)
    def _():
        acc_ref[...] = part

    @pl.when(c != 0)
    def _():
        acc_ref[...] += part

    @pl.when(c == pl.num_programs(0) - 1)
    def _():
        dwo_ref[...] = acc_ref[...].astype(BF)


def mid_grad(ids, cot, mid, dn, atts, weights, slot, tile):
    n, d = cot.shape
    rows = lambda w: pl.BlockSpec((tile, w), lambda c, *_: (c, 0))
    wos, wo_specs = out_weights(weights, d)
    return pl.pallas_call(
        functools.partial(mid_grad_kernel, slot, len(atts)),
        grid_spec=pltpu.PrefetchScalarGridSpec(
            num_scalar_prefetch=1,
            grid=(n // tile,),
            in_specs=[rows(d)] * 3 + [rows(a.shape[1]) for a in atts] + wo_specs,
            out_specs=[rows(d), rows(d), pl.BlockSpec((d, d), lambda c, *_: (0, 0))],
            scratch_shapes=[pltpu.VMEM((d, d), F32)],
        ),
        out_shape=[
            jax.ShapeDtypeStruct((n, d), BF),
            jax.ShapeDtypeStruct((n, d), BF),
            jax.ShapeDtypeStruct((d, 3 * d), BF),
        ],
        compiler_params=params(),
        cost_estimate=cost(4 * n * d * d, 18 * n * d),
        name="mid_grad",
    )(ids, cot, mid, dn, *atts, *wos)


def input_grad_kernel(n_group, *refs):
    g_refs, w_refs = refs[:n_group], refs[n_group : 4 * n_group]
    x_ref, gmid_ref = refs[4 * n_group : 4 * n_group + 2]
    out_ref = refs[-1]
    e = 0.0
    for i, g in enumerate(g_refs):
        w = jnp.concatenate([w[...] for w in w_refs[3 * i : 3 * i + 3]], axis=1)
        e = e + nt(g[...], w)
    out_ref[...] = gmid_ref[...].astype(F32) + norm_back(e, x_ref[...].astype(F32))


def input_grad(gqkvs, weights, x, gmid, rows, start, stop, filled=None):
    n, d = x.shape
    arrays = [(w, 4 * g + i) for w in weights for g in range(w.shape[1] // (4 * GW)) for i in range(3)]
    spec = lambda w: pl.BlockSpec((rows, w), lambda i: (start + i, 0))
    more = [] if filled is None else [filled]
    n_in = 4 * len(gqkvs) + 2
    count = (stop - start) * rows
    return pl.pallas_call(
        functools.partial(input_grad_kernel, len(gqkvs)),
        grid=(stop - start,),
        in_specs=[spec(3 * GW)] * len(gqkvs)
        + [pl.BlockSpec((d, GW), lambda i, g=g: (0, g)) for _, g in arrays]
        + [spec(d), spec(d)]
        + [pl.BlockSpec(memory_space=pl.ANY)] * len(more),
        out_specs=spec(d),
        out_shape=jax.ShapeDtypeStruct((n, d), F32),
        input_output_aliases={n_in: 0} if more else {},
        compiler_params=params(),
        cost_estimate=cost(6 * count * d * d, 16 * count * d),
        name="input_grad",
    )(*gqkvs, *[w for w, _ in arrays], x, gmid, *more)


def column_of(row_ref):
    row = row_ref[...].astype(F32)
    return jnp.broadcast_to(row, (128, row.shape[1])).T[:, :1]


def lane_order(to_natural):
    lane = lax.broadcasted_iota(jnp.int32, (GW, GW), 1)
    half = HEAD_DIM // 2
    if to_natural:
        source = lane // HEAD_DIM * half + lane % half + jnp.where(lane % HEAD_DIM < half, 0, HALF)
    else:
        source = lane % HALF // half * HEAD_DIM + lane // HALF * half + lane % half
    return jnp.where(lax.broadcasted_iota(jnp.int32, (GW, GW), 0) == source, 1.0, 0.0).astype(BF)


def join_kernel(place_ref, wq_ref, wk_ref, wv_ref, wo_ref, gain_ref, out_ref):
    for kind, w_ref in enumerate((wq_ref, wk_ref, wv_ref, wo_ref)):

        @pl.when(place_ref[0] == kind)
        def _(kind=kind, w_ref=w_ref):
            w = w_ref[...]
            if kind < 3:
                w = (w.astype(F32) * column_of(gain_ref)).astype(BF)
            if kind < 2:
                order = lane_order(False)
                for at in range(0, w.shape[1], GW):
                    out_ref[:, at : at + GW] = nn(w[:, at : at + GW], order).astype(BF)
            else:
                out_ref[...] = w


def join_call(place, wq, wk, wv, wo, gain):
    vmem = pl.BlockSpec(memory_space=pltpu.VMEM)
    return pl.pallas_call(
        join_kernel,
        grid_spec=pltpu.PrefetchScalarGridSpec(
            num_scalar_prefetch=1, grid=(1,), in_specs=[vmem] * 5, out_specs=vmem
        ),
        out_shape=jax.ShapeDtypeStruct(wq.shape, BF),
        compiler_params=params(),
        cost_estimate=cost(0, 1e6),
        name="join",
    )(place, wq, wk, wv, wo, gain)


def pack_kernel(wg_ref, wu_ref, wd_ref, gain_ref, a_ref, b_ref):
    rows, ff = wg_ref.shape
    units = ff // (2 * SHARDS)
    deep = wd_ref.shape[0] // 2
    side = wd_ref.shape[1] - PACK
    chunks = ff // (2 * PACK)
    base = 2 * chunks * rows
    gain = column_of(gain_ref)
    for half, out_ref in enumerate((a_ref, b_ref)):
        for w_ref, first in ((wg_ref, 0), (wu_ref, chunks)):
            for i in range(chunks):
                at = (first + i) * rows
                for j in range(PACK // units):
                    source = (i * (PACK // units) + j) * 2 * units + half * units
                    part = w_ref[:, source : source + units].astype(F32) * gain
                    out_ref[at : at + rows, j * units : (j + 1) * units] = part.astype(BF)
        at = half * deep
        out_ref[base : base + deep] = wd_ref[at : at + deep, :PACK]
        for i in range(2):
            source = at + i * (deep // 2)
            out_ref[base + deep :, i * side : (i + 1) * side] = wd_ref[source : source + deep // 2, PACK:]


def pack_call(wg, wu, wd, gain):
    size = (wg.size + wu.size + wd.size) // (2 * PACK)
    return pl.pallas_call(
        pack_kernel,
        out_shape=[jax.ShapeDtypeStruct((size, PACK), BF)] * 2,
        compiler_params=params(),
        cost_estimate=cost(0, 4e6),
        name="pack",
    )(wg, wu, wd, gain)


def row_of(column):
    return jnp.broadcast_to(column, (column.shape[0], 128)).T[:1]


def mlp_end_kernel(a0_ref, a1_ref, b0_ref, b1_ref, wg_ref, wu_ref, gain_ref, dwg_ref, dwu_ref, dwd_ref, g_ref):
    rows = wg_ref.shape[0]
    units = wg_ref.shape[1] // (2 * SHARDS)
    deep = dwd_ref.shape[0] // 2
    side = dwd_ref.shape[1] - PACK
    chunks = wg_ref.shape[1] // (2 * PACK)
    base = 2 * chunks * rows
    gain = column_of(gain_ref)
    dot = jnp.zeros((rows, units), F32)
    for half, (left, right) in enumerate(((a0_ref, a1_ref), (b0_ref, b1_ref))):
        for w_ref, out_ref, first in ((wg_ref, dwg_ref, 0), (wu_ref, dwu_ref, chunks)):
            for i in range(chunks):
                at = (first + i) * rows
                block = left[at : at + rows].astype(F32) + right[at : at + rows].astype(F32)
                for j in range(PACK // units):
                    to = (i * (PACK // units) + j) * 2 * units + half * units
                    part = block[:, j * units : (j + 1) * units]
                    dot = dot + part * w_ref[:, to : to + units].astype(F32)
                    out_ref[:, to : to + units] = part * gain
        down = left[base:].astype(F32) + right[base:].astype(F32)
        at = half * deep
        dwd_ref[at : at + deep, :PACK] = down[:deep]
        for i in range(2):
            to = at + i * (deep // 2)
            dwd_ref[to : to + deep // 2, PACK:] = down[deep:, i * side : (i + 1) * side]
    g_ref[...] = row_of(jnp.sum(dot, axis=1, keepdims=True))


def mlp_end(a0, a1, b0, b1, wg, wu, gain, down_shape):
    rows = wg.shape[0]
    return pl.pallas_call(
        mlp_end_kernel,
        out_shape=[
            jax.ShapeDtypeStruct(wg.shape, F32),
            jax.ShapeDtypeStruct(wu.shape, F32),
            jax.ShapeDtypeStruct(down_shape, F32),
            jax.ShapeDtypeStruct((1, rows), F32),
        ],
        compiler_params=params(),
        cost_estimate=cost(0, 6e6),
        name="mlp_end",
    )(a0, a1, b0, b1, wg, wu, gain)


def attn_end_kernel(place_ref, l0_ref, l1_ref, r0_ref, r1_ref, last_ref, wq_ref, wk_ref, wv_ref, gain_ref,
                    dwq_ref, dwk_ref, dwv_ref, dwo_ref, g_ref, last_buf):
    rows, d = wq_ref.shape
    reps, few, _ = last_ref.shape
    gain = column_of(gain_ref)
    for r in range(reps):
        last_buf[r * few : (r + 1) * few] = last_ref[r ^ place_ref[0]].astype(F32)

    def summed(lo, hi):
        pairs = ((l0_ref, r0_ref), (l1_ref, r1_ref))
        return jnp.concatenate([l[:, lo:hi].astype(F32) + r[:, lo:hi].astype(F32) for l, r in pairs], axis=0)

    dwo_ref[...] = summed(0, d)
    order = lane_order(True)
    groups = d // GW
    dot = jnp.zeros((rows, GW), F32)
    for g in range(groups):
        for kind, (w_ref, out_ref) in enumerate(((wq_ref, dwq_ref), (wk_ref, dwk_ref), (wv_ref, dwv_ref))):
            at = d + (3 * g + kind) * GW
            if g == groups - 1:
                block = last_buf[:, kind * GW : (kind + 1) * GW]
            else:
                block = summed(at, at + GW)
            if kind < 2:
                moved = 0.0
                for _ in range(3):
                    part = block.astype(BF)
                    moved = moved + nn(part, order)
                    block = block - part.astype(F32)
                block = moved
            cols = slice(g * GW, (g + 1) * GW)
            dot = dot + block * w_ref[:, cols].astype(F32)
            out_ref[:, cols] = block * gain
    g_ref[...] = row_of(jnp.sum(dot, axis=1, keepdims=True))


def attn_end(place, lefts, rights, last, wq, wk, wv, gain):
    rows, d = wq.shape
    vmem = pl.BlockSpec(memory_space=pltpu.VMEM)
    return pl.pallas_call(
        attn_end_kernel,
        grid_spec=pltpu.PrefetchScalarGridSpec(
            num_scalar_prefetch=1,
            grid=(1,),
            in_specs=[vmem] * 9,
            out_specs=[vmem] * 5,
            scratch_shapes=[pltpu.VMEM((rows, 3 * GW), F32)],
        ),
        out_shape=[jax.ShapeDtypeStruct((rows, d), F32)] * 4 + [jax.ShapeDtypeStruct((1, rows), F32)],
        compiler_params=params(),
        cost_estimate=cost(0, 6e6),
        name="attn_end",
    )(place, *lefts, *rights, last, wq, wk, wv, gain)


def rot_order(w):
    rows, cols = w.shape
    w = w.reshape(rows, cols // GW, GROUP, 2, HEAD_DIM // 2)
    return w.transpose(0, 1, 3, 2, 4).reshape(rows, cols)


def natural_order(w):
    rows, cols = w.shape
    w = w.reshape(rows, cols // GW, 2, GROUP, HEAD_DIM // 2)
    return w.transpose(0, 1, 3, 2, 4).reshape(rows, cols)


def join_attn(wq, wk, wv, wo, gain):
    scaled = [(w.astype(F32) * gain).astype(BF) for w in (rot_order(wq), rot_order(wk), wv)]
    return jnp.stack(scaled + [wo])


def swap(x, axis, bit, size):
    return lax.ppermute(x, axis, [(i, i ^ bit) for i in range(size)])


def shift(x, step, size):
    half = size // 2
    return lax.ppermute(x, "fsdp", [(((i // 2 + step) % half) * 2 + i % 2, i) for i in range(size)])


def pick(x, index, axis=0):
    return lax.dynamic_index_in_dim(x, index, axis, keepdims=False)


def total(*parts):
    return sum(p.astype(F32) for p in parts).astype(BF)


def along_z(mine, size):
    return jnp.stack([mine] + [shift(mine, k, size) for k in range(1, size // 2)])


def over_reps(x, reps):
    return jnp.stack([x] + [swap(x, "rep", bit, reps) for bit in range(1, reps)])


def sum_reps(x, reps):
    if reps != 4:
        return lax.psum(x, "rep").astype(F32)
    x = (x.astype(F32) + swap(x, "rep", 1, reps).astype(F32)).astype(BF)
    return x.astype(F32) + swap(x, "rep", 2, reps).astype(F32)


def body(tokens, cotangent, crop_heights, rope_positions, gain_attn, w_query, w_key, w_value, w_out,
         gain_mlp, w_gate, w_up, w_down, *, reps, size):
    crops = crop_heights.shape[0]
    n, d = tokens.shape
    slot = n // crops
    tile = TILE if n % TILE == 0 else slot
    gain1 = gain_attn.astype(F32)[:, None]
    gain2 = gain_mlp.astype(F32)[:, None]

    def gather(w):
        return lax.all_gather(w, "fsdp", axis=0, tiled=True)

    def scatter(g):
        return lax.psum_scatter(g, "fsdp", scatter_dimension=0, tiled=True)

    def reduce(g):
        return sum_reps(scatter(g), reps)

    pin = lax.optimization_barrier
    links = reps == 4 and size == SHARDS
    rep, f = lax.axis_index("rep"), lax.axis_index("fsdp")
    if links:
        place = jnp.stack([rep, f // 2, f % 2]).astype(jnp.int32)
        row1, row2 = gain_attn[None], gain_mlp[None]
        mine = join_call(place, w_query, w_key, w_value, w_out, row1)
        mine, w_gate, w_up, w_down, tokens_1 = pin((mine, w_gate, w_up, w_down, tokens))
        lines = [along_z(m, size) for m in (mine[:, :GW], mine[:, GW:])]
        sides = [swap(lines[0], "rep", bit, reps) for bit in range(1, reps)]
    else:
        place = jnp.zeros((3,), jnp.int32)
        joined = join_attn(w_query, w_key, w_value, w_out, gain1)
        every = lax.all_gather(joined, "fsdp", axis=1, tiled=True)
        every = every.reshape(4, SHARDS // 2, 2, d // SHARDS, d)
    ids = jnp.concatenate([crop_heights, place])
    if not links:
        tokens_1 = tokens
    nm1, cos, sin = norm_call(tokens_1, rope_positions)
    if links:
        *sides, lines[1], nm1, cos, sin = pin((*sides, lines[1], nm1, cos, sin))
        own = jnp.stack([lines[0]] + sides)
        own, w_gate, w_up, w_down = pin((own, w_gate, w_up, w_down))
        oth = swap(own, "fsdp", 1, size)
        sides = [swap(lines[1], "rep", bit, reps) for bit in range(1, reps)]
        packs = [
            lax.all_gather(p, "fsdp", axis=0, tiled=False) for p in pack_call(w_gate, w_up, w_down, row2)
        ]
    else:
        scaled = [(w.astype(F32) * gain2).astype(BF) for w in (w_gate, w_up)]
        wide = [gather(w).reshape(SHARDS, -1, w.shape[1]) for w in scaled]
        down = gather(w_down).reshape(SHARDS, -1, d)
        split = zip(*[[jnp.stack(h) for h in zip(*[halves(w, a) for w in ws])] for ws, a in
                      ((wide[0], 1), (wide[1], 1), (down, 0))])
        packs = [jax.vmap(pack_mlp)(*part) for part in split]

    attended, weights = [], []
    for i, cols in enumerate((slice(0, GW), slice(GW, d))):
        if not links:
            own, oth = every[:, :, 0, :, cols], every[:, :, 1, :, cols]
        elif i:
            *parts, _ = pin((lines[1], *sides, atts))
            own = jnp.stack(parts)
            oth = swap(own, "fsdp", 1, size)
        *some, w = attn_fwd(ids, nm1, cos, sin, own, oth, slot)
        attended.append(some)
        weights.append(w)
        atts = [a for _, a, _ in attended]
    mid, nm2 = out_proj(ids, tokens, atts, weights, slot, tile)
    part, dn, grad_a = mlp(ids, nm2, cotangent, mid, None, packs[0], slot, tile)
    out, dn, grad_b = mlp(ids, nm2, cotangent, part, dn, packs[1], slot, tile)
    local_a = scatter(grad_a.reshape(-1, PACK)) if links else grad_a
    local_b = scatter(grad_b.reshape(-1, PACK)) if links else grad_b
    gmid, gatt, joint = mid_grad(ids, cotangent, mid, dn, atts, weights, slot, tile)

    def backward(index, gatt, joint=None):
        w = 0 if index == 0 else 1
        qkv, att, lse = attended[w]
        return attn_bwd(qkv, gatt, att, lse, nm1, cos, sin, slot, index - w, w, joint)

    fast = False
    if links:
        local_a, gatt = pin((local_a, gatt))
        local_a = total(local_a, swap(local_a, "rep", 1, reps))
    gqkv0, joint = backward(0, gatt, joint)
    if links:
        local_a, gatt, gqkv0 = pin((local_a, gatt, gqkv0))
        other_a = swap(local_a, "rep", 2, reps)
    gqkv1, joint = backward(1, gatt, joint)
    if links:
        other_a, local_b, joint, gatt, gqkv1 = pin((other_a, local_b, joint, gatt, gqkv1))
        local_b = total(local_b, swap(local_b, "rep", 1, reps))
    joint = scatter(joint)
    gqkv2, dw2 = backward(2, gatt)
    gqkvs = [gqkv0, gqkv1, gqkv2]
    grad = lambda gmid: input_grad(gqkvs, weights, tokens, gmid, tile // 2, 0, 2 * n // tile)
    if links:
        y, x, z, core = rep // 2, rep % 2, f // 2, f % 2
        zs, rows = size // 2, d // size
        cut = dw2.reshape(zs, 2, 2, 2, rows // reps, 3 * GW)
        keep, send = pick(cut, core, 1), pick(cut, 1 - core, 1)
        got = swap(send, "fsdp", 1, size)
        keep, local_b, gqkvs[2] = pin((keep, local_b, gqkvs[2]))
        other_b = swap(local_b, "rep", 2, reps)
        side = swap(total(pick(keep, 1 - x, 2), pick(got, 1 - x, 2)), "rep", 1, reps)
        keep = total(pick(keep, x, 2), pick(got, x, 2))
        keep, gmid = pin((keep, gmid))
        grad_tokens = grad(gmid)
        grad_tokens, keep, side, joint, local_a, other_a = pin((grad_tokens, keep, side, joint, local_a, other_a))
        got = swap(total(pick(keep, 1 - y, 1), pick(side, 1 - y, 1)), "rep", 2, reps)
        cuts = joint[: rows // 2], joint[rows // 2 :]
        others = [swap(part, "rep", 1 + i, reps) for i, part in enumerate(cuts)]
        keep, side = pick(keep, y, 1), pick(side, y, 1)
        *dmlp, g2 = mlp_end(local_a, other_a, local_b, other_b, w_gate, w_up, row2, w_down.shape)
        dmlp[0], keep, side, got = pin((dmlp[0], keep, side, got))

        def at(k):
            i = (z + k) % zs
            return total(pick(keep, i), pick(side, i), pick(got, i))

        sends = [at(zs - k) for k in range(1, zs)]
        first, *others = pin((at(0), *others))
        cuts = [total(a, b) for a, b in zip(cuts, others)]
        others = [swap(part, "rep", 2 - i, reps) for i, part in enumerate(cuts)]
        part = total(first, *[shift(s, k + 1, size) for k, s in enumerate(sends)])
        every = over_reps(part, reps)
        *dattn, g1 = attn_end(place, cuts, others, every, w_query, w_key, w_value, row1)
        return (out, grad_tokens, g1.reshape(-1), *dattn, g2.reshape(-1), *dmlp)

    grad_tokens = grad(gmid)
    dw2 = reduce(dw2)
    joint = sum_reps(joint, reps)
    if fast:
        sum_a, sum_b = sum_reps(local_a, reps), sum_reps(local_b, reps)
    both = []
    if fast:
        both = [unpack_mlp(x, d // SHARDS, d) for x in (sum_a, sum_b)]
    else:
        both = [jax.vmap(lambda p: unpack_mlp(p, d // SHARDS, d))(grad) for grad in (grad_a, grad_b)]

    def rejoin(pair, axis):
        lead = pair[0].shape[:axis]
        rest = pair[0].shape[axis + 1 :]
        parts = [p.reshape(lead + (SHARDS if axis else 1, -1) + rest) for p in pair]
        return jnp.stack(parts, axis=axis + 1).reshape(lead + (-1,) + rest)

    if fast:
        raw = [rejoin([b[i] for b in both], axis) for i, axis in ((0, 1), (1, 1), (2, 0))]
    else:
        raw = []
        for i, axis in ((0, 1), (1, 1), (2, 0)):
            whole = jax.vmap(lambda a, b: rejoin([a, b], axis))(both[0][i], both[1][i])
            raw.append(reduce(whole.reshape(-1, whole.shape[-1])))
    g2 = jnp.sum(raw[0] * w_gate.astype(F32), axis=1) + jnp.sum(raw[1] * w_up.astype(F32), axis=1)
    dwg, dwu, dwd = raw[0] * gain2, raw[1] * gain2, raw[2]

    dwo, dws = joint[:, :d], [joint[:, d : d + 3 * GW], joint[:, d + 3 * GW :], dw2]
    raw = [jnp.concatenate([w[:, i * GW : (i + 1) * GW] for w in dws], axis=1) for i in range(3)]
    raw = [natural_order(raw[0]), natural_order(raw[1]), raw[2]]
    g1 = sum(jnp.sum(r * w.astype(F32), axis=1) for r, w in zip(raw, (w_query, w_key, w_value)))
    dwq, dwk, dwv = (r * gain1 for r in raw)
    return out, grad_tokens, g1, dwq, dwk, dwv, dwo, g2, dwg, dwu, dwd


def solution(mesh):
    in_specs = (
        P(("rep", "fsdp"), None),
        P(("rep", "fsdp"), None),
        P(("rep", "fsdp")),
        P(("rep", "fsdp"), None, None),
        P("fsdp"),
        P("fsdp", None),
        P("fsdp", None),
        P("fsdp", None),
        P("fsdp", None),
        P("fsdp"),
        P("fsdp", None),
        P("fsdp", None),
        P("fsdp", None),
    )
    out_specs = (
        P(("rep", "fsdp"), None),
        P(("rep", "fsdp"), None),
        P("fsdp"),
        P("fsdp", None),
        P("fsdp", None),
        P("fsdp", None),
        P("fsdp", None),
        P("fsdp"),
        P("fsdp", None),
        P("fsdp", None),
        P("fsdp", None),
    )
    sizes = dict(reps=mesh.shape["rep"], size=mesh.shape["fsdp"])
    return jax.shard_map(functools.partial(body, **sizes), mesh=mesh, in_specs=in_specs, out_specs=out_specs, check_vma=False)
```

```python
import functools
import jax
import jax.numpy as jnp
import numpy as np
from jax import lax
from jax.experimental import pallas as pl
from jax.experimental.pallas import tpu as pltpu
from jax.sharding import PartitionSpec as P

HEAD_DIM = 64
COLS = 24
GRID = 32
EPSILON = 1e-05
GROUP = 4
GW = GROUP * HEAD_DIM
HALF = GW // 2
BF = jnp.bfloat16
F32 = jnp.float32


def nn(a, b):
    return lax.dot_general(a, b, (((1,), (0,)), ((), ())), preferred_element_type=F32)


def nt(a, b):
    return lax.dot_general(a, b, (((1,), (1,)), ((), ())), preferred_element_type=F32)


def tn(a, b):
    return lax.dot_general(a, b, (((0,), (0,)), ((), ())), preferred_element_type=F32)


def params(limit=60):
    return pltpu.CompilerParams(vmem_limit_bytes=limit * 1024 * 1024)


def cost(flops, moved):
    return pl.CostEstimate(flops=int(flops), transcendentals=0, bytes_accessed=int(moved))


def inverse_rms(x):
    return lax.rsqrt(jnp.mean(x * x, axis=-1, keepdims=True) + EPSILON)


def angle_table():
    lane = np.arange(HALF)
    theta = (1.0 / 10000.0 ** (np.arange(HEAD_DIM // 4) * 4.0 / HEAD_DIM)).astype(np.float32)
    angle = np.arange(GRID, dtype=np.float32)[:, None] * theta[lane % (HEAD_DIM // 4)]
    by_row = (lane // (HEAD_DIM // 4)) % 2 == 0
    both = np.concatenate([np.cos(angle.astype(np.float64)), np.sin(angle.astype(np.float64))], axis=1)
    use = np.concatenate([by_row, by_row])
    left = np.concatenate([np.where(use, both, 0.0), np.where(use, 0.0, both)], axis=0).astype(np.float32)
    parts = []
    for _ in range(3):
        part = left.astype(jnp.bfloat16)
        parts.append(part)
        left = left - part.astype(np.float32)
    return np.concatenate(parts, axis=1)


def norm_kernel(x_ref, rope_ref, table_ref, out_ref, cos_ref, sin_ref):
    x = x_ref[...].astype(F32)
    out_ref[...] = (x * inverse_rms(x)).astype(BF)
    slot = x.shape[0]
    place = lax.broadcasted_iota(jnp.int32, (GRID, slot), 0)
    hot = jnp.concatenate([place == rope_ref[0, i : i + 1, :] for i in range(2)], axis=0)
    found = tn(jnp.where(hot, 1.0, 0.0).astype(BF), table_ref[...])
    found = found[:, :GW] + found[:, GW : 2 * GW] + found[:, 2 * GW :]
    cos_ref[...] = found[:, :HALF]
    sin_ref[...] = found[:, HALF:]


def norm_call(x, positions):
    n, d = x.shape
    crops, two, slot = positions.shape
    spec = lambda w: pl.BlockSpec((slot, w), lambda i: (i, 0))
    table = jnp.asarray(angle_table())
    return pl.pallas_call(
        norm_kernel,
        grid=(crops,),
        in_specs=[
            spec(d),
            pl.BlockSpec((1, two, slot), lambda i: (i, 0, 0)),
            pl.BlockSpec(table.shape, lambda i: (0, 0)),
        ],
        out_specs=[spec(d), spec(HALF), spec(HALF)],
        out_shape=[
            jax.ShapeDtypeStruct((n, d), BF),
            jax.ShapeDtypeStruct((n, HALF), F32),
            jax.ShapeDtypeStruct((n, HALF), F32),
        ],
        compiler_params=params(),
        cost_estimate=cost(0, 12 * n * d),
        name="norm_in",
    )(x, positions, table)


def head_masks():
    lane = lax.broadcasted_iota(jnp.int32, (1, GW), 1)
    rot = [((lane % HALF) // (HEAD_DIM // 2) == h) for h in range(GROUP)]
    nat = [(lane // HEAD_DIM == h) for h in range(GROUP)]
    return rot, nat


def mask_to(x, m):
    return x * jnp.where(m, 1.0, 0.0).astype(x.dtype)


def blocks_of(total, size):
    return [(s, min(s + size, total)) for s in range(0, total, size)]


def attn_fwd_kernel(slot, size, pair, ids_ref, nm_ref, cos_ref, sin_ref, own_hbm, oth_hbm,
                    qkv_ref, att_ref, lse_ref, w_out_ref, sem):
    group = pl.program_id(0)
    crop = pl.program_id(1)
    crops = pl.num_programs(1)
    zs = own_hbm.shape[1]
    rep, z, core = ids_ref[crops], ids_ref[crops + 1], ids_ref[crops + 2]

    @pl.when(crop == 0)
    def _():
        made = []
        for hbm, place in ((own_hbm, core), (oth_hbm, 1 - core)):
            for kind in range(4):
                for j in range(zs):
                    src = hbm.at[kind ^ rep, j, :, pl.ds(pl.multiple_of(group * GW, GW), GW)]
                    dst = w_out_ref.at[(z + j) & (zs - 1), place, :, pl.ds(kind * GW, GW)]
                    made.append(pltpu.make_async_copy(src, dst, sem.at[len(made)]))
        for copy in made:
            copy.start()
        for copy in made:
            copy.wait()

    nm = nm_ref[...]
    cos = cos_ref[...]
    sin = sin_ref[...]
    rot_m, nat_m = head_masks()
    d = nm.shape[1]

    def rotated(lo, scale):
        u = nn(nm, w_out_ref[:, :, :, lo : lo + GW].reshape(d, GW))
        a, b = u[:, :HALF], u[:, HALF:]
        r = jnp.concatenate([a * cos - b * sin, a * sin + b * cos], axis=1)
        return r.astype(BF) * jnp.asarray(scale, BF)

    q = rotated(0, HEAD_DIM ** (-0.5))
    k = rotated(GW, 1.0)
    v = nn(nm, w_out_ref[:, :, :, 2 * GW : 3 * GW].reshape(d, GW)).astype(BF)
    qkv_ref[:, :GW] = q
    qkv_ref[:, GW : 2 * GW] = k
    qkv_ref[:, 2 * GW :] = v
    qs = [mask_to(q, m) for m in rot_m]
    lane = lax.broadcasted_iota(jnp.int32, (1, 128), 1)
    units = [(s, e, h) for s, e in blocks_of(slot, size) for h in range(0, GROUP, pair)]

    def scores(s, e, h):
        stack = jnp.concatenate([qs[i][s:e] for i in range(h, h + pair)], axis=0)
        return nt(stack, k[s:e]), nt(stack, k[:s]) if s else None

    out = logs = None
    ready = scores(*units[0])
    for i, (s, e, h) in enumerate(units):
        later = scores(*units[i + 1]) if i + 1 < len(units) else None
        diag, left = ready
        w = e - s
        row = lax.broadcasted_iota(jnp.int32, (pair, w, w), 1).reshape(pair * w, w)
        col = lax.broadcasted_iota(jnp.int32, (pair, w, w), 2).reshape(pair * w, w)
        diag = jnp.where(row >= col, diag, -1e30)
        top = jnp.max(diag, axis=-1, keepdims=True)
        if s:
            top = jnp.maximum(top, jnp.max(left, axis=-1, keepdims=True))
        pd = jnp.exp(diag - top)
        total = jnp.sum(pd, axis=-1, keepdims=True)
        o = nn(pd.astype(BF), v[s:e])
        if s:
            pleft = jnp.exp(left - top)
            total = total + jnp.sum(pleft, axis=-1, keepdims=True)
            o = o + nn(pleft.astype(BF), v[:s])
        o = o * (1.0 / total)
        log = top + jnp.log(total)
        for g in range(pair):
            part = slice(g * w, (g + 1) * w)
            out = jnp.where(nat_m[h + g], o[part], out if h + g else 0.0)
            logs = jnp.where(lane == h + g, log[part], logs if h + g else 0.0)
        if h + pair == GROUP:
            att_ref[s:e, :] = out.astype(BF)
            lse_ref[0, 0, :, s:e] = logs.T[:8]
        ready = later


def attn_fwd(ids, nm, cos, sin, own, oth, slot, size=256, pair=4):
    n, d = nm.shape
    crops = n // slot
    kinds, zs, rows, width = own.shape
    groups = width // GW
    hbm = pl.BlockSpec(memory_space=pl.ANY)
    crop_spec = lambda w: pl.BlockSpec((slot, w), lambda g, c, *_: (c, 0))
    qkv, att, lse, w = pl.pallas_call(
        functools.partial(attn_fwd_kernel, slot, size, pair),
        grid_spec=pltpu.PrefetchScalarGridSpec(
            num_scalar_prefetch=1,
            grid=(groups, crops),
            in_specs=[crop_spec(d), crop_spec(HALF), crop_spec(HALF), hbm, hbm],
            out_specs=[
                pl.BlockSpec((slot, 3 * GW), lambda g, c, *_: (c, g)),
                pl.BlockSpec((slot, GW), lambda g, c, *_: (c, g)),
                pl.BlockSpec((1, 1, 8, slot), lambda g, c, *_: (g, c, 0, 0)),
                pl.BlockSpec((zs, 2, rows, 4 * GW), lambda g, c, *_: (0, 0, 0, g)),
            ],
            scratch_shapes=[pltpu.SemaphoreType.DMA((8 * zs,))],
        ),
        out_shape=[
            jax.ShapeDtypeStruct((n, groups * 3 * GW), BF),
            jax.ShapeDtypeStruct((n, groups * GW), BF),
            jax.ShapeDtypeStruct((groups, crops, 8, slot), F32),
            jax.ShapeDtypeStruct((zs, 2, rows, groups * 4 * GW), BF),
        ],
        compiler_params=params(),
        cost_estimate=cost(8e6 * groups * n, 2 * n * d),
        name="attn_fwd",
    )(ids, nm, cos, sin, own, oth)
    return qkv, att, lse, w.reshape(d, groups * 4 * GW)


def attn_bwd_kernel(slot, size, pair, qkv_ref, go_ref, att_ref, lse_ref, nm_ref, cos_ref, sin_ref, *refs):
    gqkv_ref, dw_ref, ds_ref, dq_ref, acc_ref = refs[-5:]
    crop = pl.program_id(1)
    q = qkv_ref[:, :GW]
    k = qkv_ref[:, GW : 2 * GW]
    v = qkv_ref[:, 2 * GW :]
    go = go_ref[...]
    rot_m, nat_m = head_masks()
    prod = go.astype(F32) * att_ref[...].astype(F32)
    hi = prod.astype(BF)
    lo = (prod - hi.astype(F32)).astype(BF)
    pick = (
        lax.broadcasted_iota(jnp.int32, (8, GW), 1) // HEAD_DIM
        == lax.broadcasted_iota(jnp.int32, (8, GW), 0)
    )
    pick = jnp.where(pick, 1.0, 0.0).astype(BF)
    delta = nt(pick, hi) + nt(pick, lo)
    blocks = blocks_of(slot, size)
    dk = [None] * len(blocks)
    dv = [None] * len(blocks)
    kms = [mask_to(k, m) for m in rot_m]
    vms = [mask_to(v, m) for m in nat_m]
    units = [(j, s, e, h) for j, (s, e) in enumerate(blocks) for h in range(0, GROUP, pair)]

    def stacked(parts, s, e, h):
        return jnp.concatenate([parts[i][s:e] for i in range(h, h + pair)], axis=0)

    def scores(j, s, e, h):
        return nt(stacked(kms, s, e, h), q[s:]), nt(stacked(vms, s, e, h), go[s:])

    ready = scores(*units[0])
    for i, (j, s, e, h) in enumerate(units):
        later = scores(*units[i + 1]) if i + 1 < len(units) else None
        w = e - s
        row = lax.broadcasted_iota(jnp.int32, (w, w), 0)
        col = lax.broadcasted_iota(jnp.int32, (w, w), 1)
        ps, dss = [], []
        for g in range(pair):
            sc, dp = (x[g * w : (g + 1) * w] for x in ready)
            p = jnp.exp(sc - lse_ref[0, 0, h + g : h + g + 1, s:])
            first = jnp.where(col >= row, p[:, :w], 0.0)
            p = jnp.concatenate([first, p[:, w:]], axis=1) if e < slot else first
            ds = (p * (dp - delta[h + g : h + g + 1, s:])).astype(BF)
            ds_ref[h + g, s:, s:e] = ds.T
            ps.append(p.astype(BF))
            dss.append(ds)
        dvp = nn(jnp.concatenate(ps, axis=0), go[s:])
        dkp = nn(jnp.concatenate(dss, axis=0), q[s:])
        for g in range(pair):
            part = slice(g * w, (g + 1) * w)
            dv[j] = jnp.where(nat_m[h + g], dvp[part], dv[j] if h + g else 0.0)
            dk[j] = jnp.where(rot_m[h + g], dkp[part], dk[j] if h + g else 0.0)
        ready = later
    for s, e in blocks:
        w = e - s
        parts = nn(ds_ref[:, s:e, :e].reshape(GROUP * w, e), k[:e])
        dq = 0.0
        for h in range(GROUP):
            dq = jnp.where(rot_m[h], parts[h * w : (h + 1) * w], dq)
        dq_ref[s:e] = dq
    cos = cos_ref[...]
    sin = sin_ref[...]

    def back(u, c, t):
        a, b = u[:, :HALF], u[:, HALF:]
        return jnp.concatenate([a * c + b * t, b * c - a * t], axis=1).astype(BF)

    for j, (s, e) in enumerate(blocks):
        c, t = cos[s:e], sin[s:e]
        gqkv_ref[s:e, :GW] = back(dq_ref[s:e] * (HEAD_DIM ** (-0.5)), c, t)
        gqkv_ref[s:e, GW : 2 * GW] = back(dk[j], c, t)
        gqkv_ref[s:e, 2 * GW :] = dv[j].astype(BF)
    part = tn(nm_ref[...], gqkv_ref[...])

    @pl.when(crop == 0)
    def _():
        acc_ref[...] = part

    @pl.when(crop != 0)
    def _():
        acc_ref[...] += part

    @pl.when(crop == pl.num_programs(1) - 1)
    def _():
        dw_ref[...] = acc_ref[...].astype(BF)


def attn_bwd(qkv, go, att, lse, nm, cos, sin, slot, place, first, joint=None, size=128, pair=4):
    n, d = nm.shape
    crops = n // slot
    more = [] if joint is None else [joint]
    column = 0 if joint is None else first + place + 1
    row_spec = lambda w, at: pl.BlockSpec((slot, w), lambda g, c: (c, at))
    crop_spec = lambda w: pl.BlockSpec((slot, w), lambda g, c: (c, 0))
    return pl.pallas_call(
        functools.partial(attn_bwd_kernel, slot, size, pair),
        grid=(1, crops),
        in_specs=[
            row_spec(3 * GW, place),
            row_spec(GW, first + place),
            row_spec(GW, place),
            pl.BlockSpec((1, 1, 8, slot), lambda g, c: (place, c, 0, 0)),
            crop_spec(d),
            crop_spec(HALF),
            crop_spec(HALF),
        ]
        + [pl.BlockSpec(memory_space=pl.ANY)] * len(more),
        out_specs=[crop_spec(3 * GW), pl.BlockSpec((d, 3 * GW), lambda g, c: (0, column))],
        out_shape=[
            jax.ShapeDtypeStruct((n, 3 * GW), BF),
            jax.ShapeDtypeStruct((d, 3 * GW) if joint is None else joint.shape, BF),
        ],
        input_output_aliases={7: 1} if more else {},
        scratch_shapes=[
            pltpu.VMEM((GROUP, slot, slot), BF),
            pltpu.VMEM((slot, GW), F32),
            pltpu.VMEM((d, 3 * GW), F32),
        ],
        compiler_params=params(),
        cost_estimate=cost(12e6 * n, 2 * n * d),
        name="attn_bwd",
    )(qkv, go, att, lse, nm, cos, sin, *more)


def valid_rows(ids_ref, tile, rows, slot):
    row = tile * rows + lax.broadcasted_iota(jnp.int32, (rows, 1), 0)
    crop = row // slot
    first = tile * rows // slot
    limit = jnp.zeros((rows, 1), jnp.int32)
    for i in range(-(-rows // slot) + 1):
        index = first + i
        limit = jnp.where(crop == index, ids_ref[index] * COLS, limit)
    return row - crop * slot < limit


def out_weights(weights, d):
    arrays, specs = [], []
    for w in weights:
        for g in range(w.shape[1] // (4 * GW)):
            arrays.append(w)
            specs.append(pl.BlockSpec((d, GW), lambda c, *_, g=g: (0, 4 * g + 3)))
    return arrays, specs


def out_proj_kernel(slot, n_att, ids_ref, x_ref, *refs):
    att_refs, refs = refs[:n_att], refs[n_att:]
    *wo_refs, mid_ref, nm_ref = refs
    valid = valid_rows(ids_ref, pl.program_id(0), x_ref.shape[0], slot)
    att = jnp.concatenate([a[...] for a in att_refs], axis=1)
    proj = jnp.concatenate([nn(att, w[...]) for w in wo_refs], axis=1)
    mid = x_ref[...].astype(F32) + jnp.where(valid, proj, 0.0)
    mid_ref[...] = mid.astype(BF)
    nm_ref[...] = (mid * inverse_rms(mid)).astype(BF)


def out_proj(ids, x, atts, weights, slot, tile):
    n, d = x.shape
    rows = lambda w: pl.BlockSpec((tile, w), lambda c, *_: (c, 0))
    wos, wo_specs = out_weights(weights, d)
    return pl.pallas_call(
        functools.partial(out_proj_kernel, slot, len(atts)),
        grid_spec=pltpu.PrefetchScalarGridSpec(
            num_scalar_prefetch=1,
            grid=(n // tile,),
            in_specs=[rows(d)] + [rows(a.shape[1]) for a in atts] + wo_specs,
            out_specs=[rows(d), rows(d)],
        ),
        out_shape=[jax.ShapeDtypeStruct((n, d), BF), jax.ShapeDtypeStruct((n, d), BF)],
        compiler_params=params(),
        cost_estimate=cost(2 * n * d * d, 10 * n * d),
        name="out_proj",
    )(ids, x, *atts, *wos)


PACK = 512
TILE = 768
SHARDS = 8


def halves(w, axis):
    shape = w.shape[:axis] + (-1, 2, w.shape[axis] // (2 * SHARDS) if axis else w.shape[0] // 2) + w.shape[axis + 1 :]
    w = w.reshape(shape)
    return [
        lax.index_in_dim(w, i, axis + 1, keepdims=False).reshape(w.shape[:axis] + (-1,) + w.shape[axis + 3 :])
        for i in range(2)
    ]


def pack_mlp(gate, up, down):
    wide = [w[:, i : i + PACK] for w in (gate, up) for i in range(0, w.shape[1], PACK)]
    half = down.shape[0] // 2
    tail = down[:, PACK:]
    fold = jnp.concatenate([tail[:half], tail[half:]], axis=1)
    return jnp.concatenate(wide + [down[:, :PACK], fold], axis=0)


def unpack_mlp(pack, rows, d):
    chunks = 2
    gate, up = (
        jnp.concatenate([pack[i * rows : (i + 1) * rows] for i in range(s, s + chunks)], axis=1)
        for s in (0, chunks)
    )
    base = 2 * chunks * rows
    deep = (pack.shape[0] - base) * PACK // d
    fold = pack[base + deep :]
    tail = jnp.concatenate([fold[:, : d - PACK], fold[:, d - PACK :]], axis=0)
    return gate, up, jnp.concatenate([pack[base : base + deep], tail], axis=1)


def mlp_kernel(slot, final, step, ids_ref, nm_ref, cot_ref, part_ref, *refs):
    if final:
        before_ref, *refs = refs
    (pack_hbm, out_ref, dn_ref, grad_hbm, wg_buf, wu_buf, wd_buf, hid_ref, gg_ref, gu_ref,
     ag_ref, au_ref, ad_ref, sg_ref, su_ref, sd_ref, in_sem, out_sem) = refs
    tile = pl.program_id(0)
    d = nm_ref.shape[1]
    chunks, shards, rows, _ = sg_ref.shape
    units = chunks * PACK
    some = shards // chunks
    deep = sd_ref.shape[1]
    base = 2 * chunks * rows
    side = d - PACK

    def pieces(hbm, wg, wu, wd):
        for i in range(chunks):
            yield hbm.at[:, pl.ds(i * rows, rows), :], wg.at[i]
            yield hbm.at[:, pl.ds((chunks + i) * rows, rows), :], wu.at[i]
        yield hbm.at[:, pl.ds(base, deep), :], wd.at[:, :, pl.ds(0, PACK)]
        for i in range(2):
            yield (
                hbm.at[:, pl.ds(base + deep, deep // 2), pl.ds(i * side, side)],
                wd.at[:, pl.ds(i * (deep // 2), deep // 2), pl.ds(PACK, side)],
            )

    @pl.when(tile == 0)
    def _():
        made = pieces(pack_hbm, wg_buf, wu_buf, wd_buf)
        made = [pltpu.make_async_copy(a, b, in_sem.at[i]) for i, (a, b) in enumerate(made)]
        for copy in made:
            copy.start()
        ag_ref[...] = jnp.zeros_like(ag_ref)
        au_ref[...] = jnp.zeros_like(au_ref)
        ad_ref[...] = jnp.zeros_like(ad_ref)
        for copy in made:
            copy.wait()

    valid = valid_rows(ids_ref, tile, nm_ref.shape[0], slot)
    nm = nm_ref[...]
    gb = jnp.where(valid, cot_ref[...], jnp.zeros((), BF))
    wd = wd_buf[...].reshape(units, d)

    def wide(buf, i):
        at = i * step
        return buf[at // PACK, :, :, at % PACK : at % PACK + step].reshape(d, step)

    def first(i):
        return (
            nn(nm, wide(wg_buf, i)),
            nn(nm, wide(wu_buf, i)),
            nt(gb, wd[i * step : (i + 1) * step]),
        )

    def second(i, g, u, gh):
        cols = slice(i * step, (i + 1) * step)
        sg = 0.5 * jnp.tanh(0.5 * g) + 0.5
        act = g * sg
        hid_ref[:, cols] = (act * u).astype(BF)
        gu_ref[:, cols] = (gh * act).astype(BF)
        gg_ref[:, cols] = (gh * u * (sg + act * (1.0 - sg))).astype(BF)

    ready = first(0)
    for i in range(1, units // step):
        later = first(i)
        second(i - 1, *ready)
        ready = later
    second(units // step - 1, *ready)
    nmt = nm.T
    gbt = gb.T
    o = part_ref[...].astype(F32) + jnp.where(valid, nn(hid_ref[...], wd), 0.0)
    out_ref[...] = o.astype(out_ref.dtype)
    dn = before_ref[...].astype(F32) if final else 0.0
    for i in range(chunks):
        cols = slice(i * PACK, (i + 1) * PACK)
        dn = dn + nt(gg_ref[:, cols], wg_buf[i].reshape(d, PACK)) + nt(gu_ref[:, cols], wu_buf[i].reshape(d, PACK))
    dn_ref[...] = dn.astype(dn_ref.dtype)
    for i in range(chunks):
        cols = slice(i * PACK, (i + 1) * PACK)
        ag_ref[i] += nn(nmt, gg_ref[:, cols])
        au_ref[i] += nn(nmt, gu_ref[:, cols])
        ad_ref[i] += nn(gbt, hid_ref[:, cols])

    @pl.when(tile == pl.num_programs(0) - 1)
    def _():
        sg_ref[...] = ag_ref[...].astype(BF).reshape(sg_ref.shape)
        su_ref[...] = au_ref[...].astype(BF).reshape(su_ref.shape)
        for i in range(chunks):
            sd_ref[i * some : (i + 1) * some] = ad_ref[i].astype(BF).T.reshape(some, deep, d)
        made = pieces(grad_hbm, sg_ref, su_ref, sd_ref)
        made = [pltpu.make_async_copy(b, a, out_sem.at[i]) for i, (a, b) in enumerate(made)]
        for copy in made:
            copy.start()
        for copy in made:
            copy.wait()


def mlp(ids, nm, cot, part, before, pack, slot, tile, step=256):
    n, d = nm.shape
    rows = d // SHARDS
    chunks = 2
    deep = chunks * PACK // SHARDS
    final = before is not None
    spec = pl.BlockSpec((tile, d), lambda i, *_: (i, 0))
    hbm = pl.BlockSpec(memory_space=pl.ANY)
    packed = pltpu.VMEM((chunks, SHARDS, rows, PACK), BF)
    units = pltpu.VMEM((tile, chunks * PACK), BF)
    sums = pltpu.VMEM((chunks, d, PACK), F32)
    return pl.pallas_call(
        functools.partial(mlp_kernel, slot, final, step),
        grid_spec=pltpu.PrefetchScalarGridSpec(
            num_scalar_prefetch=1,
            grid=(n // tile,),
            in_specs=[spec] * (3 + final) + [hbm],
            out_specs=[spec, spec, hbm],
            scratch_shapes=[packed, packed, pltpu.VMEM((SHARDS, deep, d), BF)]
            + [units] * 3
            + [sums] * 3
            + [packed, packed, pltpu.VMEM((SHARDS, deep, d), BF)]
            + [pltpu.SemaphoreType.DMA((2 * chunks + 3,))] * 2,
        ),
        out_shape=[
            jax.ShapeDtypeStruct((n, d), BF),
            jax.ShapeDtypeStruct((n, d), BF),
            jax.ShapeDtypeStruct(pack.shape, BF),
        ],
        compiler_params=params(),
        cost_estimate=cost(24e6 * n, 20 * n * d),
        name="mlp",
    )(ids, nm, cot, part, *([before] if final else []), pack)


def norm_back(scaled, field):
    inv = inverse_rms(field)
    return inv * scaled - field * (inv * inv * inv * jnp.mean(scaled * field, axis=-1, keepdims=True))


def mid_grad_kernel(slot, n_att, ids_ref, cot_ref, mid_ref, dn_ref, *refs):
    att_refs, refs = refs[:n_att], refs[n_att:]
    *wo_refs, gmid_ref, gatt_ref, dwo_ref, acc_ref = refs
    c = pl.program_id(0)
    valid = valid_rows(ids_ref, c, cot_ref.shape[0], slot)
    gm = cot_ref[...].astype(F32) + norm_back(dn_ref[...].astype(F32), mid_ref[...].astype(F32))
    gmid_ref[...] = gm.astype(BF)
    ga = jnp.where(valid, gm, 0.0).astype(BF)
    gatt = sum(nt(ga[:, i * GW : (i + 1) * GW], w[...]) for i, w in enumerate(wo_refs))
    gatt_ref[...] = gatt.astype(BF)
    part = tn(jnp.concatenate([a[...] for a in att_refs], axis=1), ga)

    @pl.when(c == 0)
    def _():
        acc_ref[...] = part

    @pl.when(c != 0)
    def _():
        acc_ref[...] += part

    @pl.when(c == pl.num_programs(0) - 1)
    def _():
        dwo_ref[...] = acc_ref[...].astype(BF)


def mid_grad(ids, cot, mid, dn, atts, weights, slot, tile):
    n, d = cot.shape
    rows = lambda w: pl.BlockSpec((tile, w), lambda c, *_: (c, 0))
    wos, wo_specs = out_weights(weights, d)
    return pl.pallas_call(
        functools.partial(mid_grad_kernel, slot, len(atts)),
        grid_spec=pltpu.PrefetchScalarGridSpec(
            num_scalar_prefetch=1,
            grid=(n // tile,),
            in_specs=[rows(d)] * 3 + [rows(a.shape[1]) for a in atts] + wo_specs,
            out_specs=[rows(d), rows(d), pl.BlockSpec((d, d), lambda c, *_: (0, 0))],
            scratch_shapes=[pltpu.VMEM((d, d), F32)],
        ),
        out_shape=[
            jax.ShapeDtypeStruct((n, d), BF),
            jax.ShapeDtypeStruct((n, d), BF),
            jax.ShapeDtypeStruct((d, 3 * d), BF),
        ],
        compiler_params=params(),
        cost_estimate=cost(4 * n * d * d, 18 * n * d),
        name="mid_grad",
    )(ids, cot, mid, dn, *atts, *wos)


def input_grad_kernel(n_group, *refs):
    g_refs, w_refs = refs[:n_group], refs[n_group : 4 * n_group]
    x_ref, gmid_ref = refs[4 * n_group : 4 * n_group + 2]
    out_ref = refs[-1]
    e = 0.0
    for i, g in enumerate(g_refs):
        w = jnp.concatenate([w[...] for w in w_refs[3 * i : 3 * i + 3]], axis=1)
        e = e + nt(g[...], w)
    out_ref[...] = gmid_ref[...].astype(F32) + norm_back(e, x_ref[...].astype(F32))


def input_grad(gqkvs, weights, x, gmid, rows, start, stop, filled=None):
    n, d = x.shape
    arrays = [(w, 4 * g + i) for w in weights for g in range(w.shape[1] // (4 * GW)) for i in range(3)]
    spec = lambda w: pl.BlockSpec((rows, w), lambda i: (start + i, 0))
    more = [] if filled is None else [filled]
    n_in = 4 * len(gqkvs) + 2
    count = (stop - start) * rows
    return pl.pallas_call(
        functools.partial(input_grad_kernel, len(gqkvs)),
        grid=(stop - start,),
        in_specs=[spec(3 * GW)] * len(gqkvs)
        + [pl.BlockSpec((d, GW), lambda i, g=g: (0, g)) for _, g in arrays]
        + [spec(d), spec(d)]
        + [pl.BlockSpec(memory_space=pl.ANY)] * len(more),
        out_specs=spec(d),
        out_shape=jax.ShapeDtypeStruct((n, d), F32),
        input_output_aliases={n_in: 0} if more else {},
        compiler_params=params(),
        cost_estimate=cost(6 * count * d * d, 16 * count * d),
        name="input_grad",
    )(*gqkvs, *[w for w, _ in arrays], x, gmid, *more)


def column_of(row_ref):
    row = row_ref[...].astype(F32)
    return jnp.broadcast_to(row, (128, row.shape[1])).T[:, :1]


def lane_order(to_natural):
    lane = lax.broadcasted_iota(jnp.int32, (GW, GW), 1)
    half = HEAD_DIM // 2
    if to_natural:
        source = lane // HEAD_DIM * half + lane % half + jnp.where(lane % HEAD_DIM < half, 0, HALF)
    else:
        source = lane % HALF // half * HEAD_DIM + lane // HALF * half + lane % half
    return jnp.where(lax.broadcasted_iota(jnp.int32, (GW, GW), 0) == source, 1.0, 0.0).astype(BF)


def join_kernel(place_ref, wq_ref, wk_ref, wv_ref, wo_ref, gain_ref, out_ref):
    for kind, w_ref in enumerate((wq_ref, wk_ref, wv_ref, wo_ref)):

        @pl.when(place_ref[0] == kind)
        def _(kind=kind, w_ref=w_ref):
            w = w_ref[...]
            if kind < 3:
                w = (w.astype(F32) * column_of(gain_ref)).astype(BF)
            if kind < 2:
                order = lane_order(False)
                for at in range(0, w.shape[1], GW):
                    out_ref[:, at : at + GW] = nn(w[:, at : at + GW], order).astype(BF)
            else:
                out_ref[...] = w


def join_call(place, wq, wk, wv, wo, gain):
    vmem = pl.BlockSpec(memory_space=pltpu.VMEM)
    return pl.pallas_call(
        join_kernel,
        grid_spec=pltpu.PrefetchScalarGridSpec(
            num_scalar_prefetch=1, grid=(1,), in_specs=[vmem] * 5, out_specs=vmem
        ),
        out_shape=jax.ShapeDtypeStruct(wq.shape, BF),
        compiler_params=params(),
        cost_estimate=cost(0, 1e6),
        name="join",
    )(place, wq, wk, wv, wo, gain)


def pack_kernel(wg_ref, wu_ref, wd_ref, gain_ref, a_ref, b_ref):
    rows, ff = wg_ref.shape
    units = ff // (2 * SHARDS)
    deep = wd_ref.shape[0] // 2
    side = wd_ref.shape[1] - PACK
    chunks = ff // (2 * PACK)
    base = 2 * chunks * rows
    gain = column_of(gain_ref)
    for half, out_ref in enumerate((a_ref, b_ref)):
        for w_ref, first in ((wg_ref, 0), (wu_ref, chunks)):
            for i in range(chunks):
                at = (first + i) * rows
                for j in range(PACK // units):
                    source = (i * (PACK // units) + j) * 2 * units + half * units
                    part = w_ref[:, source : source + units].astype(F32) * gain
                    out_ref[at : at + rows, j * units : (j + 1) * units] = part.astype(BF)
        at = half * deep
        out_ref[base : base + deep] = wd_ref[at : at + deep, :PACK]
        for i in range(2):
            source = at + i * (deep // 2)
            out_ref[base + deep :, i * side : (i + 1) * side] = wd_ref[source : source + deep // 2, PACK:]


def pack_call(wg, wu, wd, gain):
    size = (wg.size + wu.size + wd.size) // (2 * PACK)
    return pl.pallas_call(
        pack_kernel,
        out_shape=[jax.ShapeDtypeStruct((size, PACK), BF)] * 2,
        compiler_params=params(),
        cost_estimate=cost(0, 4e6),
        name="pack",
    )(wg, wu, wd, gain)


def row_of(column):
    return jnp.broadcast_to(column, (column.shape[0], 128)).T[:1]


def mlp_end_kernel(a0_ref, a1_ref, b0_ref, b1_ref, wg_ref, wu_ref, gain_ref, dwg_ref, dwu_ref, dwd_ref, g_ref):
    rows = wg_ref.shape[0]
    units = wg_ref.shape[1] // (2 * SHARDS)
    deep = dwd_ref.shape[0] // 2
    side = dwd_ref.shape[1] - PACK
    chunks = wg_ref.shape[1] // (2 * PACK)
    base = 2 * chunks * rows
    gain = column_of(gain_ref)
    dot = jnp.zeros((rows, units), F32)
    for half, (left, right) in enumerate(((a0_ref, a1_ref), (b0_ref, b1_ref))):
        for w_ref, out_ref, first in ((wg_ref, dwg_ref, 0), (wu_ref, dwu_ref, chunks)):
            for i in range(chunks):
                at = (first + i) * rows
                block = left[at : at + rows].astype(F32) + right[at : at + rows].astype(F32)
                for j in range(PACK // units):
                    to = (i * (PACK // units) + j) * 2 * units + half * units
                    part = block[:, j * units : (j + 1) * units]
                    dot = dot + part * w_ref[:, to : to + units].astype(F32)
                    out_ref[:, to : to + units] = part * gain
        down = left[base:].astype(F32) + right[base:].astype(F32)
        at = half * deep
        dwd_ref[at : at + deep, :PACK] = down[:deep]
        for i in range(2):
            to = at + i * (deep // 2)
            dwd_ref[to : to + deep // 2, PACK:] = down[deep:, i * side : (i + 1) * side]
    g_ref[...] = row_of(jnp.sum(dot, axis=1, keepdims=True))


def mlp_end(a0, a1, b0, b1, wg, wu, gain, down_shape):
    rows = wg.shape[0]
    return pl.pallas_call(
        mlp_end_kernel,
        out_shape=[
            jax.ShapeDtypeStruct(wg.shape, F32),
            jax.ShapeDtypeStruct(wu.shape, F32),
            jax.ShapeDtypeStruct(down_shape, F32),
            jax.ShapeDtypeStruct((1, rows), F32),
        ],
        compiler_params=params(),
        cost_estimate=cost(0, 6e6),
        name="mlp_end",
    )(a0, a1, b0, b1, wg, wu, gain)


def natural(block, order):
    moved = 0.0
    for _ in range(3):
        part = block.astype(BF)
        moved = moved + nn(part, order)
        block = block - part.astype(F32)
    return moved


def attn_end_kernel(l0_ref, l1_ref, r0_ref, r1_ref, wq_ref, wk_ref, wv_ref, gain_ref,
                    dwq_ref, dwk_ref, dwv_ref, dwo_ref, g_ref):
    rows, d = wq_ref.shape
    gain = column_of(gain_ref)

    def summed(lo, hi):
        pairs = ((l0_ref, r0_ref), (l1_ref, r1_ref))
        return jnp.concatenate([l[:, lo:hi].astype(F32) + r[:, lo:hi].astype(F32) for l, r in pairs], axis=0)

    dwo_ref[...] = summed(0, d)
    order = lane_order(True)
    dot = jnp.zeros((rows, GW), F32)
    for g in range(d // GW - 1):
        for kind, (w_ref, out_ref) in enumerate(((wq_ref, dwq_ref), (wk_ref, dwk_ref), (wv_ref, dwv_ref))):
            at = d + (3 * g + kind) * GW
            block = summed(at, at + GW)
            if kind < 2:
                block = natural(block, order)
            cols = slice(g * GW, (g + 1) * GW)
            dot = dot + block * w_ref[:, cols].astype(F32)
            out_ref[:, cols] = block * gain
    g_ref[...] = row_of(jnp.sum(dot, axis=1, keepdims=True))


def attn_end(lefts, rights, wq, wk, wv, gain):
    rows, d = wq.shape
    return pl.pallas_call(
        attn_end_kernel,
        out_shape=[jax.ShapeDtypeStruct((rows, d), F32)] * 4 + [jax.ShapeDtypeStruct((1, rows), F32)],
        compiler_params=params(),
        cost_estimate=cost(0, 6e6),
        name="attn_end",
    )(*lefts, *rights, wq, wk, wv, gain)


def last_end_kernel(place_ref, last_ref, wq_ref, wk_ref, wv_ref, gain_ref, before_ref, *refs):
    out_refs, g_ref, last_buf = refs[3:6], refs[6], refs[7]
    reps, few, _ = last_ref.shape
    gain = column_of(gain_ref)
    for r in range(reps):
        last_buf[r * few : (r + 1) * few] = last_ref[r ^ place_ref[0]].astype(F32)
    order = lane_order(True)
    dot = 0.0
    for kind, (w_ref, out_ref) in enumerate(zip((wq_ref, wk_ref, wv_ref), out_refs)):
        block = last_buf[:, kind * GW : (kind + 1) * GW]
        if kind < 2:
            block = natural(block, order)
        dot = dot + block * w_ref[...].astype(F32)
        out_ref[...] = block * gain
    g_ref[...] = before_ref[...] + row_of(jnp.sum(dot, axis=1, keepdims=True))


def last_end(place, last, wq, wk, wv, gain, g, dwq, dwk, dwv):
    rows, d = wq.shape
    vmem = pl.BlockSpec(memory_space=pltpu.VMEM)
    group = pl.BlockSpec((rows, GW), lambda i, *_: (0, d // GW - 1))
    return pl.pallas_call(
        last_end_kernel,
        grid_spec=pltpu.PrefetchScalarGridSpec(
            num_scalar_prefetch=1,
            grid=(1,),
            in_specs=[vmem, group, group, group, vmem, vmem] + [pl.BlockSpec(memory_space=pl.ANY)] * 3,
            out_specs=[group] * 3 + [vmem],
            scratch_shapes=[pltpu.VMEM((rows, 3 * GW), F32)],
        ),
        out_shape=[jax.ShapeDtypeStruct((rows, d), F32)] * 3 + [jax.ShapeDtypeStruct((1, rows), F32)],
        input_output_aliases={7: 0, 8: 1, 9: 2},
        compiler_params=params(),
        cost_estimate=cost(0, 3e6),
        name="last_end",
    )(place, last, wq, wk, wv, gain, g, dwq, dwk, dwv)


def rot_order(w):
    rows, cols = w.shape
    w = w.reshape(rows, cols // GW, GROUP, 2, HEAD_DIM // 2)
    return w.transpose(0, 1, 3, 2, 4).reshape(rows, cols)


def natural_order(w):
    rows, cols = w.shape
    w = w.reshape(rows, cols // GW, 2, GROUP, HEAD_DIM // 2)
    return w.transpose(0, 1, 3, 2, 4).reshape(rows, cols)


def join_attn(wq, wk, wv, wo, gain):
    scaled = [(w.astype(F32) * gain).astype(BF) for w in (rot_order(wq), rot_order(wk), wv)]
    return jnp.stack(scaled + [wo])


def swap(x, axis, bit, size):
    return lax.ppermute(x, axis, [(i, i ^ bit) for i in range(size)])


def shift(x, step, size):
    half = size // 2
    return lax.ppermute(x, "fsdp", [(((i // 2 + step) % half) * 2 + i % 2, i) for i in range(size)])


def pick(x, index, axis=0):
    return lax.dynamic_index_in_dim(x, index, axis, keepdims=False)


def total(*parts):
    return sum(p.astype(F32) for p in parts).astype(BF)


def along_z(mine, size):
    return jnp.stack([mine] + [shift(mine, k, size) for k in range(1, size // 2)])


def over_reps(x, reps):
    return jnp.stack([x] + [swap(x, "rep", bit, reps) for bit in range(1, reps)])


def sum_reps(x, reps):
    if reps != 4:
        return lax.psum(x, "rep").astype(F32)
    x = (x.astype(F32) + swap(x, "rep", 1, reps).astype(F32)).astype(BF)
    return x.astype(F32) + swap(x, "rep", 2, reps).astype(F32)


def body(tokens, cotangent, crop_heights, rope_positions, gain_attn, w_query, w_key, w_value, w_out,
         gain_mlp, w_gate, w_up, w_down, *, reps, size):
    crops = crop_heights.shape[0]
    n, d = tokens.shape
    slot = n // crops
    tile = TILE if n % TILE == 0 else slot
    gain1 = gain_attn.astype(F32)[:, None]
    gain2 = gain_mlp.astype(F32)[:, None]

    def gather(w):
        return lax.all_gather(w, "fsdp", axis=0, tiled=True)

    def scatter(g):
        return lax.psum_scatter(g, "fsdp", scatter_dimension=0, tiled=True)

    def reduce(g):
        return sum_reps(scatter(g), reps)

    pin = lax.optimization_barrier
    links = reps == 4 and size == SHARDS
    rep, f = lax.axis_index("rep"), lax.axis_index("fsdp")
    if links:
        place = jnp.stack([rep, f // 2, f % 2]).astype(jnp.int32)
        row1, row2 = gain_attn[None], gain_mlp[None]
        mine = join_call(place, w_query, w_key, w_value, w_out, row1)
        mine, w_gate, w_up, w_down, tokens_1 = pin((mine, w_gate, w_up, w_down, tokens))
        lines = [along_z(m, size) for m in (mine[:, :GW], mine[:, GW:])]
        sides = [swap(lines[0], "rep", bit, reps) for bit in range(1, reps)]
    else:
        place = jnp.zeros((3,), jnp.int32)
        joined = join_attn(w_query, w_key, w_value, w_out, gain1)
        every = lax.all_gather(joined, "fsdp", axis=1, tiled=True)
        every = every.reshape(4, SHARDS // 2, 2, d // SHARDS, d)
    ids = jnp.concatenate([crop_heights, place])
    if not links:
        tokens_1 = tokens
    nm1, cos, sin = norm_call(tokens_1, rope_positions)
    if links:
        *sides, lines[1], nm1, cos, sin = pin((*sides, lines[1], nm1, cos, sin))
        own = jnp.stack([lines[0]] + sides)
        own, w_gate, w_up, w_down = pin((own, w_gate, w_up, w_down))
        oth = swap(own, "fsdp", 1, size)
        sides = [swap(lines[1], "rep", bit, reps) for bit in range(1, reps)]
        packs = [
            lax.all_gather(p, "fsdp", axis=0, tiled=False) for p in pack_call(w_gate, w_up, w_down, row2)
        ]
    else:
        scaled = [(w.astype(F32) * gain2).astype(BF) for w in (w_gate, w_up)]
        wide = [gather(w).reshape(SHARDS, -1, w.shape[1]) for w in scaled]
        down = gather(w_down).reshape(SHARDS, -1, d)
        split = zip(*[[jnp.stack(h) for h in zip(*[halves(w, a) for w in ws])] for ws, a in
                      ((wide[0], 1), (wide[1], 1), (down, 0))])
        packs = [jax.vmap(pack_mlp)(*part) for part in split]

    attended, weights = [], []
    for i, cols in enumerate((slice(0, GW), slice(GW, d))):
        if not links:
            own, oth = every[:, :, 0, :, cols], every[:, :, 1, :, cols]
        elif i:
            *parts, _ = pin((lines[1], *sides, atts))
            own = jnp.stack(parts)
            oth = swap(own, "fsdp", 1, size)
        *some, w = attn_fwd(ids, nm1, cos, sin, own, oth, slot)
        attended.append(some)
        weights.append(w)
        atts = [a for _, a, _ in attended]
    mid, nm2 = out_proj(ids, tokens, atts, weights, slot, tile)
    part, dn, grad_a = mlp(ids, nm2, cotangent, mid, None, packs[0], slot, tile)
    out, dn, grad_b = mlp(ids, nm2, cotangent, part, dn, packs[1], slot, tile)
    local_a = scatter(grad_a.reshape(-1, PACK)) if links else grad_a
    local_b = scatter(grad_b.reshape(-1, PACK)) if links else grad_b
    gmid, gatt, joint = mid_grad(ids, cotangent, mid, dn, atts, weights, slot, tile)

    def backward(index, gatt, joint=None):
        w = 0 if index == 0 else 1
        qkv, att, lse = attended[w]
        return attn_bwd(qkv, gatt, att, lse, nm1, cos, sin, slot, index - w, w, joint)

    fast = False
    if links:
        local_a, gatt = pin((local_a, gatt))
        local_a = total(local_a, swap(local_a, "rep", 1, reps))
    gqkv0, joint = backward(0, gatt, joint)
    if links:
        local_a, gatt, gqkv0 = pin((local_a, gatt, gqkv0))
        other_a = swap(local_a, "rep", 2, reps)
    gqkv1, joint = backward(1, gatt, joint)
    if links:
        other_a, local_b, joint, gatt, gqkv1 = pin((other_a, local_b, joint, gatt, gqkv1))
        local_b = total(local_b, swap(local_b, "rep", 1, reps))
    joint = scatter(joint)
    gqkv2, dw2 = backward(2, gatt)
    gqkvs = [gqkv0, gqkv1, gqkv2]
    grad = lambda gmid: input_grad(gqkvs, weights, tokens, gmid, tile // 2, 0, 2 * n // tile)
    if links:
        y, x, z, core = rep // 2, rep % 2, f // 2, f % 2
        zs, rows = size // 2, d // size
        cut = dw2.reshape(zs, 2, 2, 2, rows // reps, 3 * GW)
        keep, send = pick(cut, core, 1), pick(cut, 1 - core, 1)
        got = swap(send, "fsdp", 1, size)
        keep, local_b, gqkvs[2] = pin((keep, local_b, gqkvs[2]))
        other_b = swap(local_b, "rep", 2, reps)
        side = swap(total(pick(keep, 1 - x, 2), pick(got, 1 - x, 2)), "rep", 1, reps)
        keep = total(pick(keep, x, 2), pick(got, x, 2))
        keep, gmid = pin((keep, gmid))
        grad_tokens = grad(gmid)
        grad_tokens, keep, side, joint, local_a, other_a = pin((grad_tokens, keep, side, joint, local_a, other_a))
        got = swap(total(pick(keep, 1 - y, 1), pick(side, 1 - y, 1)), "rep", 2, reps)
        cuts = joint[: rows // 2], joint[rows // 2 :]
        others = [swap(part, "rep", 1 + i, reps) for i, part in enumerate(cuts)]
        keep, side = pick(keep, y, 1), pick(side, y, 1)
        *dmlp, g2 = mlp_end(local_a, other_a, local_b, other_b, w_gate, w_up, row2, w_down.shape)
        dmlp[0], keep, side, got = pin((dmlp[0], keep, side, got))

        def at(k):
            i = (z + k) % zs
            return total(pick(keep, i), pick(side, i), pick(got, i))

        sends = [at(zs - k) for k in range(1, zs)]
        first, *others = pin((at(0), *others))
        cuts = [total(a, b) for a, b in zip(cuts, others)]
        others = [swap(part, "rep", 2 - i, reps) for i, part in enumerate(cuts)]
        part = total(first, *[shift(s, k + 1, size) for k, s in enumerate(sends)])
        sides = [swap(part, "rep", bit, reps) for bit in range(1, reps)]
        *dqkv, dwo, g1 = attn_end(cuts, others, w_query, w_key, w_value, row1)
        *sides, g1 = pin((*sides, g1))
        every = jnp.stack([part] + sides)
        *dqkv, g1 = last_end(place, every, w_query, w_key, w_value, row1, g1, *dqkv)
        return (out, grad_tokens, g1.reshape(-1), *dqkv, dwo, g2.reshape(-1), *dmlp)

    grad_tokens = grad(gmid)
    dw2 = reduce(dw2)
    joint = sum_reps(joint, reps)
    if fast:
        sum_a, sum_b = sum_reps(local_a, reps), sum_reps(local_b, reps)
    both = []
    if fast:
        both = [unpack_mlp(x, d // SHARDS, d) for x in (sum_a, sum_b)]
    else:
        both = [jax.vmap(lambda p: unpack_mlp(p, d // SHARDS, d))(grad) for grad in (grad_a, grad_b)]

    def rejoin(pair, axis):
        lead = pair[0].shape[:axis]
        rest = pair[0].shape[axis + 1 :]
        parts = [p.reshape(lead + (SHARDS if axis else 1, -1) + rest) for p in pair]
        return jnp.stack(parts, axis=axis + 1).reshape(lead + (-1,) + rest)

    if fast:
        raw = [rejoin([b[i] for b in both], axis) for i, axis in ((0, 1), (1, 1), (2, 0))]
    else:
        raw = []
        for i, axis in ((0, 1), (1, 1), (2, 0)):
            whole = jax.vmap(lambda a, b: rejoin([a, b], axis))(both[0][i], both[1][i])
            raw.append(reduce(whole.reshape(-1, whole.shape[-1])))
    g2 = jnp.sum(raw[0] * w_gate.astype(F32), axis=1) + jnp.sum(raw[1] * w_up.astype(F32), axis=1)
    dwg, dwu, dwd = raw[0] * gain2, raw[1] * gain2, raw[2]

    dwo, dws = joint[:, :d], [joint[:, d : d + 3 * GW], joint[:, d + 3 * GW :], dw2]
    raw = [jnp.concatenate([w[:, i * GW : (i + 1) * GW] for w in dws], axis=1) for i in range(3)]
    raw = [natural_order(raw[0]), natural_order(raw[1]), raw[2]]
    g1 = sum(jnp.sum(r * w.astype(F32), axis=1) for r, w in zip(raw, (w_query, w_key, w_value)))
    dwq, dwk, dwv = (r * gain1 for r in raw)
    return out, grad_tokens, g1, dwq, dwk, dwv, dwo, g2, dwg, dwu, dwd


def solution(mesh):
    in_specs = (
        P(("rep", "fsdp"), None),
        P(("rep", "fsdp"), None),
        P(("rep", "fsdp")),
        P(("rep", "fsdp"), None, None),
        P("fsdp"),
        P("fsdp", None),
        P("fsdp", None),
        P("fsdp", None),
        P("fsdp", None),
        P("fsdp"),
        P("fsdp", None),
        P("fsdp", None),
        P("fsdp", None),
    )
    out_specs = (
        P(("rep", "fsdp"), None),
        P(("rep", "fsdp"), None),
        P("fsdp"),
        P("fsdp", None),
        P("fsdp", None),
        P("fsdp", None),
        P("fsdp", None),
        P("fsdp"),
        P("fsdp", None),
        P("fsdp", None),
        P("fsdp", None),
    )
    sizes = dict(reps=mesh.shape["rep"], size=mesh.shape["fsdp"])
    return jax.shard_map(functools.partial(body, **sizes), mesh=mesh, in_specs=in_specs, out_specs=out_specs, check_vma=False)
```

```python
import functools
import jax
import jax.numpy as jnp
import numpy as np
from jax import lax
from jax.experimental import pallas as pl
from jax.experimental.pallas import tpu as pltpu
from jax.sharding import PartitionSpec as P

HEAD_DIM = 64
COLS = 24
GRID = 32
EPSILON = 1e-05
GROUP = 4
GW = GROUP * HEAD_DIM
HALF = GW // 2
BF = jnp.bfloat16
F32 = jnp.float32


def nn(a, b):
    return lax.dot_general(a, b, (((1,), (0,)), ((), ())), preferred_element_type=F32)


def nt(a, b):
    return lax.dot_general(a, b, (((1,), (1,)), ((), ())), preferred_element_type=F32)


def tn(a, b):
    return lax.dot_general(a, b, (((0,), (0,)), ((), ())), preferred_element_type=F32)


def params(limit=60):
    return pltpu.CompilerParams(vmem_limit_bytes=limit * 1024 * 1024)


def cost(flops, moved):
    return pl.CostEstimate(flops=int(flops), transcendentals=0, bytes_accessed=int(moved))


def inverse_rms(x):
    return lax.rsqrt(jnp.mean(x * x, axis=-1, keepdims=True) + EPSILON)


def angle_table():
    lane = np.arange(HALF)
    theta = (1.0 / 10000.0 ** (np.arange(HEAD_DIM // 4) * 4.0 / HEAD_DIM)).astype(np.float32)
    angle = np.arange(GRID, dtype=np.float32)[:, None] * theta[lane % (HEAD_DIM // 4)]
    by_row = (lane // (HEAD_DIM // 4)) % 2 == 0
    both = np.concatenate([np.cos(angle.astype(np.float64)), np.sin(angle.astype(np.float64))], axis=1)
    use = np.concatenate([by_row, by_row])
    left = np.concatenate([np.where(use, both, 0.0), np.where(use, 0.0, both)], axis=0).astype(np.float32)
    parts = []
    for _ in range(3):
        part = left.astype(jnp.bfloat16)
        parts.append(part)
        left = left - part.astype(np.float32)
    return np.concatenate(parts, axis=1)


def norm_kernel(x_ref, rope_ref, table_ref, out_ref, cos_ref, sin_ref):
    x = x_ref[...].astype(F32)
    out_ref[...] = (x * inverse_rms(x)).astype(BF)
    slot = x.shape[0]
    place = lax.broadcasted_iota(jnp.int32, (GRID, slot), 0)
    hot = jnp.concatenate([place == rope_ref[0, i : i + 1, :] for i in range(2)], axis=0)
    found = tn(jnp.where(hot, 1.0, 0.0).astype(BF), table_ref[...])
    found = found[:, :GW] + found[:, GW : 2 * GW] + found[:, 2 * GW :]
    cos_ref[...] = found[:, :HALF]
    sin_ref[...] = found[:, HALF:]


def norm_call(x, positions):
    n, d = x.shape
    crops, two, slot = positions.shape
    spec = lambda w: pl.BlockSpec((slot, w), lambda i: (i, 0))
    table = jnp.asarray(angle_table())
    return pl.pallas_call(
        norm_kernel,
        grid=(crops,),
        in_specs=[
            spec(d),
            pl.BlockSpec((1, two, slot), lambda i: (i, 0, 0)),
            pl.BlockSpec(table.shape, lambda i: (0, 0)),
        ],
        out_specs=[spec(d), spec(HALF), spec(HALF)],
        out_shape=[
            jax.ShapeDtypeStruct((n, d), BF),
            jax.ShapeDtypeStruct((n, HALF), F32),
            jax.ShapeDtypeStruct((n, HALF), F32),
        ],
        compiler_params=params(),
        cost_estimate=cost(0, 12 * n * d),
        name="norm_in",
    )(x, positions, table)


def head_masks():
    lane = lax.broadcasted_iota(jnp.int32, (1, GW), 1)
    rot = [((lane % HALF) // (HEAD_DIM // 2) == h) for h in range(GROUP)]
    nat = [(lane // HEAD_DIM == h) for h in range(GROUP)]
    return rot, nat


def mask_to(x, m):
    return x * jnp.where(m, 1.0, 0.0).astype(x.dtype)


def blocks_of(total, size):
    return [(s, min(s + size, total)) for s in range(0, total, size)]


def attn_fwd_kernel(slot, size, pair, ids_ref, nm_ref, cos_ref, sin_ref, own_hbm, oth_hbm,
                    qkv_ref, att_ref, lse_ref, w_out_ref, sem):
    group = pl.program_id(0)
    crop = pl.program_id(1)
    crops = pl.num_programs(1)
    zs = own_hbm.shape[1]
    rep, z, core = ids_ref[crops], ids_ref[crops + 1], ids_ref[crops + 2]

    @pl.when(crop == 0)
    def _():
        made = []
        for hbm, place in ((own_hbm, core), (oth_hbm, 1 - core)):
            for kind in range(4):
                for j in range(zs):
                    src = hbm.at[kind ^ rep, j, :, pl.ds(pl.multiple_of(group * GW, GW), GW)]
                    dst = w_out_ref.at[(z + j) & (zs - 1), place, :, pl.ds(kind * GW, GW)]
                    made.append(pltpu.make_async_copy(src, dst, sem.at[len(made)]))
        for copy in made:
            copy.start()
        for copy in made:
            copy.wait()

    nm = nm_ref[...]
    cos = cos_ref[...]
    sin = sin_ref[...]
    rot_m, nat_m = head_masks()
    d = nm.shape[1]

    def rotated(lo, scale):
        u = nn(nm, w_out_ref[:, :, :, lo : lo + GW].reshape(d, GW))
        a, b = u[:, :HALF], u[:, HALF:]
        r = jnp.concatenate([a * cos - b * sin, a * sin + b * cos], axis=1)
        return r.astype(BF) * jnp.asarray(scale, BF)

    q = rotated(0, HEAD_DIM ** (-0.5))
    k = rotated(GW, 1.0)
    v = nn(nm, w_out_ref[:, :, :, 2 * GW : 3 * GW].reshape(d, GW)).astype(BF)
    qkv_ref[:, :GW] = q
    qkv_ref[:, GW : 2 * GW] = k
    qkv_ref[:, 2 * GW :] = v
    qs = [mask_to(q, m) for m in rot_m]
    lane = lax.broadcasted_iota(jnp.int32, (1, 128), 1)
    units = [(s, e, h) for s, e in blocks_of(slot, size) for h in range(0, GROUP, pair)]

    def scores(s, e, h):
        stack = jnp.concatenate([qs[i][s:e] for i in range(h, h + pair)], axis=0)
        return nt(stack, k[s:e]), nt(stack, k[:s]) if s else None

    out = logs = None
    ready = scores(*units[0])
    for i, (s, e, h) in enumerate(units):
        later = scores(*units[i + 1]) if i + 1 < len(units) else None
        diag, left = ready
        w = e - s
        row = lax.broadcasted_iota(jnp.int32, (pair, w, w), 1).reshape(pair * w, w)
        col = lax.broadcasted_iota(jnp.int32, (pair, w, w), 2).reshape(pair * w, w)
        diag = jnp.where(row >= col, diag, -1e30)
        top = jnp.max(diag, axis=-1, keepdims=True)
        if s:
            top = jnp.maximum(top, jnp.max(left, axis=-1, keepdims=True))
        pd = jnp.exp(diag - top)
        total = jnp.sum(pd, axis=-1, keepdims=True)
        o = nn(pd.astype(BF), v[s:e])
        if s:
            pleft = jnp.exp(left - top)
            total = total + jnp.sum(pleft, axis=-1, keepdims=True)
            o = o + nn(pleft.astype(BF), v[:s])
        o = o * (1.0 / total)
        log = top + jnp.log(total)
        for g in range(pair):
            part = slice(g * w, (g + 1) * w)
            out = jnp.where(nat_m[h + g], o[part], out if h + g else 0.0)
            logs = jnp.where(lane == h + g, log[part], logs if h + g else 0.0)
        if h + pair == GROUP:
            att_ref[s:e, :] = out.astype(BF)
            lse_ref[0, 0, :, s:e] = logs.T[:8]
        ready = later


def attn_fwd(ids, nm, cos, sin, own, oth, slot, size=256, pair=4):
    n, d = nm.shape
    crops = n // slot
    kinds, zs, rows, width = own.shape
    groups = width // GW
    hbm = pl.BlockSpec(memory_space=pl.ANY)
    crop_spec = lambda w: pl.BlockSpec((slot, w), lambda g, c, *_: (c, 0))
    qkv, att, lse, w = pl.pallas_call(
        functools.partial(attn_fwd_kernel, slot, size, pair),
        grid_spec=pltpu.PrefetchScalarGridSpec(
            num_scalar_prefetch=1,
            grid=(groups, crops),
            in_specs=[crop_spec(d), crop_spec(HALF), crop_spec(HALF), hbm, hbm],
            out_specs=[
                pl.BlockSpec((slot, 3 * GW), lambda g, c, *_: (c, g)),
                pl.BlockSpec((slot, GW), lambda g, c, *_: (c, g)),
                pl.BlockSpec((1, 1, 8, slot), lambda g, c, *_: (g, c, 0, 0)),
                pl.BlockSpec((zs, 2, rows, 4 * GW), lambda g, c, *_: (0, 0, 0, g)),
            ],
            scratch_shapes=[pltpu.SemaphoreType.DMA((8 * zs,))],
        ),
        out_shape=[
            jax.ShapeDtypeStruct((n, groups * 3 * GW), BF),
            jax.ShapeDtypeStruct((n, groups * GW), BF),
            jax.ShapeDtypeStruct((groups, crops, 8, slot), F32),
            jax.ShapeDtypeStruct((zs, 2, rows, groups * 4 * GW), BF),
        ],
        compiler_params=params(),
        cost_estimate=cost(8e6 * groups * n, 2 * n * d),
        name="attn_fwd",
    )(ids, nm, cos, sin, own, oth)
    return qkv, att, lse, w.reshape(d, groups * 4 * GW)


def attn_bwd_kernel(slot, size, pair, qkv_ref, go_ref, att_ref, lse_ref, nm_ref, cos_ref, sin_ref, *refs):
    gqkv_ref, dw_ref, ds_ref, dq_ref, acc_ref = refs[-5:]
    crop = pl.program_id(1)
    q = qkv_ref[:, :GW]
    k = qkv_ref[:, GW : 2 * GW]
    v = qkv_ref[:, 2 * GW :]
    go = go_ref[...]
    rot_m, nat_m = head_masks()
    prod = go.astype(F32) * att_ref[...].astype(F32)
    hi = prod.astype(BF)
    lo = (prod - hi.astype(F32)).astype(BF)
    pick = (
        lax.broadcasted_iota(jnp.int32, (8, GW), 1) // HEAD_DIM
        == lax.broadcasted_iota(jnp.int32, (8, GW), 0)
    )
    pick = jnp.where(pick, 1.0, 0.0).astype(BF)
    delta = nt(pick, hi) + nt(pick, lo)
    blocks = blocks_of(slot, size)
    dk = [None] * len(blocks)
    dv = [None] * len(blocks)
    kms = [mask_to(k, m) for m in rot_m]
    vms = [mask_to(v, m) for m in nat_m]
    units = [(j, s, e, h) for j, (s, e) in enumerate(blocks) for h in range(0, GROUP, pair)]

    def stacked(parts, s, e, h):
        return jnp.concatenate([parts[i][s:e] for i in range(h, h + pair)], axis=0)

    def scores(j, s, e, h):
        return nt(stacked(kms, s, e, h), q[s:]), nt(stacked(vms, s, e, h), go[s:])

    ready = scores(*units[0])
    for i, (j, s, e, h) in enumerate(units):
        later = scores(*units[i + 1]) if i + 1 < len(units) else None
        w = e - s
        row = lax.broadcasted_iota(jnp.int32, (w, w), 0)
        col = lax.broadcasted_iota(jnp.int32, (w, w), 1)
        ps, dss = [], []
        for g in range(pair):
            sc, dp = (x[g * w : (g + 1) * w] for x in ready)
            p = jnp.exp(sc - lse_ref[0, 0, h + g : h + g + 1, s:])
            first = jnp.where(col >= row, p[:, :w], 0.0)
            p = jnp.concatenate([first, p[:, w:]], axis=1) if e < slot else first
            ds = (p * (dp - delta[h + g : h + g + 1, s:])).astype(BF)
            ds_ref[h + g, s:, s:e] = ds.T
            ps.append(p.astype(BF))
            dss.append(ds)
        dvp = nn(jnp.concatenate(ps, axis=0), go[s:])
        dkp = nn(jnp.concatenate(dss, axis=0), q[s:])
        for g in range(pair):
            part = slice(g * w, (g + 1) * w)
            dv[j] = jnp.where(nat_m[h + g], dvp[part], dv[j] if h + g else 0.0)
            dk[j] = jnp.where(rot_m[h + g], dkp[part], dk[j] if h + g else 0.0)
        ready = later
    for s, e in blocks:
        w = e - s
        parts = nn(ds_ref[:, s:e, :e].reshape(GROUP * w, e), k[:e])
        dq = 0.0
        for h in range(GROUP):
            dq = jnp.where(rot_m[h], parts[h * w : (h + 1) * w], dq)
        dq_ref[s:e] = dq
    cos = cos_ref[...]
    sin = sin_ref[...]

    def back(u, c, t):
        a, b = u[:, :HALF], u[:, HALF:]
        return jnp.concatenate([a * c + b * t, b * c - a * t], axis=1).astype(BF)

    for j, (s, e) in enumerate(blocks):
        c, t = cos[s:e], sin[s:e]
        gqkv_ref[s:e, :GW] = back(dq_ref[s:e] * (HEAD_DIM ** (-0.5)), c, t)
        gqkv_ref[s:e, GW : 2 * GW] = back(dk[j], c, t)
        gqkv_ref[s:e, 2 * GW :] = dv[j].astype(BF)
    part = tn(nm_ref[...], gqkv_ref[...])

    @pl.when(crop == 0)
    def _():
        acc_ref[...] = part

    @pl.when(crop != 0)
    def _():
        acc_ref[...] += part

    @pl.when(crop == pl.num_programs(1) - 1)
    def _():
        dw_ref[...] = acc_ref[...].astype(BF)


def attn_bwd(qkv, go, att, lse, nm, cos, sin, slot, place, first, joint=None, size=128, pair=4):
    n, d = nm.shape
    crops = n // slot
    more = [] if joint is None else [joint]
    column = 0 if joint is None else first + place + 1
    row_spec = lambda w, at: pl.BlockSpec((slot, w), lambda g, c: (c, at))
    crop_spec = lambda w: pl.BlockSpec((slot, w), lambda g, c: (c, 0))
    return pl.pallas_call(
        functools.partial(attn_bwd_kernel, slot, size, pair),
        grid=(1, crops),
        in_specs=[
            row_spec(3 * GW, place),
            row_spec(GW, first + place),
            row_spec(GW, place),
            pl.BlockSpec((1, 1, 8, slot), lambda g, c: (place, c, 0, 0)),
            crop_spec(d),
            crop_spec(HALF),
            crop_spec(HALF),
        ]
        + [pl.BlockSpec(memory_space=pl.ANY)] * len(more),
        out_specs=[crop_spec(3 * GW), pl.BlockSpec((d, 3 * GW), lambda g, c: (0, column))],
        out_shape=[
            jax.ShapeDtypeStruct((n, 3 * GW), BF),
            jax.ShapeDtypeStruct((d, 3 * GW) if joint is None else joint.shape, BF),
        ],
        input_output_aliases={7: 1} if more else {},
        scratch_shapes=[
            pltpu.VMEM((GROUP, slot, slot), BF),
            pltpu.VMEM((slot, GW), F32),
            pltpu.VMEM((d, 3 * GW), F32),
        ],
        compiler_params=params(),
        cost_estimate=cost(12e6 * n, 2 * n * d),
        name="attn_bwd",
    )(qkv, go, att, lse, nm, cos, sin, *more)


def valid_rows(ids_ref, tile, rows, slot):
    row = tile * rows + lax.broadcasted_iota(jnp.int32, (rows, 1), 0)
    crop = row // slot
    first = tile * rows // slot
    limit = jnp.zeros((rows, 1), jnp.int32)
    for i in range(-(-rows // slot) + 1):
        index = first + i
        limit = jnp.where(crop == index, ids_ref[index] * COLS, limit)
    return row - crop * slot < limit


def out_weights(weights, d):
    arrays, specs = [], []
    for w in weights:
        for g in range(w.shape[1] // (4 * GW)):
            arrays.append(w)
            specs.append(pl.BlockSpec((d, GW), lambda c, *_, g=g: (0, 4 * g + 3)))
    return arrays, specs


def out_proj_kernel(slot, n_att, ids_ref, x_ref, *refs):
    att_refs, refs = refs[:n_att], refs[n_att:]
    *wo_refs, mid_ref, nm_ref = refs
    valid = valid_rows(ids_ref, pl.program_id(0), x_ref.shape[0], slot)
    att = jnp.concatenate([a[...] for a in att_refs], axis=1)
    proj = jnp.concatenate([nn(att, w[...]) for w in wo_refs], axis=1)
    mid = x_ref[...].astype(F32) + jnp.where(valid, proj, 0.0)
    mid_ref[...] = mid.astype(BF)
    nm_ref[...] = (mid * inverse_rms(mid)).astype(BF)


def out_proj(ids, x, atts, weights, slot, tile):
    n, d = x.shape
    rows = lambda w: pl.BlockSpec((tile, w), lambda c, *_: (c, 0))
    wos, wo_specs = out_weights(weights, d)
    return pl.pallas_call(
        functools.partial(out_proj_kernel, slot, len(atts)),
        grid_spec=pltpu.PrefetchScalarGridSpec(
            num_scalar_prefetch=1,
            grid=(n // tile,),
            in_specs=[rows(d)] + [rows(a.shape[1]) for a in atts] + wo_specs,
            out_specs=[rows(d), rows(d)],
        ),
        out_shape=[jax.ShapeDtypeStruct((n, d), BF), jax.ShapeDtypeStruct((n, d), BF)],
        compiler_params=params(),
        cost_estimate=cost(2 * n * d * d, 10 * n * d),
        name="out_proj",
    )(ids, x, *atts, *wos)


PACK = 512
TILE = 768
SHARDS = 8


def halves(w, axis):
    shape = w.shape[:axis] + (-1, 2, w.shape[axis] // (2 * SHARDS) if axis else w.shape[0] // 2) + w.shape[axis + 1 :]
    w = w.reshape(shape)
    return [
        lax.index_in_dim(w, i, axis + 1, keepdims=False).reshape(w.shape[:axis] + (-1,) + w.shape[axis + 3 :])
        for i in range(2)
    ]


def pack_mlp(gate, up, down):
    wide = [w[:, i : i + PACK] for w in (gate, up) for i in range(0, w.shape[1], PACK)]
    half = down.shape[0] // 2
    tail = down[:, PACK:]
    fold = jnp.concatenate([tail[:half], tail[half:]], axis=1)
    return jnp.concatenate(wide + [down[:, :PACK], fold], axis=0)


def unpack_mlp(pack, rows, d):
    chunks = 2
    gate, up = (
        jnp.concatenate([pack[i * rows : (i + 1) * rows] for i in range(s, s + chunks)], axis=1)
        for s in (0, chunks)
    )
    base = 2 * chunks * rows
    deep = (pack.shape[0] - base) * PACK // d
    fold = pack[base + deep :]
    tail = jnp.concatenate([fold[:, : d - PACK], fold[:, d - PACK :]], axis=0)
    return gate, up, jnp.concatenate([pack[base : base + deep], tail], axis=1)


def mlp_kernel(slot, final, step, ids_ref, nm_ref, cot_ref, part_ref, *refs):
    if final:
        before_ref, *refs = refs
    (pack_hbm, out_ref, dn_ref, grad_hbm, wg_buf, wu_buf, wd_buf, hid_ref, gg_ref, gu_ref,
     ag_ref, au_ref, ad_ref, sg_ref, su_ref, sd_ref, in_sem, out_sem) = refs
    tile = pl.program_id(0)
    d = nm_ref.shape[1]
    chunks, shards, rows, _ = sg_ref.shape
    units = chunks * PACK
    some = shards // chunks
    deep = sd_ref.shape[1]
    base = 2 * chunks * rows
    side = d - PACK

    def pieces(hbm, wg, wu, wd):
        for i in range(chunks):
            yield hbm.at[:, pl.ds(i * rows, rows), :], wg.at[i]
            yield hbm.at[:, pl.ds((chunks + i) * rows, rows), :], wu.at[i]
        yield hbm.at[:, pl.ds(base, deep), :], wd.at[:, :, pl.ds(0, PACK)]
        for i in range(2):
            yield (
                hbm.at[:, pl.ds(base + deep, deep // 2), pl.ds(i * side, side)],
                wd.at[:, pl.ds(i * (deep // 2), deep // 2), pl.ds(PACK, side)],
            )

    @pl.when(tile == 0)
    def _():
        made = pieces(pack_hbm, wg_buf, wu_buf, wd_buf)
        made = [pltpu.make_async_copy(a, b, in_sem.at[i]) for i, (a, b) in enumerate(made)]
        for copy in made:
            copy.start()
        ag_ref[...] = jnp.zeros_like(ag_ref)
        au_ref[...] = jnp.zeros_like(au_ref)
        ad_ref[...] = jnp.zeros_like(ad_ref)
        for copy in made:
            copy.wait()

    valid = valid_rows(ids_ref, tile, nm_ref.shape[0], slot)
    nm = nm_ref[...]
    gb = jnp.where(valid, cot_ref[...], jnp.zeros((), BF))
    wd = wd_buf[...].reshape(units, d)

    def wide(buf, i):
        at = i * step
        return buf[at // PACK, :, :, at % PACK : at % PACK + step].reshape(d, step)

    def first(i):
        return (
            nn(nm, wide(wg_buf, i)),
            nn(nm, wide(wu_buf, i)),
            nt(gb, wd[i * step : (i + 1) * step]),
        )

    def second(i, g, u, gh):
        cols = slice(i * step, (i + 1) * step)
        sg = 0.5 * jnp.tanh(0.5 * g) + 0.5
        act = g * sg
        hid_ref[:, cols] = (act * u).astype(BF)
        gu_ref[:, cols] = (gh * act).astype(BF)
        gg_ref[:, cols] = (gh * u * (sg + act * (1.0 - sg))).astype(BF)

    ready = first(0)
    for i in range(1, units // step):
        later = first(i)
        second(i - 1, *ready)
        ready = later
    second(units // step - 1, *ready)
    nmt = nm.T
    gbt = gb.T
    o = part_ref[...].astype(F32) + jnp.where(valid, nn(hid_ref[...], wd), 0.0)
    out_ref[...] = o.astype(out_ref.dtype)
    dn = before_ref[...].astype(F32) if final else 0.0
    for i in range(chunks):
        cols = slice(i * PACK, (i + 1) * PACK)
        dn = dn + nt(gg_ref[:, cols], wg_buf[i].reshape(d, PACK)) + nt(gu_ref[:, cols], wu_buf[i].reshape(d, PACK))
    dn_ref[...] = dn.astype(dn_ref.dtype)
    for i in range(chunks):
        cols = slice(i * PACK, (i + 1) * PACK)
        ag_ref[i] += nn(nmt, gg_ref[:, cols])
        au_ref[i] += nn(nmt, gu_ref[:, cols])
        ad_ref[i] += nn(gbt, hid_ref[:, cols])

    @pl.when(tile == pl.num_programs(0) - 1)
    def _():
        sg_ref[...] = ag_ref[...].astype(BF).reshape(sg_ref.shape)
        su_ref[...] = au_ref[...].astype(BF).reshape(su_ref.shape)
        for i in range(chunks):
            sd_ref[i * some : (i + 1) * some] = ad_ref[i].astype(BF).T.reshape(some, deep, d)
        made = pieces(grad_hbm, sg_ref, su_ref, sd_ref)
        made = [pltpu.make_async_copy(b, a, out_sem.at[i]) for i, (a, b) in enumerate(made)]
        for copy in made:
            copy.start()
        for copy in made:
            copy.wait()


def mlp(ids, nm, cot, part, before, pack, slot, tile, step=512):
    n, d = nm.shape
    rows = d // SHARDS
    chunks = 2
    deep = chunks * PACK // SHARDS
    final = before is not None
    spec = pl.BlockSpec((tile, d), lambda i, *_: (i, 0))
    hbm = pl.BlockSpec(memory_space=pl.ANY)
    packed = pltpu.VMEM((chunks, SHARDS, rows, PACK), BF)
    units = pltpu.VMEM((tile, chunks * PACK), BF)
    sums = pltpu.VMEM((chunks, d, PACK), F32)
    return pl.pallas_call(
        functools.partial(mlp_kernel, slot, final, step),
        grid_spec=pltpu.PrefetchScalarGridSpec(
            num_scalar_prefetch=1,
            grid=(n // tile,),
            in_specs=[spec] * (3 + final) + [hbm],
            out_specs=[spec, spec, hbm],
            scratch_shapes=[packed, packed, pltpu.VMEM((SHARDS, deep, d), BF)]
            + [units] * 3
            + [sums] * 3
            + [packed, packed, pltpu.VMEM((SHARDS, deep, d), BF)]
            + [pltpu.SemaphoreType.DMA((2 * chunks + 3,))] * 2,
        ),
        out_shape=[
            jax.ShapeDtypeStruct((n, d), BF),
            jax.ShapeDtypeStruct((n, d), BF),
            jax.ShapeDtypeStruct(pack.shape, BF),
        ],
        compiler_params=params(),
        cost_estimate=cost(24e6 * n, 20 * n * d),
        name="mlp",
    )(ids, nm, cot, part, *([before] if final else []), pack)


def norm_back(scaled, field):
    inv = inverse_rms(field)
    return inv * scaled - field * (inv * inv * inv * jnp.mean(scaled * field, axis=-1, keepdims=True))


def mid_grad_kernel(slot, n_att, ids_ref, cot_ref, mid_ref, dn_ref, *refs):
    att_refs, refs = refs[:n_att], refs[n_att:]
    *wo_refs, gmid_ref, gatt_ref, dwo_ref, acc_ref = refs
    c = pl.program_id(0)
    valid = valid_rows(ids_ref, c, cot_ref.shape[0], slot)
    gm = cot_ref[...].astype(F32) + norm_back(dn_ref[...].astype(F32), mid_ref[...].astype(F32))
    gmid_ref[...] = gm.astype(BF)
    ga = jnp.where(valid, gm, 0.0).astype(BF)
    gatt = sum(nt(ga[:, i * GW : (i + 1) * GW], w[...]) for i, w in enumerate(wo_refs))
    gatt_ref[...] = gatt.astype(BF)
    part = tn(jnp.concatenate([a[...] for a in att_refs], axis=1), ga)

    @pl.when(c == 0)
    def _():
        acc_ref[...] = part

    @pl.when(c != 0)
    def _():
        acc_ref[...] += part

    @pl.when(c == pl.num_programs(0) - 1)
    def _():
        dwo_ref[...] = acc_ref[...].astype(BF)


def mid_grad(ids, cot, mid, dn, atts, weights, slot, tile):
    n, d = cot.shape
    rows = lambda w: pl.BlockSpec((tile, w), lambda c, *_: (c, 0))
    wos, wo_specs = out_weights(weights, d)
    return pl.pallas_call(
        functools.partial(mid_grad_kernel, slot, len(atts)),
        grid_spec=pltpu.PrefetchScalarGridSpec(
            num_scalar_prefetch=1,
            grid=(n // tile,),
            in_specs=[rows(d)] * 3 + [rows(a.shape[1]) for a in atts] + wo_specs,
            out_specs=[rows(d), rows(d), pl.BlockSpec((d, d), lambda c, *_: (0, 0))],
            scratch_shapes=[pltpu.VMEM((d, d), F32)],
        ),
        out_shape=[
            jax.ShapeDtypeStruct((n, d), BF),
            jax.ShapeDtypeStruct((n, d), BF),
            jax.ShapeDtypeStruct((d, 3 * d), BF),
        ],
        compiler_params=params(),
        cost_estimate=cost(4 * n * d * d, 18 * n * d),
        name="mid_grad",
    )(ids, cot, mid, dn, *atts, *wos)


def input_grad_kernel(n_group, *refs):
    g_refs, w_refs = refs[:n_group], refs[n_group : 4 * n_group]
    x_ref, gmid_ref = refs[4 * n_group : 4 * n_group + 2]
    out_ref = refs[-1]
    e = 0.0
    for i, g in enumerate(g_refs):
        w = jnp.concatenate([w[...] for w in w_refs[3 * i : 3 * i + 3]], axis=1)
        e = e + nt(g[...], w)
    out_ref[...] = gmid_ref[...].astype(F32) + norm_back(e, x_ref[...].astype(F32))


def input_grad(gqkvs, weights, x, gmid, rows, start, stop, filled=None):
    n, d = x.shape
    arrays = [(w, 4 * g + i) for w in weights for g in range(w.shape[1] // (4 * GW)) for i in range(3)]
    spec = lambda w: pl.BlockSpec((rows, w), lambda i: (start + i, 0))
    more = [] if filled is None else [filled]
    n_in = 4 * len(gqkvs) + 2
    count = (stop - start) * rows
    return pl.pallas_call(
        functools.partial(input_grad_kernel, len(gqkvs)),
        grid=(stop - start,),
        in_specs=[spec(3 * GW)] * len(gqkvs)
        + [pl.BlockSpec((d, GW), lambda i, g=g: (0, g)) for _, g in arrays]
        + [spec(d), spec(d)]
        + [pl.BlockSpec(memory_space=pl.ANY)] * len(more),
        out_specs=spec(d),
        out_shape=jax.ShapeDtypeStruct((n, d), F32),
        input_output_aliases={n_in: 0} if more else {},
        compiler_params=params(),
        cost_estimate=cost(6 * count * d * d, 16 * count * d),
        name="input_grad",
    )(*gqkvs, *[w for w, _ in arrays], x, gmid, *more)


def column_of(row_ref):
    row = row_ref[...].astype(F32)
    return jnp.broadcast_to(row, (128, row.shape[1])).T[:, :1]


def lane_order(to_natural):
    lane = lax.broadcasted_iota(jnp.int32, (GW, GW), 1)
    half = HEAD_DIM // 2
    if to_natural:
        source = lane // HEAD_DIM * half + lane % half + jnp.where(lane % HEAD_DIM < half, 0, HALF)
    else:
        source = lane % HALF // half * HEAD_DIM + lane // HALF * half + lane % half
    return jnp.where(lax.broadcasted_iota(jnp.int32, (GW, GW), 0) == source, 1.0, 0.0).astype(BF)


def join_kernel(place_ref, wq_ref, wk_ref, wv_ref, wo_ref, gain_ref, out_ref):
    for kind, w_ref in enumerate((wq_ref, wk_ref, wv_ref, wo_ref)):

        @pl.when(place_ref[0] == kind)
        def _(kind=kind, w_ref=w_ref):
            w = w_ref[...]
            if kind < 3:
                w = (w.astype(F32) * column_of(gain_ref)).astype(BF)
            if kind < 2:
                order = lane_order(False)
                for at in range(0, w.shape[1], GW):
                    out_ref[:, at : at + GW] = nn(w[:, at : at + GW], order).astype(BF)
            else:
                out_ref[...] = w


def join_call(place, wq, wk, wv, wo, gain):
    vmem = pl.BlockSpec(memory_space=pltpu.VMEM)
    return pl.pallas_call(
        join_kernel,
        grid_spec=pltpu.PrefetchScalarGridSpec(
            num_scalar_prefetch=1, grid=(1,), in_specs=[vmem] * 5, out_specs=vmem
        ),
        out_shape=jax.ShapeDtypeStruct(wq.shape, BF),
        compiler_params=params(),
        cost_estimate=cost(0, 1e6),
        name="join",
    )(place, wq, wk, wv, wo, gain)


def pack_kernel(wg_ref, wu_ref, wd_ref, gain_ref, a_ref, b_ref):
    rows, ff = wg_ref.shape
    units = ff // (2 * SHARDS)
    deep = wd_ref.shape[0] // 2
    side = wd_ref.shape[1] - PACK
    chunks = ff // (2 * PACK)
    base = 2 * chunks * rows
    gain = column_of(gain_ref)
    for half, out_ref in enumerate((a_ref, b_ref)):
        for w_ref, first in ((wg_ref, 0), (wu_ref, chunks)):
            for i in range(chunks):
                at = (first + i) * rows
                for j in range(PACK // units):
                    source = (i * (PACK // units) + j) * 2 * units + half * units
                    part = w_ref[:, source : source + units].astype(F32) * gain
                    out_ref[at : at + rows, j * units : (j + 1) * units] = part.astype(BF)
        at = half * deep
        out_ref[base : base + deep] = wd_ref[at : at + deep, :PACK]
        for i in range(2):
            source = at + i * (deep // 2)
            out_ref[base + deep :, i * side : (i + 1) * side] = wd_ref[source : source + deep // 2, PACK:]


def pack_call(wg, wu, wd, gain):
    size = (wg.size + wu.size + wd.size) // (2 * PACK)
    return pl.pallas_call(
        pack_kernel,
        out_shape=[jax.ShapeDtypeStruct((size, PACK), BF)] * 2,
        compiler_params=params(),
        cost_estimate=cost(0, 4e6),
        name="pack",
    )(wg, wu, wd, gain)


def row_of(column):
    return jnp.broadcast_to(column, (column.shape[0], 128)).T[:1]


def mlp_end_kernel(a0_ref, a1_ref, b0_ref, b1_ref, wg_ref, wu_ref, gain_ref, dwg_ref, dwu_ref, dwd_ref, g_ref):
    rows = wg_ref.shape[0]
    units = wg_ref.shape[1] // (2 * SHARDS)
    deep = dwd_ref.shape[0] // 2
    side = dwd_ref.shape[1] - PACK
    chunks = wg_ref.shape[1] // (2 * PACK)
    base = 2 * chunks * rows
    gain = column_of(gain_ref)
    dot = jnp.zeros((rows, units), F32)
    for half, (left, right) in enumerate(((a0_ref, a1_ref), (b0_ref, b1_ref))):
        for w_ref, out_ref, first in ((wg_ref, dwg_ref, 0), (wu_ref, dwu_ref, chunks)):
            for i in range(chunks):
                at = (first + i) * rows
                block = left[at : at + rows].astype(F32) + right[at : at + rows].astype(F32)
                for j in range(PACK // units):
                    to = (i * (PACK // units) + j) * 2 * units + half * units
                    part = block[:, j * units : (j + 1) * units]
                    dot = dot + part * w_ref[:, to : to + units].astype(F32)
                    out_ref[:, to : to + units] = part * gain
        down = left[base:].astype(F32) + right[base:].astype(F32)
        at = half * deep
        dwd_ref[at : at + deep, :PACK] = down[:deep]
        for i in range(2):
            to = at + i * (deep // 2)
            dwd_ref[to : to + deep // 2, PACK:] = down[deep:, i * side : (i + 1) * side]
    g_ref[...] = row_of(jnp.sum(dot, axis=1, keepdims=True))


def mlp_end(a0, a1, b0, b1, wg, wu, gain, down_shape):
    rows = wg.shape[0]
    return pl.pallas_call(
        mlp_end_kernel,
        out_shape=[
            jax.ShapeDtypeStruct(wg.shape, F32),
            jax.ShapeDtypeStruct(wu.shape, F32),
            jax.ShapeDtypeStruct(down_shape, F32),
            jax.ShapeDtypeStruct((1, rows), F32),
        ],
        compiler_params=params(),
        cost_estimate=cost(0, 6e6),
        name="mlp_end",
    )(a0, a1, b0, b1, wg, wu, gain)


def natural(block, order):
    moved = 0.0
    for _ in range(3):
        part = block.astype(BF)
        moved = moved + nn(part, order)
        block = block - part.astype(F32)
    return moved


def attn_end_kernel(l0_ref, l1_ref, r0_ref, r1_ref, wq_ref, wk_ref, wv_ref, gain_ref,
                    dwq_ref, dwk_ref, dwv_ref, dwo_ref, g_ref):
    rows, d = wq_ref.shape
    gain = column_of(gain_ref)

    def summed(lo, hi):
        pairs = ((l0_ref, r0_ref), (l1_ref, r1_ref))
        return jnp.concatenate([l[:, lo:hi].astype(F32) + r[:, lo:hi].astype(F32) for l, r in pairs], axis=0)

    dwo_ref[...] = summed(0, d)
    order = lane_order(True)
    dot = jnp.zeros((rows, GW), F32)
    for g in range(d // GW - 1):
        for kind, (w_ref, out_ref) in enumerate(((wq_ref, dwq_ref), (wk_ref, dwk_ref), (wv_ref, dwv_ref))):
            at = d + (3 * g + kind) * GW
            block = summed(at, at + GW)
            if kind < 2:
                block = natural(block, order)
            cols = slice(g * GW, (g + 1) * GW)
            dot = dot + block * w_ref[:, cols].astype(F32)
            out_ref[:, cols] = block * gain
    g_ref[...] = row_of(jnp.sum(dot, axis=1, keepdims=True))


def attn_end(lefts, rights, wq, wk, wv, gain):
    rows, d = wq.shape
    return pl.pallas_call(
        attn_end_kernel,
        out_shape=[jax.ShapeDtypeStruct((rows, d), F32)] * 4 + [jax.ShapeDtypeStruct((1, rows), F32)],
        compiler_params=params(),
        cost_estimate=cost(0, 6e6),
        name="attn_end",
    )(*lefts, *rights, wq, wk, wv, gain)


def last_end_kernel(place_ref, last_ref, wq_ref, wk_ref, wv_ref, gain_ref, before_ref, *refs):
    out_refs, g_ref, last_buf = refs[3:6], refs[6], refs[7]
    reps, few, _ = last_ref.shape
    gain = column_of(gain_ref)
    for r in range(reps):
        last_buf[r * few : (r + 1) * few] = last_ref[r ^ place_ref[0]].astype(F32)
    order = lane_order(True)
    dot = 0.0
    for kind, (w_ref, out_ref) in enumerate(zip((wq_ref, wk_ref, wv_ref), out_refs)):
        block = last_buf[:, kind * GW : (kind + 1) * GW]
        if kind < 2:
            block = natural(block, order)
        dot = dot + block * w_ref[...].astype(F32)
        out_ref[...] = block * gain
    g_ref[...] = before_ref[...] + row_of(jnp.sum(dot, axis=1, keepdims=True))


def last_end(place, last, wq, wk, wv, gain, g, dwq, dwk, dwv):
    rows, d = wq.shape
    vmem = pl.BlockSpec(memory_space=pltpu.VMEM)
    group = pl.BlockSpec((rows, GW), lambda i, *_: (0, d // GW - 1))
    return pl.pallas_call(
        last_end_kernel,
        grid_spec=pltpu.PrefetchScalarGridSpec(
            num_scalar_prefetch=1,
            grid=(1,),
            in_specs=[vmem, group, group, group, vmem, vmem] + [pl.BlockSpec(memory_space=pl.ANY)] * 3,
            out_specs=[group] * 3 + [vmem],
            scratch_shapes=[pltpu.VMEM((rows, 3 * GW), F32)],
        ),
        out_shape=[jax.ShapeDtypeStruct((rows, d), F32)] * 3 + [jax.ShapeDtypeStruct((1, rows), F32)],
        input_output_aliases={7: 0, 8: 1, 9: 2},
        compiler_params=params(),
        cost_estimate=cost(0, 3e6),
        name="last_end",
    )(place, last, wq, wk, wv, gain, g, dwq, dwk, dwv)


def rot_order(w):
    rows, cols = w.shape
    w = w.reshape(rows, cols // GW, GROUP, 2, HEAD_DIM // 2)
    return w.transpose(0, 1, 3, 2, 4).reshape(rows, cols)


def natural_order(w):
    rows, cols = w.shape
    w = w.reshape(rows, cols // GW, 2, GROUP, HEAD_DIM // 2)
    return w.transpose(0, 1, 3, 2, 4).reshape(rows, cols)


def join_attn(wq, wk, wv, wo, gain):
    scaled = [(w.astype(F32) * gain).astype(BF) for w in (rot_order(wq), rot_order(wk), wv)]
    return jnp.stack(scaled + [wo])


def swap(x, axis, bit, size):
    return lax.ppermute(x, axis, [(i, i ^ bit) for i in range(size)])


def shift(x, step, size):
    half = size // 2
    return lax.ppermute(x, "fsdp", [(((i // 2 + step) % half) * 2 + i % 2, i) for i in range(size)])


def pick(x, index, axis=0):
    return lax.dynamic_index_in_dim(x, index, axis, keepdims=False)


def total(*parts):
    return sum(p.astype(F32) for p in parts).astype(BF)


def along_z(mine, size):
    return jnp.stack([mine] + [shift(mine, k, size) for k in range(1, size // 2)])


def over_reps(x, reps):
    return jnp.stack([x] + [swap(x, "rep", bit, reps) for bit in range(1, reps)])


def sum_reps(x, reps):
    if reps != 4:
        return lax.psum(x, "rep").astype(F32)
    x = (x.astype(F32) + swap(x, "rep", 1, reps).astype(F32)).astype(BF)
    return x.astype(F32) + swap(x, "rep", 2, reps).astype(F32)


def body(tokens, cotangent, crop_heights, rope_positions, gain_attn, w_query, w_key, w_value, w_out,
         gain_mlp, w_gate, w_up, w_down, *, reps, size):
    crops = crop_heights.shape[0]
    n, d = tokens.shape
    slot = n // crops
    tile = TILE if n % TILE == 0 else slot
    gain1 = gain_attn.astype(F32)[:, None]
    gain2 = gain_mlp.astype(F32)[:, None]

    def gather(w):
        return lax.all_gather(w, "fsdp", axis=0, tiled=True)

    def scatter(g):
        return lax.psum_scatter(g, "fsdp", scatter_dimension=0, tiled=True)

    def reduce(g):
        return sum_reps(scatter(g), reps)

    pin = lax.optimization_barrier
    links = reps == 4 and size == SHARDS
    rep, f = lax.axis_index("rep"), lax.axis_index("fsdp")
    if links:
        place = jnp.stack([rep, f // 2, f % 2]).astype(jnp.int32)
        row1, row2 = gain_attn[None], gain_mlp[None]
        mine = join_call(place, w_query, w_key, w_value, w_out, row1)
        mine, w_gate, w_up, w_down, tokens_1 = pin((mine, w_gate, w_up, w_down, tokens))
        lines = [along_z(m, size) for m in (mine[:, :GW], mine[:, GW:])]
        sides = [swap(lines[0], "rep", bit, reps) for bit in range(1, reps)]
    else:
        place = jnp.zeros((3,), jnp.int32)
        joined = join_attn(w_query, w_key, w_value, w_out, gain1)
        every = lax.all_gather(joined, "fsdp", axis=1, tiled=True)
        every = every.reshape(4, SHARDS // 2, 2, d // SHARDS, d)
    ids = jnp.concatenate([crop_heights, place])
    if not links:
        tokens_1 = tokens
    nm1, cos, sin = norm_call(tokens_1, rope_positions)
    if links:
        *sides, lines[1], nm1, cos, sin = pin((*sides, lines[1], nm1, cos, sin))
        own = jnp.stack([lines[0]] + sides)
        own, w_gate, w_up, w_down = pin((own, w_gate, w_up, w_down))
        oth = swap(own, "fsdp", 1, size)
        sides = [swap(lines[1], "rep", bit, reps) for bit in range(1, reps)]
        packs = [
            lax.all_gather(p, "fsdp", axis=0, tiled=False) for p in pack_call(w_gate, w_up, w_down, row2)
        ]
    else:
        scaled = [(w.astype(F32) * gain2).astype(BF) for w in (w_gate, w_up)]
        wide = [gather(w).reshape(SHARDS, -1, w.shape[1]) for w in scaled]
        down = gather(w_down).reshape(SHARDS, -1, d)
        split = zip(*[[jnp.stack(h) for h in zip(*[halves(w, a) for w in ws])] for ws, a in
                      ((wide[0], 1), (wide[1], 1), (down, 0))])
        packs = [jax.vmap(pack_mlp)(*part) for part in split]

    attended, weights = [], []
    for i, cols in enumerate((slice(0, GW), slice(GW, d))):
        if not links:
            own, oth = every[:, :, 0, :, cols], every[:, :, 1, :, cols]
        elif i:
            *parts, _ = pin((lines[1], *sides, atts))
            own = jnp.stack(parts)
            oth = swap(own, "fsdp", 1, size)
        *some, w = attn_fwd(ids, nm1, cos, sin, own, oth, slot)
        attended.append(some)
        weights.append(w)
        atts = [a for _, a, _ in attended]
    mid, nm2 = out_proj(ids, tokens, atts, weights, slot, tile)
    part, dn, grad_a = mlp(ids, nm2, cotangent, mid, None, packs[0], slot, tile)
    out, dn, grad_b = mlp(ids, nm2, cotangent, part, dn, packs[1], slot, tile)
    local_a = scatter(grad_a.reshape(-1, PACK)) if links else grad_a
    local_b = scatter(grad_b.reshape(-1, PACK)) if links else grad_b
    gmid, gatt, joint = mid_grad(ids, cotangent, mid, dn, atts, weights, slot, tile)

    def backward(index, gatt, joint=None):
        w = 0 if index == 0 else 1
        qkv, att, lse = attended[w]
        return attn_bwd(qkv, gatt, att, lse, nm1, cos, sin, slot, index - w, w, joint)

    fast = False
    if links:
        local_a, gatt = pin((local_a, gatt))
        local_a = total(local_a, swap(local_a, "rep", 1, reps))
    gqkv0, joint = backward(0, gatt, joint)
    if links:
        local_a, gatt, gqkv0 = pin((local_a, gatt, gqkv0))
        other_a = swap(local_a, "rep", 2, reps)
    gqkv1, joint = backward(1, gatt, joint)
    if links:
        other_a, local_b, joint, gatt, gqkv1 = pin((other_a, local_b, joint, gatt, gqkv1))
        local_b = total(local_b, swap(local_b, "rep", 1, reps))
    joint = scatter(joint)
    gqkv2, dw2 = backward(2, gatt)
    gqkvs = [gqkv0, gqkv1, gqkv2]
    grad = lambda gmid: input_grad(gqkvs, weights, tokens, gmid, tile // 2, 0, 2 * n // tile)
    if links:
        y, x, z, core = rep // 2, rep % 2, f // 2, f % 2
        zs, rows = size // 2, d // size
        cut = dw2.reshape(zs, 2, 2, 2, rows // reps, 3 * GW)
        keep, send = pick(cut, core, 1), pick(cut, 1 - core, 1)
        got = swap(send, "fsdp", 1, size)
        keep, local_b, gqkvs[2] = pin((keep, local_b, gqkvs[2]))
        other_b = swap(local_b, "rep", 2, reps)
        side = swap(total(pick(keep, 1 - x, 2), pick(got, 1 - x, 2)), "rep", 1, reps)
        keep = total(pick(keep, x, 2), pick(got, x, 2))
        keep, gmid = pin((keep, gmid))
        grad_tokens = grad(gmid)
        grad_tokens, keep, side, joint, local_a, other_a = pin((grad_tokens, keep, side, joint, local_a, other_a))
        got = swap(total(pick(keep, 1 - y, 1), pick(side, 1 - y, 1)), "rep", 2, reps)
        cuts = joint[: rows // 2], joint[rows // 2 :]
        others = [swap(part, "rep", 1 + i, reps) for i, part in enumerate(cuts)]
        keep, side = pick(keep, y, 1), pick(side, y, 1)
        *dmlp, g2 = mlp_end(local_a, other_a, local_b, other_b, w_gate, w_up, row2, w_down.shape)
        dmlp[0], keep, side, got = pin((dmlp[0], keep, side, got))

        def at(k):
            i = (z + k) % zs
            return total(pick(keep, i), pick(side, i), pick(got, i))

        sends = [at(zs - k) for k in range(1, zs)]
        first, *others = pin((at(0), *others))
        cuts = [total(a, b) for a, b in zip(cuts, others)]
        others = [swap(part, "rep", 2 - i, reps) for i, part in enumerate(cuts)]
        part = total(first, *[shift(s, k + 1, size) for k, s in enumerate(sends)])
        sides = [swap(part, "rep", bit, reps) for bit in range(1, reps)]
        *dqkv, dwo, g1 = attn_end(cuts, others, w_query, w_key, w_value, row1)
        *sides, g1 = pin((*sides, g1))
        every = jnp.stack([part] + sides)
        *dqkv, g1 = last_end(place, every, w_query, w_key, w_value, row1, g1, *dqkv)
        return (out, grad_tokens, g1.reshape(-1), *dqkv, dwo, g2.reshape(-1), *dmlp)

    grad_tokens = grad(gmid)
    dw2 = reduce(dw2)
    joint = sum_reps(joint, reps)
    if fast:
        sum_a, sum_b = sum_reps(local_a, reps), sum_reps(local_b, reps)
    both = []
    if fast:
        both = [unpack_mlp(x, d // SHARDS, d) for x in (sum_a, sum_b)]
    else:
        both = [jax.vmap(lambda p: unpack_mlp(p, d // SHARDS, d))(grad) for grad in (grad_a, grad_b)]

    def rejoin(pair, axis):
        lead = pair[0].shape[:axis]
        rest = pair[0].shape[axis + 1 :]
        parts = [p.reshape(lead + (SHARDS if axis else 1, -1) + rest) for p in pair]
        return jnp.stack(parts, axis=axis + 1).reshape(lead + (-1,) + rest)

    if fast:
        raw = [rejoin([b[i] for b in both], axis) for i, axis in ((0, 1), (1, 1), (2, 0))]
    else:
        raw = []
        for i, axis in ((0, 1), (1, 1), (2, 0)):
            whole = jax.vmap(lambda a, b: rejoin([a, b], axis))(both[0][i], both[1][i])
            raw.append(reduce(whole.reshape(-1, whole.shape[-1])))
    g2 = jnp.sum(raw[0] * w_gate.astype(F32), axis=1) + jnp.sum(raw[1] * w_up.astype(F32), axis=1)
    dwg, dwu, dwd = raw[0] * gain2, raw[1] * gain2, raw[2]

    dwo, dws = joint[:, :d], [joint[:, d : d + 3 * GW], joint[:, d + 3 * GW :], dw2]
    raw = [jnp.concatenate([w[:, i * GW : (i + 1) * GW] for w in dws], axis=1) for i in range(3)]
    raw = [natural_order(raw[0]), natural_order(raw[1]), raw[2]]
    g1 = sum(jnp.sum(r * w.astype(F32), axis=1) for r, w in zip(raw, (w_query, w_key, w_value)))
    dwq, dwk, dwv = (r * gain1 for r in raw)
    return out, grad_tokens, g1, dwq, dwk, dwv, dwo, g2, dwg, dwu, dwd


def solution(mesh):
    in_specs = (
        P(("rep", "fsdp"), None),
        P(("rep", "fsdp"), None),
        P(("rep", "fsdp")),
        P(("rep", "fsdp"), None, None),
        P("fsdp"),
        P("fsdp", None),
        P("fsdp", None),
        P("fsdp", None),
        P("fsdp", None),
        P("fsdp"),
        P("fsdp", None),
        P("fsdp", None),
        P("fsdp", None),
    )
    out_specs = (
        P(("rep", "fsdp"), None),
        P(("rep", "fsdp"), None),
        P("fsdp"),
        P("fsdp", None),
        P("fsdp", None),
        P("fsdp", None),
        P("fsdp", None),
        P("fsdp"),
        P("fsdp", None),
        P("fsdp", None),
        P("fsdp", None),
    )
    sizes = dict(reps=mesh.shape["rep"], size=mesh.shape["fsdp"])
    return jax.shard_map(functools.partial(body, **sizes), mesh=mesh, in_specs=in_specs, out_specs=out_specs, check_vma=False)
```
